32 devices in a mesh: dp: 8 (over z, x), mp: 4 (over y, core).
Axes of the slice: x: 2, y: 2, z: 4, core: 2. Of those that a mesh axis runs over, the one named last changes fastest.
Arguments:
- tokens: bfloat16 [16, 1024, 2048], P(None, 'dp', 'mp'), may hold values from -6 to 6
- cotangent: bfloat16 [16, 1024, 2048], P(None, 'dp', 'mp'), may hold values from -6 to 6
- lengths: int32 [16], replicated, may hold values from 1 to 1024, 14745 in all
- adapter_index: int32 [16], replicated, may hold values from 0 to 7
- ln_gain: float32 [2048], replicated, may hold values from 0.5 to 1.5
- ln_bias: float32 [2048], replicated, may hold values from -2 to 2
- w_qkv: bfloat16 [3, 2048, 2048], P(None, 'dp', 'mp'), may hold values from -0.125 to 0.125
- qkv_bias: bfloat16 [3, 2048], P(None, 'mp'), may hold values from -3 to 3
- w_dense: bfloat16 [2048, 2048], P('mp', 'dp'), may hold values from -1 to 1
- w_fc1: bfloat16 [2048, 8192], P('dp', 'mp'), may hold values from -0.125 to 0.125
- fc1_bias: bfloat16 [8192], P('mp'), may hold values from -3 to 3
- w_fc2: bfloat16 [8192, 2048], P('mp', 'dp'), may hold values from -0.125 to 0.125
- out_bias: bfloat16 [2048], P('mp'), may hold values from -3 to 3
- qkv_down: float32 [128, 2048], P(('dp', 'mp')), may hold values from -0.125 to 0.125
- qkv_up: float32 [3, 128, 2048], P(None, 'dp', 'mp'), may hold values from -0.75 to 0.75
- dense_down: float32 [128, 2048], P('dp', 'mp'), may hold values from -1 to 1
- dense_up: float32 [128, 2048], P(('dp', 'mp')), may hold values from -0.75 to 0.75
- fc1_down: float32 [128, 2048], P(('dp', 'mp')), may hold values from -0.125 to 0.125
- fc1_up: float32 [128, 8192], P('dp', 'mp'), may hold values from -0.75 to 0.75
- fc2_down: float32 [128, 8192], P('dp', 'mp'), may hold values from -0.125 to 0.125
- fc2_up: float32 [128, 2048], P(('dp', 'mp')), may hold values from -0.75 to 0.75
Outputs:
- output: bfloat16 [16, 1024, 2048], P(None, 'dp', 'mp')
- input_grad: bfloat16 [16, 1024, 2048], P(None, 'dp', 'mp')
- grad_qkv_down: float32 [128, 2048], P(('dp', 'mp'))
- grad_qkv_up: float32 [3, 128, 2048], P(None, 'dp', 'mp')
- grad_dense_down: float32 [128, 2048], P('dp', 'mp')
- grad_dense_up: float32 [128, 2048], P(('dp', 'mp'))
- grad_fc1_down: float32 [128, 2048], P(('dp', 'mp'))
- grad_fc1_up: float32 [128, 8192], P('dp', 'mp')
- grad_fc2_down: float32 [128, 8192], P('dp', 'mp')
- grad_fc2_up: float32 [128, 2048], P(('dp', 'mp'))
The draws below stay inside these ranges and needn't reach their ends.
Inputs may be any that keep to these rules, and one draw needn't show every extreme that they name: The lengths add up to 14745.
All inputs are finite; a program needn't handle non-finite values.
Results may differ from the reference program's by a relative error of at most 0.011.
Values may be sent and summed in bfloat16 or wider, within the bound.
No kernel may reach another device: no remote copies, remote signals or barrier semaphores. Data moves between devices by JAX's collectives and lax.ppermute only.
A program may use at most 384 MiB of HBM per device.

```python
import math
import jax
import jax.numpy as jnp
import numpy as np
from jax import lax

D = 2048
HEADS = 32
HD = 64
ROT = 32
FF = 8192
ADAPT = 8
RANK = 16
SLOT = 1024
SEQS = 16


def with_ends(drawn, rng, least, top_value):
    shape = drawn.shape
    spot = [jax.random.randint(jax.random.fold_in(rng, axis), (), 0, shape[axis]) for axis in range(len(shape))]
    drawn = drawn.at[tuple(spot)].set(least)
    longest = shape.index(max(shape))
    spot[longest] = (spot[longest] + 1) % shape[longest]
    return drawn.at[tuple(spot)].set(top_value)


def levels(stream_key, dims, pieces, least, high):
    gain = 1.0
    for dim, parts in pieces:
        draws = jax.random.uniform(jax.random.fold_in(jax.random.fold_in(stream_key, 6), dim), (parts,), jnp.float32, least / len(pieces), high / len(pieces))
        gain = gain * jnp.repeat(jnp.exp(draws), dims[dim] // parts).reshape((-1,) + (1,) * (len(dims) - 1 - dim))
    return gain


def profile(number_of, total, reach, skew):
    weights = [(1 << 20) // math.isqrt(rank ** skew) + 1 for rank in range(2, number_of + 1)]
    rest, holding = total - reach - (number_of - 1), [1] * (number_of - 1)
    while rest > 0:
        movable = [i for i in range(number_of - 1) if holding[i] < reach]
        mass, budget = sum([weights[i] for i in movable]), rest
        for i in movable:
            addition = min(reach - holding[i], max(1, budget * weights[i] // mass), rest)
            holding[i] = holding[i] + addition
            rest = rest - addition
    return np.array([reach] + holding)


def uneven(key, amount, total, most, slope):
    if amount == 2:
        one = jax.random.randint(key, (), max(1, total - most), min(most, total - 1) + 1)
        return jnp.stack([one, total - one])
    sizes = jnp.asarray(profile(amount, total, most, slope), jnp.int32)
    twos = (amount - 1) // 2
    giver, sink = sizes[1:1 + 2 * twos:2], sizes[2:2 + 2 * twos:2]
    room = jnp.minimum(giver - 1, most - sink)
    moved = jax.random.randint(jax.random.fold_in(key, 1), (twos,), 0, 1 << 20) % (room + 1)
    sizes = sizes.at[1:1 + 2 * twos:2].set(giver - moved).at[2:2 + 2 * twos:2].set(sink + moved)
    return sizes[jax.random.permutation(jax.random.fold_in(key, 2), amount)]


def noise(own_key, shape, width, limit, shards=(), held_as=jnp.bfloat16):
    drawn = jax.random.normal(own_key, shape, jnp.float32) * width
    if len(shards) > 0:
        drawn = levels(own_key, shape, shards, -0.22, 0.18) * drawn
    return jnp.clip(drawn, min=-limit, max=limit).astype(held_as)


def setup_inputs(seed: int = 0) -> dict:
    keys = jax.random.split(jax.random.key(seed), 22)
    return {
        "tokens": noise(keys[0], (SEQS, SLOT, D), 1.0, 6.0, ((1, 8), (2, 4))),
        "cotangent": noise(keys[1], (SEQS, SLOT, D), 1.0, 6.0, ((1, 8), (2, 4))),
        "lengths": uneven(keys[2], SEQS, SEQS * SLOT * 9 // 10, SLOT, 1).astype(jnp.int32),
        "adapter_index": with_ends(jax.random.randint(keys[3], (SEQS,), 0, ADAPT), jax.random.fold_in(keys[3], 1), 0, ADAPT - 1).astype(jnp.int32),
        "ln_gain": jnp.clip(1.0 + 0.1 * jax.random.normal(keys[4], (D,), jnp.float32), 0.5, 1.5),
        "ln_bias": noise(keys[5], (D,), 0.3, 2.0, (), jnp.float32),
        "w_qkv": noise(keys[6], (3, D, D), D ** -0.5, 0.125, ((1, 8), (2, 4))),
        "qkv_bias": noise(keys[7], (3, D), 0.5, 3.0, ((1, 4),)),
        "w_dense": noise(keys[8], (D, D), (D // 64) ** -0.5, 1.0, ((0, 4), (1, 8))),
        "w_fc1": noise(keys[9], (D, FF), D ** -0.5, 0.125, ((0, 8), (1, 4))),
        "fc1_bias": noise(keys[10], (FF,), 0.5, 3.0, ((0, 4),)),
        "w_fc2": noise(keys[11], (FF, D), (FF // 4) ** -0.5, 0.125, ((0, 4), (1, 8))),
        "out_bias": noise(keys[12], (D,), 0.5, 3.0, ((0, 4),)),
        "qkv_down": noise(keys[13], (ADAPT * RANK, D), D ** -0.5, 0.125, ((0, 32),), jnp.float32),
        "qkv_up": noise(keys[14], (3, ADAPT * RANK, D), (4 * RANK) ** -0.5, 0.75, ((1, 8), (2, 4)), jnp.float32),
        "dense_down": noise(keys[15], (ADAPT * RANK, D), (D // 64) ** -0.5, 1.0, ((0, 8), (1, 4)), jnp.float32),
        "dense_up": noise(keys[16], (ADAPT * RANK, D), (4 * RANK) ** -0.5, 0.75, ((0, 32),), jnp.float32),
        "fc1_down": noise(keys[17], (ADAPT * RANK, D), D ** -0.5, 0.125, ((0, 32),), jnp.float32),
        "fc1_up": noise(keys[18], (ADAPT * RANK, FF), (4 * RANK) ** -0.5, 0.75, ((0, 8), (1, 4)), jnp.float32),
        "fc2_down": noise(keys[19], (ADAPT * RANK, FF), (FF // 4) ** -0.5, 0.125, ((0, 8), (1, 4)), jnp.float32),
        "fc2_up": noise(keys[20], (ADAPT * RANK, D), (4 * RANK) ** -0.5, 0.75, ((0, 32),), jnp.float32),
    }


epsilon = 1e-05
exact_dot = lax.Precision.HIGHEST
masked_score = -1e+30

@jax.custom_vjp
def low(v):
    return lax.optimization_barrier(v.astype(jnp.bfloat16)).astype(jnp.float32)

@jax.custom_vjp
def low_back(v):
    return v

def low_keep(v):
    return (low(v), None)

def low_pass(kept, grad):
    return (grad,)

def back_keep(v):
    return (v, None)

def back_low(kept, grad):
    return (low(grad),)
low.defvjp(low_keep, low_pass)
low_back.defvjp(back_keep, back_low)

def rotary_tables():
    half_rot = ROT // 2
    places = jnp.arange(SLOT, dtype=jnp.float32)
    frequency = 1.0 / 10000.0 ** (jnp.arange(half_rot, dtype=jnp.float32) * 2.0 / ROT)
    phases = places[:, None] * frequency[None, :]
    return (jnp.cos(phases)[:, None, :], jnp.sin(phases)[:, None, :])

def rotate(tensor, cosine_table, sine_table):
    half_rot = ROT // 2
    first_half = tensor[..., :half_rot]
    second_half = tensor[..., half_rot:ROT]
    return jnp.concatenate([first_half * cosine_table - second_half * sine_table, second_half * cosine_table + first_half * sine_table, tensor[..., ROT:]], -1)

def gelu_tanh(inner_value):
    return 0.5 * inner_value * (1.0 + jnp.tanh(0.7978845608028654 * (inner_value + 0.044715 * inner_value * inner_value * inner_value)))

def high_dot(left, right):
    return jnp.dot(left, right, precision=exact_dot)

def adapter_rows(matrix, row_start, axis_pos):
    return lax.dynamic_slice_in_dim(matrix, row_start, RANK, axis_pos)

def layer(values_in, adapters, frozen, seq_length, adapter_pick):
    qkv_down, qkv_up, dense_down, dense_up, fc1_down, fc1_up, fc2_down, fc2_up = adapters
    ln_gain, ln_bias, w_qkv, qkv_bias, w_dense, w_fc1, fc1_bias, w_fc2, out_bias = frozen
    row_start = (adapter_pick * RANK).astype(jnp.int32)
    centred = values_in - lax.optimization_barrier(jnp.mean(values_in, -1, keepdims=True))
    scale_inv = lax.rsqrt(lax.optimization_barrier(jnp.mean(centred * centred, -1, keepdims=True)) + epsilon)
    normalized_input = low(centred * scale_inv * ln_gain + ln_bias)
    mix_qkv = high_dot(normalized_input, adapter_rows(qkv_down, row_start, 0).T)
    projected_rows = jnp.einsum('ld,cde->cle', normalized_input, w_qkv, precision=exact_dot) + qkv_bias[:, None, :]
    projected_rows = projected_rows + jnp.einsum('lr,cre->cle', mix_qkv, adapter_rows(qkv_up, row_start, 1), precision=exact_dot)
    projected_rows = low_back(projected_rows).reshape(3, SLOT, HEADS, HD)
    cosine_table, sine_table = rotary_tables()
    queries = low(rotate(projected_rows[0], cosine_table, sine_table))
    keys_all = low(rotate(projected_rows[1], cosine_table, sine_table))
    values_all = low(projected_rows[2])
    places = jnp.arange(SLOT)
    allowed = (places[None, :] <= places[:, None]) & (places[None, :] < seq_length)
    scores = low_back(jnp.einsum('qhe,khe->hqk', queries, keys_all, precision=exact_dot) * 0.125)
    scores = jnp.where(allowed[None], scores, masked_score)
    largest = lax.optimization_barrier(jnp.max(scores, -1, keepdims=True))
    weights = jnp.exp(scores - largest)
    probs = weights / lax.optimization_barrier(jnp.sum(weights, -1, keepdims=True))
    attention_output = jnp.einsum('hqk,khe->qhe', low(probs), values_all, precision=exact_dot).reshape(SLOT, D)
    attention_output = low(low_back(attention_output))
    mix_fc1 = high_dot(normalized_input, adapter_rows(fc1_down, row_start, 0).T)
    hidden_state = low_back(high_dot(normalized_input, w_fc1) + fc1_bias + high_dot(mix_fc1, adapter_rows(fc1_up, row_start, 0)))
    activated_rows = low(gelu_tanh(hidden_state))
    mix_dense = high_dot(attention_output, adapter_rows(dense_down, row_start, 0).T)
    mix_fc2 = high_dot(activated_rows, adapter_rows(fc2_down, row_start, 0).T)
    branch = high_dot(attention_output, w_dense) + high_dot(mix_dense, adapter_rows(dense_up, row_start, 0))
    branch = branch + high_dot(activated_rows, w_fc2) + high_dot(mix_fc2, adapter_rows(fc2_up, row_start, 0))
    keep_rows = (places < seq_length).astype(jnp.float32)[:, None]
    return keep_rows * (values_in + branch + out_bias)

def reference(tokens, cotangent, lengths, adapter_index, ln_gain, ln_bias, w_qkv, qkv_bias, w_dense, w_fc1, fc1_bias, w_fc2, out_bias, qkv_down, qkv_up, dense_down, dense_up, fc1_down, fc1_up, fc2_down, fc2_up):
    frozen = tuple((item.astype(jnp.float32) for item in (ln_gain, ln_bias, w_qkv, qkv_bias, w_dense, w_fc1, fc1_bias, w_fc2, out_bias)))
    adapters = (qkv_down, qkv_up, dense_down, dense_up, fc1_down, fc1_up, fc2_down, fc2_up)

    def one_sequence(carried, item):
        seq_tokens, seq_grad, seq_length, adapter_pick = item

        def forward(values_in, adapter_set):
            return layer(values_in, adapter_set, frozen, seq_length, adapter_pick)
        result, pull = jax.vjp(forward, seq_tokens.astype(jnp.float32), adapters)
        input_part, adapter_part = pull(seq_grad.astype(jnp.float32))
        carried = jax.tree.map(lambda left, right: left + right, carried, adapter_part)
        return (carried, (result.astype(jnp.bfloat16), input_part.astype(jnp.bfloat16)))
    start_grads = jax.tree.map(jnp.zeros_like, adapters)
    totals, (results, input_grads) = lax.scan(one_sequence, start_grads, (tokens, cotangent, lengths, adapter_index))
    return (results, input_grads, totals[0], totals[1], totals[2], totals[3], totals[4], totals[5], totals[6], totals[7])
```

```python
import functools

import jax
import jax.numpy as jnp
import numpy as np
from jax import lax
from jax.experimental import pallas as pl
from jax.experimental.pallas import tpu as pltpu
from jax.sharding import PartitionSpec as P

HD = 64
ROT = 32
RANK = 16
SLOT = 1024
EPSILON = 1e-05
MASKED = -1e30
BF16 = jnp.bfloat16
F32 = jnp.float32
ANY = pl.BlockSpec(memory_space=pl.ANY)
TILE = 256


def mm(left, right):
    return jnp.dot(left, right, preferred_element_type=F32)


def mm_nt(left, right):
    return lax.dot_general(left, right, (((1,), (1,)), ((), ())), preferred_element_type=F32)


def mm_tn(left, right):
    return lax.dot_general(left, right, (((0,), (0,)), ((), ())), preferred_element_type=F32)


def rotary_tables():
    half = ROT // 2
    places = np.arange(SLOT, dtype=np.float32)
    frequency = np.float32(1.0) / np.float32(10000.0) ** (
        np.arange(half, dtype=np.float32) * np.float32(2.0) / np.float32(ROT)
    )
    phases = (places[:, None] * frequency[None, :]).astype(np.float32)
    cosine, sine = np.cos(phases), np.sin(phases)
    zero = np.zeros_like(sine)
    rest = np.zeros((SLOT, HD - ROT), np.float32)
    cos_head = np.concatenate([cosine, cosine, rest + 1.0], 1)
    up_head = np.concatenate([-sine, zero, rest], 1)
    down_head = np.concatenate([zero, sine, rest], 1)
    return tuple(
        jnp.asarray(np.concatenate([t, t], 1), F32) for t in (cos_head, up_head, down_head)
    )


def rotate(value, cos, up, down):
    return (
        value * cos
        + pltpu.roll(value, 128 - ROT // 2, axis=1) * up
        + pltpu.roll(value, ROT // 2, axis=1) * down
    )


def deal(lengths, adapter_index, groups, local_seqs):
    count = lengths.shape[0]
    pos = jnp.arange(count, dtype=jnp.int32)
    ranking = lengths * count + pos
    rank = jnp.sum((ranking[None, :] > ranking[:, None]).astype(jnp.int32), 1)
    round_num = rank // groups
    within = rank % groups
    target = jnp.where(round_num % 2 == 0, within, groups - 1 - within)
    place = target * local_seqs + round_num
    chosen = (place[None, :] == pos[:, None]).astype(jnp.int32)

    def pick(values):
        return jnp.sum(chosen * values[None, :], 1).astype(jnp.int32)

    return pick(pos), pick(lengths), pick(adapter_index)


def move_rows_kernel(order, source, target, sem, *, scatter):
    def copy(i):
        j = order[i]
        if scatter:
            return pltpu.make_async_copy(source.at[i], target.at[j], sem.at[i])
        return pltpu.make_async_copy(source.at[j], target.at[i], sem.at[i])

    for i in range(source.shape[0]):
        copy(i).start()
    for i in range(source.shape[0]):
        copy(i).wait()


def move_rows(values, order, scatter):
    return pl.pallas_call(
        functools.partial(move_rows_kernel, scatter=scatter),
        out_shape=jax.ShapeDtypeStruct(values.shape, values.dtype),
        grid_spec=pltpu.PrefetchScalarGridSpec(
            num_scalar_prefetch=1,
            grid=(1,),
            in_specs=[ANY],
            out_specs=ANY,
            scratch_shapes=[pltpu.SemaphoreType.DMA((values.shape[0],))],
        ),
        cost_estimate=pl.CostEstimate(
            flops=0, transcendentals=0, bytes_accessed=4 * values.size
        ),
        name="scatter_rows" if scatter else "gather_rows",
    )(order, values)


def weight_copies(kind, refs, order, target, sem, stacked):
    count = refs[0].shape[0] if stacked else len(refs)
    rows = target.shape[1 if kind in ("q", "lane") else 0]
    width = rows // count
    copies = []
    for s in range(count):
        source = refs[0].at[s] if stacked else refs[s]
        offset = s * width if stacked else pl.multiple_of(order[s] * width, width)
        if kind == "q":
            place = target.at[:, pl.ds(offset, width), :]
        elif kind == "row":
            place = target.at[pl.ds(offset, width), :]
        else:
            place = target.at[:, pl.ds(offset, width)]
        copies.append(pltpu.make_async_copy(source, place, sem.at[s]))
    return copies


def first_step():
    return (pl.program_id(0) == 0) & (pl.program_id(1) == 0)


def norm_kernel(meta, a0, a1, a2, a3, gain, bias, normed, stats, row):
    member = meta[0]
    share = a0.shape[-1]
    for r, ref in enumerate((a0, a1, a2, a3)):
        offset = pl.multiple_of((member ^ r) * share, share)
        row[:, pl.ds(offset, share)] = ref[:, 0].reshape(row.shape[0], share).astype(F32)
    value = row[...]
    mean = jnp.mean(value, -1, keepdims=True)
    centred = value - mean
    scale = lax.rsqrt(jnp.mean(centred * centred, -1, keepdims=True) + EPSILON)
    normed[...] = (centred * scale * gain[...] + bias[...]).astype(BF16)
    lane = lax.broadcasted_iota(jnp.int32, stats.shape, 1)
    stats[...] = jnp.where(lane == 0, mean, scale)


def qkv_kernel(
    stacked, count, meta, order, normed, local_maps, full_maps, bias, cos, up, down, *rest
):
    weights, rest = rest[:count], rest[count:]
    queries, keys, values, mixes, w, sem = rest

    @pl.when(first_step())
    def _():
        copies = weight_copies("q", weights, order, w, sem, stacked)
        for c in copies:
            c.start()
        for c in copies:
            c.wait()

    x = normed[...]
    d = x.shape[1]
    share = queries.shape[1]
    maps = jnp.concatenate([full_maps[:, 0:d], full_maps[:, d : 2 * d]], 0)
    mix = mm_nt(x, maps)
    mixes[...] = mix
    mix_low = mix[:, :RANK].astype(BF16)
    for c, out in enumerate((queries, keys, values)):
        value = mm(x, w[c]) + bias[c : c + 1, :] + mm(
            mix_low, local_maps[:, c * share : (c + 1) * share]
        )
        if c == 2:
            out[...] = value.astype(BF16)
        else:
            for j in range(share // 128):
                part = value[:, j * 128 : (j + 1) * 128]
                out[:, j * 128 : (j + 1) * 128] = rotate(
                    part, cos[...], up[...], down[...]
                ).astype(BF16)


def branch_kernel(
    stacked, count, places, meta, order, a0, a1, a2, a3, local_maps, full_maps, *rest
):
    weights, rest = rest[:count], rest[count:]
    branch, attn_grad, backs, row, w, sem = rest

    @pl.when(first_step())
    def _():
        copies = weight_copies("lane", weights, order, w, sem, stacked)
        for c in copies:
            c.start()
        for c in copies:
            c.wait()

    member = meta[0]
    length = meta[1 + pl.program_id(0)]
    share = a0.shape[-1]
    d = row.shape[1]
    dense_at = places
    for r, ref in enumerate((a0, a1, a2, a3)):
        offset = pl.multiple_of((member ^ r) * share, share)
        row[:, pl.ds(offset, share)] = ref[:, 0].reshape(row.shape[0], share)
    slot = pl.program_id(1) * row.shape[0] + lax.broadcasted_iota(jnp.int32, (row.shape[0], 1), 0)
    keep = (slot < length).astype(F32)
    value = (row[...].astype(F32) * keep).astype(BF16)
    branch[...] = value
    maps = jnp.concatenate([full_maps[:, 2 * d : 3 * d], full_maps[:, 3 * d : 4 * d]], 0)
    back = mm_nt(value, maps)
    backs[...] = back
    attn_grad[...] = (
        mm_nt(value, w[...])
        + mm(back[:, :RANK].astype(BF16), local_maps[:, dense_at : dense_at + share])
    ).astype(BF16)


def attention_kernel(
    meta, queries, keys, values, out_grad, cos, up, down, attended, dq, dk, dv, dk_sum, dv_sum
):
    length = meta[1 + pl.program_id(0)]
    rows = TILE
    heads = 128 // HD
    dk_sum[...] = jnp.zeros_like(dk_sum)
    dv_sum[...] = jnp.zeros_like(dv_sum)
    for i in range(SLOT // rows):
        at = i * rows
        n = at + rows
        row_id = at + lax.broadcasted_iota(jnp.int32, (rows, n), 0)
        col_id = lax.broadcasted_iota(jnp.int32, (rows, n), 1)
        allowed = (col_id <= row_id) & (col_id < length)
        outs = []
        dqs = []
        for h in range(heads):
            lanes = slice(h * HD, (h + 1) * HD)
            q = queries[at:n, lanes]
            k = keys[0:n, lanes]
            v = values[0:n, lanes]
            g = out_grad[at:n, lanes]
            score = jnp.where(allowed, mm_nt(q, k) * 0.125, MASKED)
            top = jnp.max(score, -1, keepdims=True)
            weight = jnp.exp(score - top)
            probs = weight * (1.0 / jnp.sum(weight, -1, keepdims=True))
            low = probs.astype(BF16)
            outs.append(mm(low, v))
            prob_grad = mm_nt(g, v)
            inner = jnp.sum(probs * prob_grad, -1, keepdims=True)
            score_grad = (probs * (prob_grad - inner)).astype(BF16)
            dqs.append(mm(score_grad, k) * 0.125)
            dk_sum[h, 0:n, :] += mm_tn(score_grad, q) * 0.125
            dv_sum[h, 0:n, :] += mm_tn(low, g)
        attended[at:n, :] = jnp.concatenate(outs, 1).astype(BF16)
        dq[at:n, :] = rotate(
            jnp.concatenate(dqs, 1), cos[at:n, :], -up[at:n, :], -down[at:n, :]
        ).astype(BF16)
    for i in range(SLOT // rows):
        at = i * rows
        n = at + rows
        total = jnp.concatenate([dk_sum[h, at:n, :] for h in range(heads)], 1)
        dk[at:n, :] = rotate(total, cos[at:n, :], -up[at:n, :], -down[at:n, :]).astype(BF16)
        dv[at:n, :] = jnp.concatenate([dv_sum[h, at:n, :] for h in range(heads)], 1).astype(BF16)


def layer_kernel(
    stacked,
    counts,
    places,
    meta,
    order,
    normed,
    branch,
    attended,
    dq,
    dk,
    dv,
    mixes,
    backs,
    local_maps,
    full_maps,
    fc1_bias,
    gain,
    ln_bias,
    *rest,
):
    refs = []
    for count in counts:
        refs.append(rest[:count])
        rest = rest[count:]
    outs, grads = rest[0:4], rest[4:8]
    row_sums, grad_local, grad_full = rest[8:11]
    wq, wd, w1, w2, out_sum, grad_sum, sem = rest[11:]

    @pl.when(first_step())
    def _():
        copies = []
        for i, (kind, target) in enumerate(
            (("q", wq), ("lane", wd), ("row", w1), ("lane", w2))
        ):
            copies += weight_copies(kind, refs[i], order, target, sem.at[i], stacked[i])
        for c in copies:
            c.start()
        for c in copies:
            c.wait()

    @pl.when(pl.program_id(1) == 0)
    def _():
        grad_local[...] = jnp.zeros_like(grad_local)
        grad_full[...] = jnp.zeros_like(grad_full)

    member = meta[0]
    d = normed.shape[1]
    share = attended.shape[1]
    ff = w1.shape[1]
    dense_at, fc1_at, fc2_at = places
    x = normed[...]
    b = branch[...]
    att = attended[...]
    mix = mixes[...].astype(BF16)
    back = backs[...].astype(BF16)
    mix_qkv, mix_fc1 = mix[:, :RANK], mix[:, RANK:]
    back_dense, back_fc2 = back[:, :RANK], back[:, RANK:]
    mix_dense = mm_nt(att, local_maps[:, dense_at : dense_at + share])
    grad_local[0, :, dense_at : dense_at + share] += mm_tn(back_dense, att)
    out_sum[...] = mm(att, wd[...])
    back_qkv = jnp.zeros((x.shape[0], RANK), F32)
    for c, part in enumerate((dq, dk, dv)):
        value = part[...]
        lanes = slice(c * share, (c + 1) * share)
        back_qkv += mm_nt(value, local_maps[:, lanes])
        grad_local[0, :, lanes] += mm_tn(mix_qkv, value)
        if c == 0:
            grad_sum[...] = mm_nt(value, wq[c])
        else:
            grad_sum[...] += mm_nt(value, wq[c])
    mix_fc2 = jnp.zeros((x.shape[0], RANK), F32)
    back_fc1 = jnp.zeros((x.shape[0], RANK), F32)
    step = 512
    for at in range(0, ff, step):
        lanes = slice(at, at + step)
        up_at = slice(fc1_at + at, fc1_at + at + step)
        down_at = slice(fc2_at + at, fc2_at + at + step)
        v = mm(x, w1[:, lanes]) + fc1_bias[:, lanes] + mm(mix_fc1, local_maps[:, up_at])
        square = v * v
        t = jnp.tanh(0.7978845608028654 * (v + 0.044715 * v * square))
        half = 0.5 * (1.0 + t)
        act = (v * half).astype(BF16)
        slope = half + (0.5 * 0.7978845608028654) * v * (1.0 - t * t) * (
            1.0 + (3.0 * 0.044715) * square
        )
        pull = mm_nt(b, w2[lanes, :]) + mm(back_fc2, local_maps[:, down_at])
        hidden_grad = (pull * slope).astype(BF16)
        out_sum[...] += mm(act, w2[lanes, :])
        grad_sum[...] += mm_nt(hidden_grad, w1[:, lanes])
        mix_fc2 += mm_nt(act, local_maps[:, down_at])
        back_fc1 += mm_nt(hidden_grad, local_maps[:, up_at])
        grad_local[0, :, up_at] += mm_tn(mix_fc1, hidden_grad)
        grad_local[0, :, down_at] += mm_tn(back_fc2, act)
    out_mix = jnp.concatenate([mix_dense, mix_fc2], 1).astype(BF16)
    in_mix = jnp.concatenate([back_qkv, back_fc1], 1).astype(BF16)
    out_sum[...] += mm(
        out_mix, jnp.concatenate([full_maps[:, 2 * d : 3 * d], full_maps[:, 3 * d : 4 * d]], 0)
    )
    grad_sum[...] += mm(
        in_mix, jnp.concatenate([full_maps[:, 0:d], full_maps[:, d : 2 * d]], 0)
    )
    in_update = mm_tn(in_mix, x)
    out_update = mm_tn(out_mix, b)
    grad_full[0, :, 0:d] += in_update[:RANK]
    grad_full[0, :, d : 2 * d] += in_update[RANK:]
    grad_full[0, :, 2 * d : 3 * d] += out_update[:RANK]
    grad_full[0, :, 3 * d : 4 * d] += out_update[RANK:]
    total = grad_sum[...]
    first = jnp.sum(total * gain[...], -1, keepdims=True)
    second = jnp.sum(total * (x.astype(F32) - ln_bias[...]), -1, keepdims=True)
    lane = lax.broadcasted_iota(jnp.int32, (x.shape[0], 128), 1)
    sums = jnp.where(lane == 0, first, second)
    row_sums[...] = jnp.transpose(sums)[0:8, :]
    width = d // 4
    for r in range(4):
        offset = pl.multiple_of((member ^ r) * width, width)
        outs[r][...] = out_sum[:, pl.ds(offset, width)].astype(BF16)
        grads[r][...] = grad_sum[:, pl.ds(offset, width)].astype(BF16)


def out_kernel(meta, x, part, first, second, bias, out):
    length = meta[1 + pl.program_id(0)]
    rows, share = part.shape
    slot = pl.program_id(1) * rows + lax.broadcasted_iota(jnp.int32, (rows, 1), 0)
    keep = (slot < length).astype(F32)
    total = part[...].astype(F32) + first[...].astype(F32) + second[...].astype(F32)
    value = keep * (x[:, 0].reshape(rows, share).astype(F32) + total + bias[...])
    out[:, 0] = value.astype(BF16).reshape(out.shape[0], out.shape[2], share)


def grad_kernel(meta, x, cot, part, first, second, stats, row_sums, gain, out, *, d):
    length = meta[1 + pl.program_id(0)]
    rows, share = part.shape
    slot = pl.program_id(1) * rows + lax.broadcasted_iota(jnp.int32, (rows, 1), 0)
    keep = (slot < length).astype(F32)
    total = part[...].astype(F32) + first[...].astype(F32) + second[...].astype(F32)
    mean, scale = stats[:, 0:1], stats[:, 1:2]
    unit = (x[:, 0].reshape(rows, share).astype(F32) - mean) * scale
    sums = jnp.transpose(
        jnp.concatenate([row_sums[...], jnp.zeros((120, rows), F32)], 0)
    ) * (1.0 / d)
    value = scale * (total * gain[...] - sums[:, 0:1] - unit * sums[:, 1:2])
    value += keep * cot[:, 0].reshape(rows, share).astype(F32)
    out[:, 0] = value.astype(BF16).reshape(out.shape[0], out.shape[2], share)


def local(
    tokens,
    cotangent,
    lengths,
    adapter_index,
    ln_gain,
    ln_bias,
    w_qkv,
    qkv_bias,
    w_dense,
    w_fc1,
    fc1_bias,
    w_fc2,
    out_bias,
    qkv_down,
    qkv_up,
    dense_down,
    dense_up,
    fc1_down,
    fc1_up,
    fc2_down,
    fc2_up,
):
    groups = lax.axis_size("dp")
    members = lax.axis_size("mp")
    group = lax.axis_index("dp")
    member = lax.axis_index("mp")
    seqs = tokens.shape[0] // groups
    block, share = tokens.shape[1], tokens.shape[2]
    d = share * members
    ff = w_fc1.shape[1]
    tiles = SLOT // TILE
    per_tile = TILE // block
    count_rows = seqs * SLOT
    permutation, dealt_lengths, dealt_adapters = deal(lengths, adapter_index, groups, seqs)
    my_lengths = lax.dynamic_slice_in_dim(dealt_lengths, group * seqs, seqs)
    my_adapters = lax.dynamic_slice_in_dim(dealt_adapters, group * seqs, seqs)
    meta = jnp.concatenate([member[None].astype(jnp.int32), my_lengths, my_adapters])

    def entered(values):
        dealt = move_rows(values, permutation, False)
        mine = lax.all_to_all(dealt, "dp", split_axis=0, concat_axis=0, tiled=True)
        across = lax.ppermute(mine, "mp", [(i, i ^ 2) for i in range(members)])
        beside = lax.ppermute(mine, "mp", [(i, i ^ 1) for i in range(members)])
        both = lax.ppermute(across, "mp", [(i, i ^ 1) for i in range(members)])
        shape = (groups, seqs, block, share)
        return tuple(a.reshape(shape) for a in (mine, beside, across, both))

    rows_in = entered(tokens)
    grads_in = entered(cotangent)

    wide = (d // groups) % 128 == 0

    def gathered(weight, axis):
        if wide:
            return lax.all_gather(weight, "dp", axis=0, tiled=False)
        return lax.all_gather(weight, "dp", axis=axis, tiled=True)[None]

    order = jnp.arange(groups, dtype=jnp.int32)
    all_qkv = gathered(w_qkv, 1)
    local_part = jnp.concatenate(
        [qkv_up[0], qkv_up[1], qkv_up[2], dense_down, fc1_up, fc2_down], 1
    ).astype(BF16)
    full_part = jnp.concatenate([qkv_down, fc1_down, dense_up, fc2_up], 1).astype(BF16)
    local_maps = lax.all_gather(local_part, "dp", axis=0, tiled=True)
    full_maps = lax.all_gather(full_part, ("dp", "mp"), axis=0, tiled=True)
    all_dense = gathered(w_dense, 1)
    all_fc1 = gathered(w_fc1, 0)
    all_fc2 = gathered(w_fc2, 1)
    slots = all_fc1.shape[0]
    cols = local_part.shape[1]
    dense_at = 3 * share
    fc1_at = dense_at + share
    fc2_at = fc1_at + ff

    cos, up, down = rotary_tables()
    gain_row = ln_gain[None, :]
    bias_row = ln_bias[None, :]

    piece = pl.BlockSpec((per_tile, 1, block, share), lambda s, t, *_: (t, s, 0, 0))
    wide_row = pl.BlockSpec((TILE, d), lambda s, t, *_: (s * tiles + t, 0))
    share_row = pl.BlockSpec((TILE, share), lambda s, t, *_: (s * tiles + t, 0))
    stat_row = pl.BlockSpec((TILE, 128), lambda s, t, *_: (s * tiles + t, 0))
    mix_row = pl.BlockSpec((TILE, 2 * RANK), lambda s, t, *_: (s * tiles + t, 0))
    table_row = pl.BlockSpec((TILE, 128), lambda s, t, *_: (t, 0))
    local_map = pl.BlockSpec((RANK, cols), lambda s, t, meta, *_: (meta[1 + seqs + s], 0))
    full_map = pl.BlockSpec((RANK, 4 * d), lambda s, t, meta, *_: (meta[1 + seqs + s], 0))

    def whole(shape):
        return pl.BlockSpec(shape, lambda s, t, *_: tuple(0 for _ in shape))

    def shaped(*shape, dtype=BF16):
        return jax.ShapeDtypeStruct(shape, dtype)

    def cost(flops, nbytes, exps=0):
        return pl.CostEstimate(
            flops=int(flops), transcendentals=int(exps), bytes_accessed=int(nbytes)
        )

    limit = pltpu.CompilerParams(vmem_limit_bytes=58 * 1024 * 1024)

    normed, stats = pl.pallas_call(
        norm_kernel,
        out_shape=(shaped(count_rows, d), shaped(count_rows, 128, dtype=F32)),
        grid_spec=pltpu.PrefetchScalarGridSpec(
            num_scalar_prefetch=1,
            grid=(seqs, tiles),
            in_specs=[piece] * 4 + [whole((1, d))] * 2,
            out_specs=[wide_row, stat_row],
            scratch_shapes=[pltpu.VMEM((TILE, d), F32)],
        ),
        compiler_params=limit,
        cost_estimate=cost(10 * count_rows * d, 4 * count_rows * d),
        name="norm_rows",
    )(meta, *rows_in, gain_row, bias_row)

    queries, keys, values, mixes = pl.pallas_call(
        functools.partial(qkv_kernel, True, 1),
        out_shape=(
            shaped(count_rows, share),
            shaped(count_rows, share),
            shaped(count_rows, share),
            shaped(count_rows, 2 * RANK, dtype=F32),
        ),
        grid_spec=pltpu.PrefetchScalarGridSpec(
            num_scalar_prefetch=2,
            grid=(seqs, tiles),
            in_specs=[wide_row, local_map, full_map, whole((3, share))]
            + [table_row] * 3
            + [ANY],
            out_specs=[share_row, share_row, share_row, mix_row],
            scratch_shapes=[
                pltpu.VMEM((3, d, share), BF16),
                pltpu.SemaphoreType.DMA((slots,)),
            ],
        ),
        compiler_params=limit,
        cost_estimate=cost(6 * count_rows * d * share, 16 * 2**20),
        name="project_rows",
    )(meta, order, normed, local_maps, full_maps, qkv_bias.astype(F32), cos, up, down, all_qkv)

    branch, attn_grad, backs = pl.pallas_call(
        functools.partial(branch_kernel, True, 1, dense_at),
        out_shape=(
            shaped(count_rows, d),
            shaped(count_rows, share),
            shaped(count_rows, 2 * RANK, dtype=F32),
        ),
        grid_spec=pltpu.PrefetchScalarGridSpec(
            num_scalar_prefetch=2,
            grid=(seqs, tiles),
            in_specs=[piece] * 4 + [local_map, full_map, ANY],
            out_specs=[wide_row, share_row, mix_row],
            scratch_shapes=[
                pltpu.VMEM((TILE, d), BF16),
                pltpu.VMEM((share, d), BF16),
                pltpu.SemaphoreType.DMA((slots,)),
            ],
        ),
        compiler_params=limit,
        cost_estimate=cost(2 * count_rows * d * share, 20 * 2**20),
        name="branch_rows",
    )(meta, order, *grads_in, local_maps, full_maps, all_dense)

    pair = pl.BlockSpec((SLOT, 128), lambda s, h, *_: (s, h))
    attended, dq, dk, dv = pl.pallas_call(
        attention_kernel,
        out_shape=(shaped(count_rows, share),) * 4,
        grid_spec=pltpu.PrefetchScalarGridSpec(
            num_scalar_prefetch=1,
            grid=(seqs, share // 128),
            in_specs=[pair] * 4 + [whole((SLOT, 128))] * 3,
            out_specs=[pair] * 4,
            scratch_shapes=[
                pltpu.VMEM((128 // HD, SLOT, HD), F32),
                pltpu.VMEM((128 // HD, SLOT, HD), F32),
            ],
        ),
        compiler_params=limit,
        cost_estimate=cost(
            6 * 4 * count_rows * SLOT * share, 16 * 2**20, count_rows * SLOT * share // HD
        ),
        name="attend_rows",
    )(meta, queries, keys, values, attn_grad, cos, up, down)

    grad_block = pl.BlockSpec((1, RANK, cols), lambda s, t, *_: (s, 0, 0))
    full_block = pl.BlockSpec((1, RANK, 4 * d), lambda s, t, *_: (s, 0, 0))
    sum_block = pl.BlockSpec((8, TILE), lambda s, t, *_: (0, s * tiles + t))
    results = pl.pallas_call(
        functools.partial(layer_kernel, (True,) * 4, (1,) * 4, (dense_at, fc1_at, fc2_at)),
        out_shape=(shaped(count_rows, share),) * 8
        + (
            shaped(8, count_rows, dtype=F32),
            shaped(seqs, RANK, cols, dtype=F32),
            shaped(seqs, RANK, 4 * d, dtype=F32),
        ),
        grid_spec=pltpu.PrefetchScalarGridSpec(
            num_scalar_prefetch=2,
            grid=(seqs, tiles),
            in_specs=[wide_row, wide_row]
            + [share_row] * 4
            + [mix_row] * 2
            + [local_map, full_map, whole((1, ff)), whole((1, d)), whole((1, d))]
            + [ANY] * 4,
            out_specs=[share_row] * 8 + [sum_block, grad_block, full_block],
            scratch_shapes=[
                pltpu.VMEM((3, d, share), BF16),
                pltpu.VMEM((share, d), BF16),
                pltpu.VMEM((d, ff), BF16),
                pltpu.VMEM((ff, d), BF16),
                pltpu.VMEM((TILE, d), F32),
                pltpu.VMEM((TILE, d), F32),
                pltpu.SemaphoreType.DMA((4, slots)),
            ],
        ),
        compiler_params=limit,
        cost_estimate=cost(
            8 * count_rows * d * ff + 8 * count_rows * d * share, 80 * 2**20, count_rows * ff
        ),
        name="layer_rows",
    )(
        meta,
        order,
        normed,
        branch,
        attended,
        dq,
        dk,
        dv,
        mixes,
        backs,
        local_maps,
        full_maps,
        fc1_bias.astype(F32)[None, :],
        gain_row,
        bias_row,
        all_qkv,
        all_dense,
        all_fc1,
        all_fc2,
    )
    outs, grads = results[0:4], results[4:8]
    row_sums, grad_local, grad_full = results[8:11]

    def near(value):
        return lax.ppermute(value, "mp", [(i, i ^ 1) for i in range(members)])

    def far(value):
        return lax.ppermute(value, "mp", [(i, i ^ 2) for i in range(members)])

    def add_low(left, right):
        return (left.astype(F32) + right.astype(F32)).astype(BF16)

    def reduced(parts):
        second = far(add_low(parts[2], near(parts[3])))
        first = near(parts[1])
        return parts[0], first, second

    half_sums = row_sums + near(row_sums)
    row_totals = half_sums + far(half_sums)
    out_parts = reduced(outs)
    grad_parts = reduced(grads)
    out_shape = shaped(groups, seqs, block, share)
    out_rows = pl.pallas_call(
        out_kernel,
        out_shape=out_shape,
        grid_spec=pltpu.PrefetchScalarGridSpec(
            num_scalar_prefetch=1,
            grid=(seqs, tiles),
            in_specs=[piece] + [share_row] * 3 + [whole((1, share))],
            out_specs=piece,
        ),
        compiler_params=limit,
        cost_estimate=cost(6 * count_rows * share, 10 * count_rows * share),
        name="output_rows",
    )(meta, rows_in[0], *out_parts, out_bias.astype(F32)[None, :])
    back_out = lax.all_to_all(
        out_rows.reshape(groups * seqs, block, share),
        "dp",
        split_axis=0,
        concat_axis=0,
        tiled=True,
    )
    my_gain = lax.dynamic_slice_in_dim(gain_row, member * share, share, 1)
    grad_rows = pl.pallas_call(
        functools.partial(grad_kernel, d=d),
        out_shape=out_shape,
        grid_spec=pltpu.PrefetchScalarGridSpec(
            num_scalar_prefetch=1,
            grid=(seqs, tiles),
            in_specs=[piece] * 2
            + [share_row] * 3
            + [stat_row, sum_block, whole((1, share))],
            out_specs=piece,
        ),
        compiler_params=limit,
        cost_estimate=cost(10 * count_rows * share, 12 * count_rows * share),
        name="input_grad_rows",
    )(meta, rows_in[0], grads_in[0], *grad_parts, stats, row_totals, my_gain)
    back_grad = lax.all_to_all(
        grad_rows.reshape(groups * seqs, block, share),
        "dp",
        split_axis=0,
        concat_axis=0,
        tiled=True,
    )
    output = move_rows(back_out, permutation, True)
    input_grad = move_rows(back_grad, permutation, True)

    rows_full = grad_full.reshape(seqs * RANK * 4, members, share).astype(BF16)
    traded = lax.all_to_all(
        jnp.transpose(rows_full, (1, 0, 2)), "mp", split_axis=0, concat_axis=0, tiled=True
    )
    my_full = jnp.sum(traded.astype(F32), 0).reshape(seqs, RANK, 4 * share)
    update = jnp.concatenate([grad_local, my_full], 2)
    adapters = qkv_down.shape[0] * groups * members // RANK
    spread = jnp.zeros((adapters, RANK, cols + 4 * share), F32)
    for s in range(seqs):
        here = jnp.arange(adapters, dtype=jnp.int32) == my_adapters[s]
        spread = spread + jnp.where(here[:, None, None], update[s][None], 0.0)
    owned = adapters * RANK // groups
    sent = spread.astype(BF16).reshape(groups, owned, cols + 4 * share)
    arrived = lax.all_to_all(sent, "dp", split_axis=0, concat_axis=0, tiled=True)
    summed = jnp.sum(arrived.astype(F32), 0)
    split_rows = summed[:, cols:].reshape(members, owned // members, 4 * share).astype(BF16)
    mine = lax.all_to_all(split_rows, "mp", split_axis=0, concat_axis=0, tiled=True)
    mine = mine.astype(F32).reshape(members, owned // members, 4, share)
    mine = jnp.transpose(mine, (2, 1, 0, 3)).reshape(4, owned // members, d)
    return (
        output,
        input_grad,
        mine[0],
        jnp.stack([summed[:, c * share : (c + 1) * share] for c in range(3)], 0),
        summed[:, dense_at:fc1_at],
        mine[2],
        mine[1],
        summed[:, fc1_at:fc2_at],
        summed[:, fc2_at:cols],
        mine[3],
    )


def solution(mesh):
    return jax.shard_map(
        local,
        mesh=mesh,
        in_specs=(
            P(None, "dp", "mp"),
            P(None, "dp", "mp"),
            P(),
            P(),
            P(),
            P(),
            P(None, "dp", "mp"),
            P(None, "mp"),
            P("mp", "dp"),
            P("dp", "mp"),
            P("mp"),
            P("mp", "dp"),
            P("mp"),
            P(("dp", "mp"), None),
            P(None, "dp", "mp"),
            P("dp", "mp"),
            P(("dp", "mp"), None),
            P(("dp", "mp"), None),
            P("dp", "mp"),
            P("dp", "mp"),
            P(("dp", "mp"), None),
        ),
        out_specs=(
            P(None, "dp", "mp"),
            P(None, "dp", "mp"),
            P(("dp", "mp"), None),
            P(None, "dp", "mp"),
            P("dp", "mp"),
            P(("dp", "mp"), None),
            P(("dp", "mp"), None),
            P("dp", "mp"),
            P("dp", "mp"),
            P(("dp", "mp"), None),
        ),
        check_vma=False,
    )
```

```python
import functools

import jax
import jax.numpy as jnp
import numpy as np
from jax import lax
from jax.experimental import pallas as pl
from jax.experimental.pallas import tpu as pltpu
from jax.sharding import PartitionSpec as P

HD = 64
ROT = 32
RANK = 16
SLOT = 1024
EPSILON = 1e-05
MASKED = -1e30
BF16 = jnp.bfloat16
F32 = jnp.float32
ANY = pl.BlockSpec(memory_space=pl.ANY)
TILE = 256
COST = 1.0


def after(value, *others):
    return lax.optimization_barrier((value,) + others)[0] if others else value


def mm(left, right):
    return jnp.dot(left, right, preferred_element_type=F32)


def mm_nt(left, right):
    return lax.dot_general(left, right, (((1,), (1,)), ((), ())), preferred_element_type=F32)


def mm_tn(left, right):
    return lax.dot_general(left, right, (((0,), (0,)), ((), ())), preferred_element_type=F32)


def rotary_tables():
    half = ROT // 2
    places = np.arange(SLOT, dtype=np.float32)
    frequency = np.float32(1.0) / np.float32(10000.0) ** (
        np.arange(half, dtype=np.float32) * np.float32(2.0) / np.float32(ROT)
    )
    phases = (places[:, None] * frequency[None, :]).astype(np.float32)
    cosine, sine = np.cos(phases), np.sin(phases)
    zero = np.zeros_like(sine)
    rest = np.zeros((SLOT, HD - ROT), np.float32)
    cos_head = np.concatenate([cosine, cosine, rest + 1.0], 1)
    up_head = np.concatenate([-sine, zero, rest], 1)
    down_head = np.concatenate([zero, sine, rest], 1)
    return tuple(
        jnp.asarray(np.concatenate([t, t], 1), F32) for t in (cos_head, up_head, down_head)
    )


def rotate(value, cos, up, down):
    return (
        value * cos
        + pltpu.roll(value, 128 - ROT // 2, axis=1) * up
        + pltpu.roll(value, ROT // 2, axis=1) * down
    )


def deal(lengths, adapter_index, groups, local_seqs):
    count = lengths.shape[0]
    pos = jnp.arange(count, dtype=jnp.int32)
    ranking = lengths * count + pos
    rank = jnp.sum((ranking[None, :] > ranking[:, None]).astype(jnp.int32), 1)
    round_num = rank // groups
    within = rank % groups
    target = jnp.where(round_num % 2 == 0, within, groups - 1 - within)
    place = target * local_seqs + round_num
    chosen = (place[None, :] == pos[:, None]).astype(jnp.int32)

    def pick(values):
        return jnp.sum(chosen * values[None, :], 1).astype(jnp.int32)

    return pick(pos), pick(lengths), pick(adapter_index)


def gather_rows_kernel(order, source, target, held, sem_in, sem_out):
    count = source.shape[0]
    fetch = [
        pltpu.make_async_copy(source.at[order[i]], held.at[i], sem_in.at[i]) for i in range(count)
    ]
    store = [pltpu.make_async_copy(held.at[i], target.at[i], sem_out.at[i]) for i in range(count)]
    for copy in fetch:
        copy.start()
    for i in range(count):
        fetch[i].wait()
        store[i].start()
    for copy in store:
        copy.wait()


def scatter_rows_kernel(order, *refs):
    seqs = len(refs) - 4
    sources, (target, held, sem_in, sem_out) = refs[:seqs], refs[seqs:]
    groups = sources[0].shape[0]
    fetch = []
    store = []
    for g in range(groups):
        for s in range(seqs):
            i = g * seqs + s
            fetch.append(pltpu.make_async_copy(sources[s].at[g], held.at[i], sem_in.at[i]))
            store.append(pltpu.make_async_copy(held.at[i], target.at[order[i]], sem_out.at[i]))
    for copy in fetch:
        copy.start()
    for take, put in zip(fetch, store, strict=True):
        take.wait()
        put.start()
    for copy in store:
        copy.wait()


def move_rows(kernel, order, arrays, name):
    count = sum(a.shape[0] for a in arrays)
    rest = arrays[0].shape[1:]
    size = sum(a.size for a in arrays)
    return pl.pallas_call(
        kernel,
        out_shape=jax.ShapeDtypeStruct((count,) + rest, BF16),
        grid_spec=pltpu.PrefetchScalarGridSpec(
            num_scalar_prefetch=1,
            grid=(1,),
            in_specs=[ANY] * len(arrays),
            out_specs=ANY,
            scratch_shapes=[
                pltpu.VMEM((count,) + rest, BF16),
                pltpu.SemaphoreType.DMA((count,)),
                pltpu.SemaphoreType.DMA((count,)),
            ],
        ),
        compiler_params=pltpu.CompilerParams(vmem_limit_bytes=16 * 1024 * 1024),
        cost_estimate=pl.CostEstimate(flops=0, transcendentals=0, bytes_accessed=int(4 * size * COST)),
        name=name,
    )(order, *arrays)


def weight_copies(kind, refs, order, target, sem, stacked):
    count = refs[0].shape[0] if stacked else len(refs)
    rows = target.shape[1 if kind in ("q", "lane") else 0]
    width = rows // count
    copies = []
    for s in range(count):
        source = refs[0].at[s] if stacked else refs[s]
        offset = s * width if stacked else pl.multiple_of(order[s] * width, width)
        if kind == "q":
            place = target.at[:, pl.ds(offset, width), :]
        elif kind == "row":
            place = target.at[pl.ds(offset, width), :]
        else:
            place = target.at[:, pl.ds(offset, width)]
        copies.append(pltpu.make_async_copy(source, place, sem.at[s]))
    return copies


def mlp_copies(first, second, order, w1, w2, sems):
    if second:
        copies = weight_copies("row", first, order, w1, sems[0], True)
        return copies + weight_copies("lane", second, order, w2, sems[1], True)
    packed = first[0]
    count = packed.shape[0]
    width = w1.shape[0] // count
    copies = []
    for s in range(count):
        lanes = pl.ds(s * width, width)
        copies.append(
            pltpu.make_async_copy(packed.at[s, 0:width, :], w1.at[lanes, :], sems[0].at[s])
        )
        for i in range(0, w2.shape[0], width):
            copies.append(
                pltpu.make_async_copy(
                    packed.at[s, width : 2 * width, i : i + width],
                    w2.at[i : i + width, lanes],
                    sems[1 + i // width].at[s],
                )
            )
    return copies


def first_step():
    return (pl.program_id(0) == 0) & (pl.program_id(1) == 0)


def norm_kernel(meta, a0, a1, a2, a3, gain, bias, normed, stats, row):
    member = meta[0]
    share = a0.shape[-1]
    for r, ref in enumerate((a0, a1, a2, a3)):
        offset = pl.multiple_of((member ^ r) * share, share)
        row[:, pl.ds(offset, share)] = ref[:, 0].reshape(row.shape[0], share).astype(F32)
    value = row[...]
    mean = jnp.mean(value, -1, keepdims=True)
    centred = value - mean
    scale = lax.rsqrt(jnp.mean(centred * centred, -1, keepdims=True) + EPSILON)
    normed[...] = (centred * scale * gain[...] + bias[...]).astype(BF16)
    lane = lax.broadcasted_iota(jnp.int32, stats.shape, 1)
    stats[...] = jnp.where(lane == 0, mean, scale)


def qkv_kernel(
    stacked, count, meta, order, normed, local_maps, full_maps, bias, cos, up, down, *rest
):
    weights, rest = rest[:count], rest[count:]
    queries, keys, values, mixes, w, sem = rest

    @pl.when(first_step())
    def _():
        copies = weight_copies("q", weights, order, w, sem, stacked)
        for c in copies:
            c.start()
        for c in copies:
            c.wait()

    x = normed[...]
    d = x.shape[1]
    share = queries.shape[1]
    maps = jnp.concatenate([full_maps[:, 0:d], full_maps[:, d : 2 * d]], 0)
    mix = mm_nt(x, maps)
    mixes[...] = mix
    mix_low = mix[:, :RANK].astype(BF16)
    for c, out in enumerate((queries, keys, values)):
        value = mm(x, w[c]) + bias[c : c + 1, :] + mm(
            mix_low, local_maps[:, c * share : (c + 1) * share]
        )
        if c == 2:
            out[...] = value.astype(BF16)
        else:
            for j in range(share // 128):
                part = value[:, j * 128 : (j + 1) * 128]
                out[:, j * 128 : (j + 1) * 128] = rotate(
                    part, cos[...], up[...], down[...]
                ).astype(BF16)


def branch_kernel(
    stacked, count, places, meta, order, a0, a1, a2, a3, local_maps, full_maps, token, *rest
):
    weights, rest = rest[:count], rest[count:]
    branch, attn_grad, backs, row, w, sem = rest

    @pl.when(first_step())
    def _():
        copies = weight_copies("lane", weights, order, w, sem, stacked)
        for c in copies:
            c.start()
        for c in copies:
            c.wait()

    member = meta[0]
    length = meta[1 + pl.program_id(0)]
    share = a0.shape[-1]
    d = row.shape[1]
    dense_at = places
    for r, ref in enumerate((a0, a1, a2, a3)):
        offset = pl.multiple_of((member ^ r) * share, share)
        row[:, pl.ds(offset, share)] = ref[:, 0].reshape(row.shape[0], share)
    slot = pl.program_id(1) * row.shape[0] + lax.broadcasted_iota(jnp.int32, (row.shape[0], 1), 0)
    keep = (slot < length).astype(F32)
    value = (row[...].astype(F32) * keep).astype(BF16)
    branch[...] = value
    maps = jnp.concatenate([full_maps[:, 2 * d : 3 * d], full_maps[:, 3 * d : 4 * d]], 0)
    back = mm_nt(value, maps)
    backs[...] = back
    attn_grad[...] = (
        mm_nt(value, w[...])
        + mm(back[:, :RANK].astype(BF16), local_maps[:, dense_at : dense_at + share])
    ).astype(BF16)


def attention_kernel(
    meta, queries, keys, values, out_grad, cos, up, down, attended, dq, dk, dv, dk_sum, dv_sum
):
    length = meta[1 + pl.program_id(0)]
    rows = TILE
    heads = 128 // HD
    dk_sum[...] = jnp.zeros_like(dk_sum)
    dv_sum[...] = jnp.zeros_like(dv_sum)
    for i in range(SLOT // rows):
        at = i * rows
        n = at + rows
        row_id = at + lax.broadcasted_iota(jnp.int32, (rows, n), 0)
        col_id = lax.broadcasted_iota(jnp.int32, (rows, n), 1)
        allowed = (col_id <= row_id) & (col_id < length)
        outs = []
        dqs = []
        for h in range(heads):
            lanes = slice(h * HD, (h + 1) * HD)
            q = queries[at:n, lanes]
            k = keys[0:n, lanes]
            v = values[0:n, lanes]
            g = out_grad[at:n, lanes]
            score = jnp.where(allowed, mm_nt(q, k) * 0.125, MASKED)
            top = jnp.max(score, -1, keepdims=True)
            weight = jnp.exp(score - top)
            probs = weight * (1.0 / jnp.sum(weight, -1, keepdims=True))
            low = probs.astype(BF16)
            outs.append(mm(low, v))
            prob_grad = mm_nt(g, v)
            inner = jnp.sum(probs * prob_grad, -1, keepdims=True)
            score_grad = (probs * (prob_grad - inner)).astype(BF16)
            dqs.append(mm(score_grad, k) * 0.125)
            dk_sum[h, 0:n, :] += mm_tn(score_grad, q) * 0.125
            dv_sum[h, 0:n, :] += mm_tn(low, g)
        attended[at:n, :] = jnp.concatenate(outs, 1).astype(BF16)
        dq[at:n, :] = rotate(
            jnp.concatenate(dqs, 1), cos[at:n, :], -up[at:n, :], -down[at:n, :]
        ).astype(BF16)
    for i in range(SLOT // rows):
        at = i * rows
        n = at + rows
        total = jnp.concatenate([dk_sum[h, at:n, :] for h in range(heads)], 1)
        dk[at:n, :] = rotate(total, cos[at:n, :], -up[at:n, :], -down[at:n, :]).astype(BF16)
        dv[at:n, :] = jnp.concatenate([dv_sum[h, at:n, :] for h in range(heads)], 1).astype(BF16)


def mlp_half(
    x, b, mix_fc1, back_fc2, w1, w2, up_maps, down_maps, fc1_bias, out_sum, grad_sum, grads
):
    mix_fc2 = jnp.zeros((x.shape[0], RANK), F32)
    back_fc1 = jnp.zeros((x.shape[0], RANK), F32)
    step = 512
    for at in range(0, w1.shape[1], step):
        lanes = slice(at, at + step)
        up_map, down_map = up_maps[:, lanes], down_maps[:, lanes]
        v = mm(x, w1[:, lanes]) + fc1_bias[:, lanes] + mm(mix_fc1, up_map)
        square = v * v
        t = jnp.tanh(0.7978845608028654 * (v + 0.044715 * v * square))
        half = 0.5 * (1.0 + t)
        act = (v * half).astype(BF16)
        slope = half + (0.5 * 0.7978845608028654) * v * (1.0 - t * t) * (
            1.0 + (3.0 * 0.044715) * square
        )
        pull = mm_nt(b, w2[lanes, :]) + mm(back_fc2, down_map)
        hidden_grad = (pull * slope).astype(BF16)
        out_sum[...] += mm(act, w2[lanes, :])
        grad_sum[...] += mm_nt(hidden_grad, w1[:, lanes])
        mix_fc2 += mm_nt(act, down_map)
        back_fc1 += mm_nt(hidden_grad, up_map)
        grads[0][:, lanes] += mm_tn(mix_fc1, hidden_grad)
        grads[1][:, lanes] += mm_tn(back_fc2, act)
    return mix_fc2, back_fc1


def run_copies(copies):
    for c in copies:
        c.start()
    for c in copies:
        c.wait()


def split_refs(rest, counts):
    refs = []
    for count in counts:
        refs.append(rest[:count])
        rest = rest[count:]
    return refs, rest


def first_kernel(
    stacked,
    counts,
    meta,
    order,
    normed,
    branch,
    attended,
    dq,
    dk,
    dv,
    mixes,
    backs,
    local_maps,
    full_maps,
    fc1_bias,
    *rest,
):
    refs, rest = split_refs(rest, counts)
    out_sum, grad_sum, carried, grad_local, grad_full = rest[0:5]
    wq, wd, w1, w2, sem = rest[5:]

    @pl.when(first_step())
    def _():
        copies = []
        for i, (kind, target) in enumerate((("q", wq), ("lane", wd))):
            copies += weight_copies(kind, refs[i], order, target, sem.at[i], stacked[i])
        sems = [sem.at[i] for i in range(2, sem.shape[0])]
        run_copies(copies + mlp_copies(refs[2], refs[3], order, w1, w2, sems))

    @pl.when(pl.program_id(1) == 0)
    def _():
        grad_local[...] = jnp.zeros_like(grad_local)
        grad_full[...] = jnp.zeros_like(grad_full)

    d = normed.shape[1]
    share = attended.shape[1]
    fh = w1.shape[1]
    dense_at = 3 * share
    fc1_at = dense_at + share
    fc2_at = fc1_at + 2 * fh
    x = normed[...]
    b = branch[...]
    att = attended[...]
    mix = mixes[...].astype(BF16)
    back = backs[...].astype(BF16)
    mix_qkv, mix_fc1 = mix[:, :RANK], mix[:, RANK:]
    back_dense, back_fc2 = back[:, :RANK], back[:, RANK:]
    dense_map = local_maps[:, dense_at:fc1_at]
    mix_dense = mm_nt(att, dense_map).astype(BF16)
    grad_local[0, :, dense_at:fc1_at] += mm_tn(back_dense, att)
    out_sum[...] = mm(att, wd[...]) + mm(mix_dense, full_maps[:, 2 * d : 3 * d])
    grad_full[0, :, d : 2 * d] += mm_tn(mix_dense, b)
    back_qkv = jnp.zeros((x.shape[0], RANK), F32)
    for c, part in enumerate((dq, dk, dv)):
        value = part[...]
        lanes = slice(c * share, (c + 1) * share)
        back_qkv += mm_nt(value, local_maps[:, lanes])
        grad_local[0, :, lanes] += mm_tn(mix_qkv, value)
        if c == 0:
            grad_sum[...] = mm_nt(value, wq[c])
        else:
            grad_sum[...] += mm_nt(value, wq[c])
    back_qkv = back_qkv.astype(BF16)
    grad_sum[...] += mm(back_qkv, full_maps[:, 0:d])
    grad_full[0, :, 0:d] += mm_tn(back_qkv, x)
    mix_fc2, back_fc1 = mlp_half(
        x,
        b,
        mix_fc1,
        back_fc2,
        w1,
        w2,
        local_maps[:, fc1_at : fc1_at + fh],
        local_maps[:, fc2_at : fc2_at + fh],
        fc1_bias,
        out_sum,
        grad_sum,
        (
            grad_local.at[0, :, fc1_at : fc1_at + fh],
            grad_local.at[0, :, fc1_at + fh : fc1_at + 2 * fh],
        ),
    )
    carried[:, :RANK] = mix_fc2
    carried[:, RANK:] = back_fc1


def last_kernel(
    stacked,
    counts,
    resumed,
    meta,
    order,
    normed,
    branch,
    out_part,
    grad_part,
    mixes,
    backs,
    carried,
    local_maps,
    full_maps,
    fc1_bias,
    gain,
    ln_bias,
    *rest,
):
    refs, rest = split_refs(rest, counts)
    if resumed:
        local_before, full_before = rest[9:11]
        rest = rest[11:]
    outs, grads = rest[0:4], rest[4:8]
    row_sums, grad_local, grad_full = rest[8:11]
    w1, w2, out_sum, grad_sum, sem = rest[11:]

    @pl.when(pl.program_id(0) == 0)
    def _():
        sems = [sem.at[i] for i in range(sem.shape[0])]
        run_copies(mlp_copies(refs[0], refs[1], order, w1, w2, sems))
        if resumed:
            grad_local[...] = local_before[...]
            grad_full[...] = full_before[...]
        else:
            grad_local[...] = jnp.zeros_like(grad_local)
            grad_full[...] = jnp.zeros_like(grad_full)

    member = meta[0]
    d = normed.shape[1]
    fh = w1.shape[1]
    fc1_at = d
    fc2_at = fc1_at + 2 * fh
    x = normed[...]
    b = branch[...]
    mix_fc1 = mixes[:, RANK:].astype(BF16)
    back_fc2 = backs[:, RANK:].astype(BF16)
    out_sum[...] = out_part[...]
    grad_sum[...] = grad_part[...]
    mix_fc2, back_fc1 = mlp_half(
        x,
        b,
        mix_fc1,
        back_fc2,
        w1,
        w2,
        local_maps[:, fc1_at + fh : fc1_at + 2 * fh],
        local_maps[:, fc2_at + fh : fc2_at + 2 * fh],
        fc1_bias,
        out_sum,
        grad_sum,
        (grad_local.at[:, 0:fh], grad_local.at[:, fh : 2 * fh]),
    )
    mix_fc2 = (mix_fc2 + carried[:, :RANK]).astype(BF16)
    back_fc1 = (back_fc1 + carried[:, RANK:]).astype(BF16)
    out_sum[...] += mm(mix_fc2, full_maps[:, 3 * d : 4 * d])
    grad_full[:, d : 2 * d] += mm_tn(mix_fc2, b)
    grad_full[:, 0:d] += mm_tn(back_fc1, x)
    total = grad_sum[...] + mm(back_fc1, full_maps[:, d : 2 * d])
    grad_sum[...] = total
    first = jnp.sum(total * gain[...], -1, keepdims=True)
    second = jnp.sum(total * (x.astype(F32) - ln_bias[...]), -1, keepdims=True)
    lane = lax.broadcasted_iota(jnp.int32, (x.shape[0], 128), 1)
    row_sums[...] = jnp.transpose(jnp.where(lane == 0, first, second))[0:8, :]
    width = d // 4
    for r in range(4):
        offset = pl.multiple_of((member ^ r) * width, width)
        outs[r][...] = out_sum[:, pl.ds(offset, width)].astype(BF16)
        grads[r][...] = grad_sum[:, pl.ds(offset, width)].astype(BF16)


def kept_rows(length, rows):
    slot = pl.program_id(0) * rows + lax.broadcasted_iota(jnp.int32, (rows, 1), 0)
    return (slot < length).astype(F32)


def out_kernel(seq, meta, x, part, first, second, bias, out):
    rows, share = part.shape
    total = part[...].astype(F32) + first[...].astype(F32) + second[...].astype(F32)
    value = x[:, 0].reshape(rows, share).astype(F32) + total + bias[...]
    value = value * kept_rows(meta[1 + seq], rows)
    out[...] = value.astype(BF16).reshape(out.shape)


def grad_kernel(seq, d, meta, x, cot, part, first, second, stats, row_sums, gain, out):
    rows, share = part.shape
    total = part[...].astype(F32) + first[...].astype(F32) + second[...].astype(F32)
    mean, scale = stats[:, 0:1], stats[:, 1:2]
    unit = (x[:, 0].reshape(rows, share).astype(F32) - mean) * scale
    sums = jnp.transpose(
        jnp.concatenate([row_sums[...], jnp.zeros((120, rows), F32)], 0)
    ) * (1.0 / d)
    value = scale * (total * gain[...] - sums[:, 0:1] - unit * sums[:, 1:2])
    value += kept_rows(meta[1 + seq], rows) * cot[:, 0].reshape(rows, share).astype(F32)
    out[...] = value.astype(BF16).reshape(out.shape)


def local(
    tokens,
    cotangent,
    lengths,
    adapter_index,
    ln_gain,
    ln_bias,
    w_qkv,
    qkv_bias,
    w_dense,
    w_fc1,
    fc1_bias,
    w_fc2,
    out_bias,
    qkv_down,
    qkv_up,
    dense_down,
    dense_up,
    fc1_down,
    fc1_up,
    fc2_down,
    fc2_up,
):
    groups = lax.axis_size("dp")
    members = lax.axis_size("mp")
    group = lax.axis_index("dp")
    member = lax.axis_index("mp")
    seqs = tokens.shape[0] // groups
    block, share = tokens.shape[1], tokens.shape[2]
    d = share * members
    ff = w_fc1.shape[1]
    tiles = SLOT // TILE
    per_tile = TILE // block
    count_rows = seqs * SLOT
    permutation, dealt_lengths, dealt_adapters = deal(lengths, adapter_index, groups, seqs)
    my_lengths = lax.dynamic_slice_in_dim(dealt_lengths, group * seqs, seqs)
    my_adapters = lax.dynamic_slice_in_dim(dealt_adapters, group * seqs, seqs)
    meta = jnp.concatenate([member[None].astype(jnp.int32), my_lengths, my_adapters])

    def near(value):
        return lax.ppermute(value, "mp", [(i, i ^ 1) for i in range(members)])

    def far(value):
        return lax.ppermute(value, "mp", [(i, i ^ 2) for i in range(members)])

    def hop(value):
        return near(value[0:8])

    def dealt(values):
        return move_rows(gather_rows_kernel, permutation, (values,), "gather_rows")

    def entered(values):
        return lax.all_to_all(values, "dp", split_axis=0, concat_axis=0, tiled=True)

    def widened(mine, across):
        shape = (groups, seqs, block, share)
        return tuple(a.reshape(shape) for a in (mine, near(mine), across, near(across)))

    dealt_tokens = dealt(tokens)
    my_tokens = entered(dealt_tokens)
    far_tokens = far(my_tokens)

    wide = (d // groups) % 128 == 0
    inner = 2
    outer = groups // inner
    place_out, place_in = group // inner, group % inner

    def gathered(weight, axis):
        if wide:
            return (lax.all_gather(weight, "dp", axis=0, tiled=False),)
        return (lax.all_gather(weight, "dp", axis=axis, tiled=True)[None],)

    def beside(value):
        return lax.ppermute(value, "dp", [(i, i ^ 1) for i in range(groups)])

    def onward(value):
        return lax.ppermute(value, "dp", [(i, (i + inner) % groups) for i in range(groups)])

    def ring(weight, axis, *waits):
        if not wide:
            return gathered(weight, axis), ()
        held = [weight]
        crossed = []
        for k in range(outer - 1):
            step = after(held[k], *waits, *crossed[-1:])
            crossed.append(beside(held[k]))
            held.append(onward(step))
            waits = ()
        done = tuple(held) + tuple(crossed)
        crossed.append(beside(held[-1]))
        return tuple(a for pair in zip(held, crossed, strict=True) for a in pair), done

    order = jnp.stack(
        [
            (place_out - k) % outer * inner + (place_in + j) % inner
            for k in range(outer)
            for j in range(inner)
        ]
    ).astype(jnp.int32)
    all_qkv, ring_early = ring(w_qkv, 1, my_tokens)
    rows_in = widened(my_tokens, after(far_tokens, *ring_early))
    cos, up, down = rotary_tables()
    gain_row = ln_gain[None, :]
    bias_row = ln_bias[None, :]

    piece = pl.BlockSpec((per_tile, 1, block, share), lambda s, t, *_: (t, s, 0, 0))
    wide_row = pl.BlockSpec((TILE, d), lambda s, t, *_: (s * tiles + t, 0))
    share_row = pl.BlockSpec((TILE, share), lambda s, t, *_: (s * tiles + t, 0))
    stat_row = pl.BlockSpec((TILE, 128), lambda s, t, *_: (s * tiles + t, 0))
    mix_row = pl.BlockSpec((TILE, 2 * RANK), lambda s, t, *_: (s * tiles + t, 0))
    table_row = pl.BlockSpec((TILE, 128), lambda s, t, *_: (t, 0))
    cols = 4 * share + 2 * ff
    local_map = pl.BlockSpec((RANK, cols), lambda s, t, meta, *_: (meta[1 + seqs + s], 0))
    full_map = pl.BlockSpec((RANK, 4 * d), lambda s, t, *_: (s, 0))

    def whole(shape):
        return pl.BlockSpec(shape, lambda s, t, *_: tuple(0 for _ in shape))

    def shaped(*shape, dtype=BF16):
        return jax.ShapeDtypeStruct(shape, dtype)

    def cost(flops, nbytes, exps=0):
        return pl.CostEstimate(
            flops=int(flops * COST), transcendentals=int(exps * COST), bytes_accessed=int(nbytes * COST)
        )

    limit = pltpu.CompilerParams(vmem_limit_bytes=58 * 1024 * 1024)

    normed, stats = pl.pallas_call(
        norm_kernel,
        out_shape=(shaped(count_rows, d), shaped(count_rows, 128, dtype=F32)),
        grid_spec=pltpu.PrefetchScalarGridSpec(
            num_scalar_prefetch=1,
            grid=(seqs, tiles),
            in_specs=[piece] * 4 + [whole((1, d))] * 2,
            out_specs=[wide_row, stat_row],
            scratch_shapes=[pltpu.VMEM((TILE, d), F32)],
        ),
        compiler_params=limit,
        cost_estimate=cost(10 * count_rows * d, 4 * count_rows * d),
        name="norm_rows",
    )(meta, *rows_in, gain_row, bias_row)

    my_cotangent = entered(after(dealt(cotangent), *ring_early, *rows_in))
    fh = ff // 2
    local_part = jnp.concatenate(
        [qkv_up[0], qkv_up[1], qkv_up[2], dense_down, fc1_up, fc2_down], 1
    ).astype(BF16)
    cols = local_part.shape[1]
    full_rows = qkv_down.shape[0]
    full_part = jnp.stack([qkv_down, fc1_down, dense_up, fc2_up], 1).astype(BF16)
    full_part = after(full_part, dealt_tokens)
    full_part = jnp.transpose(full_part.reshape(full_rows, 4, members, share), (2, 0, 1, 3))
    full_part = lax.all_to_all(
        full_part.reshape(members, full_rows, 4 * share),
        "mp",
        split_axis=0,
        concat_axis=0,
        tiled=True,
    )
    all_part = jnp.concatenate(
        [local_part, full_part.reshape(members * full_rows, 4 * share)], 1
    )
    all_part = after(all_part, my_tokens)
    local_maps = lax.all_gather(all_part, "dp", axis=0, tiled=True)
    my_maps = jnp.stack(
        [
            lax.dynamic_slice(
                local_maps, (my_adapters[s] * RANK, cols), (RANK, 4 * share)
            )
            for s in range(seqs)
        ]
    ).reshape(seqs * RANK, 4, share)
    full_maps = jnp.transpose(lax.all_gather(my_maps, "mp", axis=0, tiled=False), (1, 2, 0, 3))
    full_maps = full_maps.reshape(seqs * RANK, 4 * d)
    all_dense = gathered(after(w_dense, local_maps), 1)
    w_fc1, w_fc2 = after(w_fc1, my_cotangent), after(w_fc2, my_cotangent)
    my_cotangent = after(my_cotangent, full_maps, *all_qkv)
    far_cotangent = far(my_cotangent)

    def mlp_weights(j):
        first, second = w_fc1[:, j * fh : (j + 1) * fh], w_fc2[j * fh : (j + 1) * fh, :]
        if not wide:
            return gathered(first, 0), gathered(second, 1)
        width = second.shape[1]
        parts = [second[i : i + width] for i in range(0, fh, width)]
        packed = jnp.concatenate([first, jnp.concatenate(parts, 1)], 0)
        return (lax.all_gather(packed, "dp", axis=0, tiled=False),), ()

    halves_fc = [mlp_weights(j) for j in range(2)]
    slots = groups
    dense_at = 3 * share

    queries, keys, values, mixes = pl.pallas_call(
        functools.partial(qkv_kernel, len(all_qkv) == 1, len(all_qkv)),
        out_shape=(
            shaped(count_rows, share),
            shaped(count_rows, share),
            shaped(count_rows, share),
            shaped(count_rows, 2 * RANK, dtype=F32),
        ),
        grid_spec=pltpu.PrefetchScalarGridSpec(
            num_scalar_prefetch=2,
            grid=(seqs, tiles),
            in_specs=[wide_row, local_map, full_map, whole((3, share))]
            + [table_row] * 3
            + [ANY] * len(all_qkv),
            out_specs=[share_row, share_row, share_row, mix_row],
            scratch_shapes=[
                pltpu.VMEM((3, d, share), BF16),
                pltpu.SemaphoreType.DMA((slots,)),
            ],
        ),
        compiler_params=limit,
        cost_estimate=cost(6 * count_rows * d * share, 16 * 2**20),
        name="project_rows",
    )(meta, order, normed, local_maps, full_maps, qkv_bias.astype(F32), cos, up, down, *all_qkv)

    projected = hop(mixes)
    grads_in = widened(my_cotangent, after(far_cotangent, projected))
    branch, attn_grad, backs = pl.pallas_call(
        functools.partial(branch_kernel, len(all_dense) == 1, len(all_dense), dense_at),
        out_shape=(
            shaped(count_rows, d),
            shaped(count_rows, share),
            shaped(count_rows, 2 * RANK, dtype=F32),
        ),
        grid_spec=pltpu.PrefetchScalarGridSpec(
            num_scalar_prefetch=2,
            grid=(seqs, tiles),
            in_specs=[piece] * 4 + [local_map, full_map] + [ANY] * (1 + len(all_dense)),
            out_specs=[wide_row, share_row, mix_row],
            scratch_shapes=[
                pltpu.VMEM((TILE, d), BF16),
                pltpu.VMEM((share, d), BF16),
                pltpu.SemaphoreType.DMA((slots,)),
            ],
        ),
        compiler_params=limit,
        cost_estimate=cost(2 * count_rows * d * share, 20 * 2**20),
        name="branch_rows",
    )(meta, order, *grads_in, local_maps, full_maps, projected, *all_dense)

    pair = pl.BlockSpec((SLOT, 128), lambda s, h, *_: (s, h))
    attended, dq, dk, dv = pl.pallas_call(
        attention_kernel,
        out_shape=(shaped(count_rows, share),) * 4,
        grid_spec=pltpu.PrefetchScalarGridSpec(
            num_scalar_prefetch=1,
            grid=(seqs, share // 128),
            in_specs=[pair] * 4 + [whole((SLOT, 128))] * 3,
            out_specs=[pair] * 4,
            scratch_shapes=[
                pltpu.VMEM((128 // HD, SLOT, HD), F32),
                pltpu.VMEM((128 // HD, SLOT, HD), F32),
            ],
        ),
        compiler_params=limit,
        cost_estimate=cost(
            6 * 4 * count_rows * SLOT * share, 16 * 2**20, count_rows * SLOT * share // HD
        ),
        name="attend_rows",
    )(meta, queries, keys, values, attn_grad, cos, up, down)

    def per_seq(*shape):
        return pl.BlockSpec((1,) + shape, lambda s, t, *_: (s,) + tuple(0 for _ in shape))

    first_weights = (all_qkv, all_dense) + halves_fc[0]
    counts = tuple(len(w) for w in first_weights)
    first_cols = 4 * share + 2 * fh
    bias_all = fc1_bias.astype(F32)[None, :]
    out_part, grad_part, carried, local_first, full_first = pl.pallas_call(
        functools.partial(first_kernel, tuple(c == 1 for c in counts), counts),
        out_shape=(
            shaped(count_rows, d, dtype=F32),
            shaped(count_rows, d, dtype=F32),
            shaped(count_rows, 2 * RANK, dtype=F32),
            shaped(seqs, RANK, first_cols, dtype=F32),
            shaped(seqs, RANK, 2 * d, dtype=F32),
        ),
        grid_spec=pltpu.PrefetchScalarGridSpec(
            num_scalar_prefetch=2,
            grid=(seqs, tiles),
            in_specs=[wide_row, wide_row]
            + [share_row] * 4
            + [mix_row] * 2
            + [local_map, full_map, whole((1, fh))]
            + [ANY] * sum(counts),
            out_specs=[
                wide_row,
                wide_row,
                mix_row,
                per_seq(RANK, first_cols),
                per_seq(RANK, 2 * d),
            ],
            scratch_shapes=[
                pltpu.VMEM((3, d, share), BF16),
                pltpu.VMEM((share, d), BF16),
                pltpu.VMEM((d, fh), BF16),
                pltpu.VMEM((fh, d), BF16),
                pltpu.SemaphoreType.DMA((3 + fh // (d // slots), slots)),
            ],
        ),
        compiler_params=limit,
        cost_estimate=cost(
            8 * count_rows * d * fh + 8 * count_rows * d * share, 80 * 2**20, count_rows * fh
        ),
        name="first_half",
    )(
        meta,
        order,
        normed,
        branch,
        attended,
        dq,
        dk,
        dv,
        mixes,
        backs,
        local_maps,
        full_maps,
        bias_all[:, :fh],
        *[a for w in first_weights for a in w],
    )

    def add_low(left, right):
        return (left.astype(F32) + right.astype(F32)).astype(BF16)

    def half_reduced(parts):
        return add_low(parts[2], near(parts[3]))

    def reduced(parts, half):
        return parts[0], near(parts[1]), far(half)

    adapters = qkv_down.shape[0] * groups * members // RANK
    owned = adapters * RANK // groups

    blocks = RANK // owned
    each = owned // members

    def spread_sums(local_grad, full_grad):
        width = full_grad.shape[2]
        rows = full_grad.astype(BF16).reshape(seqs, blocks, members, each, width)
        rows = jnp.transpose(rows, (2, 0, 1, 3, 4)).reshape(members, seqs * blocks * each, width)
        traded = lax.all_to_all(rows, "mp", split_axis=0, concat_axis=0, tiled=True)
        mine = jnp.sum(traded.astype(F32), 0).reshape(seqs, blocks * each * members, width // members)
        update = jnp.concatenate([local_grad, mine], 2)
        spread = jnp.zeros((adapters,) + update.shape[1:], F32)
        for s in range(seqs):
            here = jnp.arange(adapters, dtype=jnp.int32) == my_adapters[s]
            spread = spread + jnp.where(here[:, None, None], update[s][None], 0.0)
        return spread.astype(BF16).reshape(groups, owned, update.shape[2])

    def owned_sums(arrived, width):
        summed = jnp.sum(arrived.astype(F32), 0)
        mine = summed[:, width:].reshape(each, -1, d)
        return summed, jnp.transpose(mine, (1, 0, 2))

    sent_first = spread_sums(local_first, full_first)
    arrived_first = entered(sent_first)
    last_weights = halves_fc[1]
    counts = tuple(len(w) for w in last_weights)
    my_gain = lax.dynamic_slice_in_dim(gain_row, member * share, share, 1)
    def last_call(seq, first_tile, count, token, given):
        def rows_of(width):
            return pl.BlockSpec((TILE, width), lambda t, *_: (seq * tiles + first_tile + t, 0))

        def fixed(shape, first=0):
            return pl.BlockSpec(shape, lambda t, *_: (first,) + (0,) * (len(shape) - 1))

        def own(width):
            return pl.BlockSpec((TILE, width), lambda t, *_: (first_tile + t, 0))

        sum_block = pl.BlockSpec((8, TILE), lambda t, *_: (0, first_tile + t))
        own_map = pl.BlockSpec((RANK, cols), lambda t, meta, *_: (meta[1 + seqs + seq], 0))
        operands = (
            token,
            order,
            normed,
            branch,
            out_part,
            grad_part,
            mixes,
            backs,
            carried,
            local_maps,
            full_maps,
            bias_all[:, fh:],
            gain_row,
            bias_row,
            *[a for w in last_weights for a in w],
        )
        given = tuple(given)
        return pl.pallas_call(
            functools.partial(
                last_kernel, tuple(c == 1 for c in counts), counts, len(given) > 0
            ),
            out_shape=(shaped(SLOT, share),) * 8
            + (
                shaped(8, SLOT, dtype=F32),
                shaped(RANK, 2 * fh, dtype=F32),
                shaped(RANK, 2 * d, dtype=F32),
            ),
            grid_spec=pltpu.PrefetchScalarGridSpec(
                num_scalar_prefetch=2,
                grid=(count,),
                in_specs=[rows_of(d)] * 4
                + [rows_of(2 * RANK)] * 3
                + [own_map, fixed((RANK, 4 * d), seq)]
                + [fixed((1, fh)), fixed((1, d)), fixed((1, d))]
                + [ANY] * (sum(counts) + 9 * (len(given) > 0))
                + [fixed((RANK, 2 * fh)), fixed((RANK, 2 * d))] * (len(given) > 0),
                out_specs=[own(share)] * 8
                + [sum_block, fixed((RANK, 2 * fh)), fixed((RANK, 2 * d))],
                scratch_shapes=[
                    pltpu.VMEM((d, fh), BF16),
                    pltpu.VMEM((fh, d), BF16),
                    pltpu.VMEM((TILE, d), F32),
                    pltpu.VMEM((TILE, d), F32),
                    pltpu.SemaphoreType.DMA((1 + fh // (d // slots), slots)),
                ],
            ),
            input_output_aliases={len(operands) + i: i for i in range(len(given))},
            compiler_params=limit,
            cost_estimate=cost(
                8 * count * TILE * d * fh, 10 * count * 2**20, count * TILE * fh
            ),
            name="last_half",
        )(*operands, *given)

    def out_call(seq, parts):
        return pl.pallas_call(
            functools.partial(out_kernel, seq),
            out_shape=shaped(groups, block, share),
            grid_spec=pltpu.PrefetchScalarGridSpec(
                num_scalar_prefetch=1,
                grid=(tiles,),
                in_specs=[piece_of(seq)] + [own_row] * 3 + [row_block],
                out_specs=back_block,
            ),
            compiler_params=limit,
            cost_estimate=cost(6 * SLOT * share, 10 * SLOT * share),
            name="output_rows",
        )(meta, rows_in[0], *parts, out_bias.astype(F32)[None, :])

    def grad_call(seq, parts, totals):
        return pl.pallas_call(
            functools.partial(grad_kernel, seq, d),
            out_shape=shaped(groups, block, share),
            grid_spec=pltpu.PrefetchScalarGridSpec(
                num_scalar_prefetch=1,
                grid=(tiles,),
                in_specs=[piece_of(seq)] * 2
                + [own_row] * 3
                + [
                    pl.BlockSpec((TILE, 128), lambda t, *_: (seq * tiles + t, 0)),
                    pl.BlockSpec((8, TILE), lambda t, *_: (0, t)),
                    row_block,
                ],
                out_specs=back_block,
            ),
            compiler_params=limit,
            cost_estimate=cost(10 * SLOT * share, 12 * SLOT * share),
            name="input_grad_rows",
        )(meta, rows_in[0], grads_in[0], *parts, stats, totals, my_gain)

    def piece_of(seq):
        return pl.BlockSpec((per_tile, 1, block, share), lambda t, *_: (t, seq, 0, 0))

    own_row = pl.BlockSpec((TILE, share), lambda t, *_: (t, 0))
    row_block = pl.BlockSpec((1, share), lambda t, *_: (0, 0))
    back_block = pl.BlockSpec((per_tile, block, share), lambda t, *_: (t, 0, 0))

    def near_sums(results, *waits):
        parts = [after(results[r], *waits) if r in (2, 6) else results[r] for r in range(8)]
        half_sums = results[8] + near(results[8])
        return parts, half_reduced(parts[0:4]), half_reduced(parts[4:8]), half_sums

    def far_sums(parts, half_out, half_grad, half_sums):
        return (
            reduced(parts[0:4], half_out),
            reduced(parts[4:8], half_grad),
            half_sums + far(half_sums),
        )

    back_outs = []
    back_grads = []
    local_last = []
    full_last = []
    waits = (arrived_first,)
    token = after(meta, sent_first)
    for seq in range(seqs):
        if seq == 0:
            results = last_call(seq, 0, tiles, token, ())
        else:
            results = last_call(seq, 0, tiles // 2, token, ())
            out_rows = out_call(seq - 1, after(out_parts, results[9]))
            results = last_call(
                seq, tiles // 2, tiles - tiles // 2, after(meta, out_rows), results
            )
            back_outs.append(entered(after(out_rows, *back_grads)))
        local_last.append(results[9])
        full_last.append(results[10])
        halves = near_sums(results, *waits)
        if seq > 0:
            grad_rows = grad_call(seq - 1, after(grad_parts, results[9]), row_totals)
            back_grads.append(entered(after(grad_rows, back_outs[-1])))
        out_parts, grad_parts, row_totals = far_sums(*halves)
        token = after(meta, *halves[1:])
        waits = (out_parts[2], grad_parts[2])
    sent_last = spread_sums(jnp.stack(local_last), after(jnp.stack(full_last), *halves[1:]))
    out_rows = out_call(seqs - 1, out_parts)
    back_outs.append(entered(after(out_rows, *back_grads)))
    grad_rows = grad_call(seqs - 1, grad_parts, row_totals)
    arrived_last = entered(after(sent_last, grad_rows, back_outs[-1]))
    back_grads.append(entered(after(grad_rows, arrived_last)))
    output = move_rows(scatter_rows_kernel, permutation, back_outs, "scatter_rows")
    input_grad = move_rows(scatter_rows_kernel, permutation, back_grads, "scatter_rows")

    first_sums, first_full = owned_sums(arrived_first, first_cols)
    last_sums, last_full = owned_sums(arrived_last, 2 * fh)
    fc1_at = 4 * share
    return (
        output,
        input_grad,
        first_full[0],
        jnp.stack([first_sums[:, c * share : (c + 1) * share] for c in range(3)], 0),
        first_sums[:, dense_at:fc1_at],
        first_full[1],
        last_full[0],
        jnp.concatenate([first_sums[:, fc1_at : fc1_at + fh], last_sums[:, 0:fh]], 1),
        jnp.concatenate(
            [first_sums[:, fc1_at + fh : fc1_at + 2 * fh], last_sums[:, fh : 2 * fh]], 1
        ),
        last_full[1],
    )


def solution(mesh):
    return jax.shard_map(
        local,
        mesh=mesh,
        in_specs=(
            P(None, "dp", "mp"),
            P(None, "dp", "mp"),
            P(),
            P(),
            P(),
            P(),
            P(None, "dp", "mp"),
            P(None, "mp"),
            P("mp", "dp"),
            P("dp", "mp"),
            P("mp"),
            P("mp", "dp"),
            P("mp"),
            P(("dp", "mp"), None),
            P(None, "dp", "mp"),
            P("dp", "mp"),
            P(("dp", "mp"), None),
            P(("dp", "mp"), None),
            P("dp", "mp"),
            P("dp", "mp"),
            P(("dp", "mp"), None),
        ),
        out_specs=(
            P(None, "dp", "mp"),
            P(None, "dp", "mp"),
            P(("dp", "mp"), None),
            P(None, "dp", "mp"),
            P("dp", "mp"),
            P(("dp", "mp"), None),
            P(("dp", "mp"), None),
            P("dp", "mp"),
            P("dp", "mp"),
            P(("dp", "mp"), None),
        ),
        check_vma=False,
    )
```

```python
import functools

import jax
import jax.numpy as jnp
import numpy as np
from jax import lax
from jax.experimental import pallas as pl
from jax.experimental.pallas import tpu as pltpu
from jax.sharding import PartitionSpec as P

HD = 64
ROT = 32
RANK = 16
SLOT = 1024
EPSILON = 1e-05
MASKED = -1e30
BF16 = jnp.bfloat16
F32 = jnp.float32
ANY = pl.BlockSpec(memory_space=pl.ANY)
TILE = 256
BIG = 256
COST = 1.0


def after(value, *others):
    return lax.optimization_barrier((value,) + others)[0] if others else value


def mm(left, right):
    return jnp.dot(left, right, preferred_element_type=F32)


def mm_nt(left, right):
    return lax.dot_general(left, right, (((1,), (1,)), ((), ())), preferred_element_type=F32)


def mm_tn(left, right):
    return lax.dot_general(left, right, (((0,), (0,)), ((), ())), preferred_element_type=F32)


def rotary_tables():
    half = ROT // 2
    places = np.arange(SLOT, dtype=np.float32)
    frequency = np.float32(1.0) / np.float32(10000.0) ** (
        np.arange(half, dtype=np.float32) * np.float32(2.0) / np.float32(ROT)
    )
    phases = (places[:, None] * frequency[None, :]).astype(np.float32)
    cosine, sine = np.cos(phases), np.sin(phases)
    zero = np.zeros_like(sine)
    rest = np.zeros((SLOT, HD - ROT), np.float32)
    cos_head = np.concatenate([cosine, cosine, rest + 1.0], 1)
    up_head = np.concatenate([-sine, zero, rest], 1)
    down_head = np.concatenate([zero, sine, rest], 1)
    return tuple(
        jnp.asarray(np.concatenate([t, t], 1), F32) for t in (cos_head, up_head, down_head)
    )


def rotate(value, cos, up, down):
    return (
        value * cos
        + pltpu.roll(value, 128 - ROT // 2, axis=1) * up
        + pltpu.roll(value, ROT // 2, axis=1) * down
    )


def deal(lengths, adapter_index, groups, local_seqs):
    count = lengths.shape[0]
    pos = jnp.arange(count, dtype=jnp.int32)
    ranking = lengths * count + pos
    rank = jnp.sum((ranking[None, :] > ranking[:, None]).astype(jnp.int32), 1)
    round_num = rank // groups
    within = rank % groups
    target = jnp.where(round_num % 2 == 0, within, groups - 1 - within)
    place = target * local_seqs + round_num
    chosen = (place[None, :] == pos[:, None]).astype(jnp.int32)

    def pick(values):
        return jnp.sum(chosen * values[None, :], 1).astype(jnp.int32)

    return pick(pos), pick(lengths), pick(adapter_index)


def gather_rows_kernel(order, source, target, held, sem_in, sem_out):
    count = source.shape[0]
    fetch = [
        pltpu.make_async_copy(source.at[order[i]], held.at[i], sem_in.at[i]) for i in range(count)
    ]
    store = [pltpu.make_async_copy(held.at[i], target.at[i], sem_out.at[i]) for i in range(count)]
    for copy in fetch:
        copy.start()
    for i in range(count):
        fetch[i].wait()
        store[i].start()
    for copy in store:
        copy.wait()


def scatter_rows_kernel(order, *refs):
    seqs = len(refs) - 4
    sources, (target, held, sem_in, sem_out) = refs[:seqs], refs[seqs:]
    groups = sources[0].shape[0]
    fetch = []
    store = []
    for g in range(groups):
        for s in range(seqs):
            i = g * seqs + s
            fetch.append(pltpu.make_async_copy(sources[s].at[g], held.at[i], sem_in.at[i]))
            store.append(pltpu.make_async_copy(held.at[i], target.at[order[i]], sem_out.at[i]))
    for copy in fetch:
        copy.start()
    for take, put in zip(fetch, store, strict=True):
        take.wait()
        put.start()
    for copy in store:
        copy.wait()


def move_rows(kernel, order, arrays, name):
    count = sum(a.shape[0] for a in arrays)
    rest = arrays[0].shape[1:]
    size = sum(a.size for a in arrays)
    return pl.pallas_call(
        kernel,
        out_shape=jax.ShapeDtypeStruct((count,) + rest, BF16),
        grid_spec=pltpu.PrefetchScalarGridSpec(
            num_scalar_prefetch=1,
            grid=(1,),
            in_specs=[ANY] * len(arrays),
            out_specs=ANY,
            scratch_shapes=[
                pltpu.VMEM((count,) + rest, BF16),
                pltpu.SemaphoreType.DMA((count,)),
                pltpu.SemaphoreType.DMA((count,)),
            ],
        ),
        compiler_params=pltpu.CompilerParams(vmem_limit_bytes=16 * 1024 * 1024),
        cost_estimate=pl.CostEstimate(flops=0, transcendentals=0, bytes_accessed=int(4 * size * COST)),
        name=name,
    )(order, *arrays)


def weight_copies(kind, refs, order, target, sem, stacked):
    count = refs[0].shape[0] if stacked else len(refs)
    rows = target.shape[1 if kind in ("q", "lane") else 0]
    width = rows // count
    copies = []
    for s in range(count):
        source = refs[0].at[s] if stacked else refs[s]
        offset = s * width if stacked else pl.multiple_of(order[s] * width, width)
        if kind == "q":
            place = target.at[:, pl.ds(offset, width), :]
        elif kind == "row":
            place = target.at[pl.ds(offset, width), :]
        else:
            place = target.at[:, pl.ds(offset, width)]
        copies.append(pltpu.make_async_copy(source, place, sem.at[s]))
    return copies


def mlp_copies(first, second, order, w1, w2, sems):
    if second:
        copies = weight_copies("row", first, order, w1, sems[0], True)
        return copies + weight_copies("lane", second, order, w2, sems[1], True)
    packed = first[0]
    count = packed.shape[0]
    width = w1.shape[0] // count
    copies = []
    for s in range(count):
        lanes = pl.ds(s * width, width)
        copies.append(
            pltpu.make_async_copy(packed.at[s, 0:width, :], w1.at[lanes, :], sems[0].at[s])
        )
        for i in range(0, w2.shape[0], width):
            copies.append(
                pltpu.make_async_copy(
                    packed.at[s, width : 2 * width, i : i + width],
                    w2.at[i : i + width, lanes],
                    sems[1 + i // width].at[s],
                )
            )
    return copies


def first_step():
    return (pl.program_id(0) == 0) & (pl.program_id(1) == 0)


def norm_kernel(meta, a0, a1, a2, a3, gain, bias, normed, stats, row):
    member = meta[0]
    share = a0.shape[-1]
    for r, ref in enumerate((a0, a1, a2, a3)):
        offset = pl.multiple_of((member ^ r) * share, share)
        row[:, pl.ds(offset, share)] = ref[:, 0].reshape(row.shape[0], share).astype(F32)
    value = row[...]
    mean = jnp.mean(value, -1, keepdims=True)
    centred = value - mean
    scale = lax.rsqrt(jnp.mean(centred * centred, -1, keepdims=True) + EPSILON)
    normed[...] = (centred * scale * gain[...] + bias[...]).astype(BF16)
    lane = lax.broadcasted_iota(jnp.int32, stats.shape, 1)
    stats[...] = jnp.where(lane == 0, mean, scale)


def qkv_kernel(
    stacked, count, meta, order, normed, local_maps, full_maps, bias, cos, up, down, *rest
):
    weights, rest = rest[:count], rest[count:]
    queries, keys, values, mixes, w, sem = rest

    @pl.when(first_step())
    def _():
        copies = weight_copies("q", weights, order, w, sem, stacked)
        for c in copies:
            c.start()
        for c in copies:
            c.wait()

    x = normed[...]
    d = x.shape[1]
    share = queries.shape[1]
    maps = jnp.concatenate([full_maps[:, 0:d], full_maps[:, d : 2 * d]], 0)
    mix = mm_nt(x, maps)
    mixes[:, : 2 * RANK] = mix
    mix_low = mix[:, :RANK].astype(BF16)
    for c, out in enumerate((queries, keys, values)):
        value = mm(x, w[c]) + bias[c : c + 1, :] + mm(
            mix_low, local_maps[:, c * share : (c + 1) * share]
        )
        if c == 2:
            out[...] = value.astype(BF16)
        else:
            for j in range(share // 128):
                part = value[:, j * 128 : (j + 1) * 128]
                out[:, j * 128 : (j + 1) * 128] = rotate(
                    part, cos[...], up[...], down[...]
                ).astype(BF16)


def branch_kernel(
    stacked, count, places, meta, order, a0, a1, a2, a3, local_maps, full_maps, token, *rest
):
    weights, rest = rest[:count], rest[count:]
    branch, attn_grad, backs, row, w, sem = rest

    @pl.when(first_step())
    def _():
        copies = weight_copies("lane", weights, order, w, sem, stacked)
        for c in copies:
            c.start()
        for c in copies:
            c.wait()

    member = meta[0]
    length = meta[1 + pl.program_id(0)]
    share = a0.shape[-1]
    d = row.shape[1]
    dense_at = places
    for r, ref in enumerate((a0, a1, a2, a3)):
        offset = pl.multiple_of((member ^ r) * share, share)
        row[:, pl.ds(offset, share)] = ref[:, 0].reshape(row.shape[0], share)
    slot = pl.program_id(1) * row.shape[0] + lax.broadcasted_iota(jnp.int32, (row.shape[0], 1), 0)
    keep = (slot < length).astype(F32)
    value = (row[...].astype(F32) * keep).astype(BF16)
    branch[...] = value
    maps = jnp.concatenate([full_maps[:, 2 * d : 3 * d], full_maps[:, 3 * d : 4 * d]], 0)
    back = mm_nt(value, maps)
    backs[:, : 2 * RANK] = back
    attn_grad[...] = (
        mm_nt(value, w[...])
        + mm(back[:, :RANK].astype(BF16), local_maps[:, dense_at : dense_at + share])
    ).astype(BF16)


def attention_kernel(
    meta,
    queries,
    keys,
    values,
    out_grad,
    cos,
    up,
    down,
    attended,
    dq,
    dk,
    dv,
    dk_sum,
    dv_sum,
    outside,
):
    length = meta[1 + pl.program_id(0)]
    rows = 512
    heads = 128 // HD

    @pl.when(pl.program_id(1) == 0)
    def _():
        place = lax.broadcasted_iota(jnp.int32, outside.shape, 0)
        outside[...] = jnp.where(place < length, 0.0, MASKED)

    zero = jnp.zeros((), BF16)
    head_of = lax.broadcasted_iota(jnp.int32, (SLOT, 128), 1) // HD
    own_keys = [jnp.where(head_of == h, keys[...], zero) for h in range(heads)]
    own_values = [jnp.where(head_of == h, values[...], zero) for h in range(heads)]
    below = lax.broadcasted_iota(jnp.int32, (rows, rows), 0) <= lax.broadcasted_iota(
        jnp.int32, (rows, rows), 1
    )
    dk_sum[...] = jnp.zeros_like(dk_sum)
    dv_sum[...] = jnp.zeros_like(dv_sum)
    for at in range(0, SLOT, rows):
        n = at + rows
        all_q = queries[at:n, :] * jnp.asarray(0.125, BF16)
        all_g = out_grad[at:n, :]
        out = jnp.zeros((128, rows), F32)
        dq_sum = jnp.zeros((128, rows), F32)
        for h in range(heads):
            q = jnp.where(head_of[:rows] == h, all_q, zero)
            g = jnp.where(head_of[:rows] == h, all_g, zero)
            score = mm_nt(keys[0:n, :], q)
            score = score + jnp.concatenate([outside[0:n, :]] * (rows // 128), 1)
            corner = jnp.where(below, score[at:n], MASKED)
            score = jnp.concatenate([score[0:at], corner], 0) if at else corner
            weight = jnp.exp(score - jnp.max(score, 0, keepdims=True))
            probs = weight * (1.0 / jnp.sum(weight, 0, keepdims=True))
            low = probs.astype(BF16)
            prob_grad = mm_nt(values[0:n, :], g)
            inner = jnp.sum(probs * prob_grad, 0, keepdims=True)
            score_grad = (probs * (prob_grad - inner)).astype(BF16)
            out += mm_tn(own_values[h][0:n], low)
            dq_sum += mm_tn(own_keys[h][0:n], score_grad)
            dk_sum[0:n, :] += mm(score_grad, q)
            dv_sum[0:n, :] += mm(low, g)
        attended[at:n, :] = jnp.transpose(out).astype(BF16)
        dq[at:n, :] = rotate(
            jnp.transpose(dq_sum) * 0.125, cos[at:n, :], -up[at:n, :], -down[at:n, :]
        ).astype(BF16)
    dk[...] = rotate(dk_sum[...], cos[...], -up[...], -down[...]).astype(BF16)
    dv[...] = dv_sum[...].astype(BF16)


def mlp_half(
    x, b, mix_fc1, back_fc2, w1, w2, up_maps, down_maps, fc1_bias, active, hidden_grad, grads
):
    step = 512
    for at in range(0, w1.shape[1], step):
        lanes = slice(at, at + step)
        v = mm(x[...], w1[:, lanes]) + fc1_bias[:, lanes] + mm(mix_fc1, up_maps[:, lanes])
        square = v * v
        t = jnp.tanh(0.7978845608028654 * (v + 0.044715 * v * square))
        half = 0.5 * (1.0 + t)
        slope = half + (0.5 * 0.7978845608028654) * v * (1.0 - t * t) * (
            1.0 + (3.0 * 0.044715) * square
        )
        active[:, lanes] = (v * half).astype(BF16)
        pull = mm_nt(b[...], w2[lanes, :]) + mm(back_fc2, down_maps[:, lanes])
        hidden_grad[:, lanes] = (pull * slope).astype(BF16)
    grads[0][...] += mm_tn(mix_fc1, hidden_grad[...])
    grads[1][...] += mm_tn(back_fc2, active[...])
    return mm_nt(active[...], down_maps), mm_nt(hidden_grad[...], up_maps)


def run_copies(copies):
    for c in copies:
        c.start()
    for c in copies:
        c.wait()


def split_refs(rest, counts):
    refs = []
    for count in counts:
        refs.append(rest[:count])
        rest = rest[count:]
    return refs, rest


def first_kernel(
    stacked,
    counts,
    meta,
    order,
    normed,
    branch,
    attended,
    dq,
    dk,
    dv,
    mixes,
    backs,
    local_maps,
    full_maps,
    fc1_bias,
    *rest,
):
    refs, rest = split_refs(rest, counts)
    out_sum, grad_sum, carried, grad_local, grad_full = rest[0:5]
    wq, wd, w1, w2, active, hidden_grad, sem = rest[5:]

    @pl.when(first_step())
    def _():
        copies = []
        for i, (kind, target) in enumerate((("q", wq), ("lane", wd))):
            copies += weight_copies(kind, refs[i], order, target, sem.at[i], stacked[i])
        sems = [sem.at[i] for i in range(2, sem.shape[0])]
        run_copies(copies + mlp_copies(refs[2], refs[3], order, w1, w2, sems))

    @pl.when(pl.program_id(1) == 0)
    def _():
        grad_local[...] = jnp.zeros_like(grad_local)
        grad_full[...] = jnp.zeros_like(grad_full)

    d = normed.shape[1]
    share = attended.shape[1]
    fh = w1.shape[1]
    dense_at = 3 * share
    fc1_at = dense_at + share
    fc2_at = fc1_at + 2 * fh
    att = attended[...]
    mix = mixes[:, : 2 * RANK].astype(BF16)
    back = backs[:, : 2 * RANK].astype(BF16)
    mix_qkv, mix_fc1 = mix[:, :RANK], mix[:, RANK:]
    back_dense, back_fc2 = back[:, :RANK], back[:, RANK:]
    mix_dense = mm_nt(att, local_maps[:, dense_at:fc1_at])
    grad_local[0, :, dense_at:fc1_at] += mm_tn(back_dense, att)
    grad_full[0, :, d : 2 * d] += mm_tn(mix_dense.astype(BF16), branch[...])
    back_qkv = jnp.zeros(mix_dense.shape, F32)
    for c, part in enumerate((dq, dk, dv)):
        lanes = slice(c * share, (c + 1) * share)
        back_qkv += mm_nt(part[...], local_maps[:, lanes])
        grad_local[0, :, lanes] += mm_tn(mix_qkv, part[...])
    grad_full[0, :, 0:d] += mm_tn(back_qkv.astype(BF16), normed[...])
    mix_fc2, back_fc1 = mlp_half(
        normed,
        branch,
        mix_fc1,
        back_fc2,
        w1,
        w2,
        local_maps[:, fc1_at : fc1_at + fh],
        local_maps[:, fc2_at : fc2_at + fh],
        fc1_bias,
        active,
        hidden_grad,
        (
            grad_local.at[0, :, fc1_at : fc1_at + fh],
            grad_local.at[0, :, fc1_at + fh : fc1_at + 2 * fh],
        ),
    )
    for at in range(0, d, 512):
        lanes = slice(at, at + 512)
        total = mm(att, wd[:, lanes]) + mm(active[...], w2[:, lanes])
        out_sum[:, lanes] = total.astype(BF16)
        total = mm_nt(hidden_grad[...], w1[lanes, :])
        for c, part in enumerate((dq, dk, dv)):
            total += mm_nt(part[...], wq[c, lanes, :])
        grad_sum[:, lanes] = total.astype(BF16)
    carried[:, 0:RANK] = mix_dense
    carried[:, RANK : 2 * RANK] = mix_fc2
    carried[:, 2 * RANK : 3 * RANK] = back_qkv
    carried[:, 3 * RANK : 4 * RANK] = back_fc1


def last_kernel(
    stacked,
    counts,
    resumed,
    meta,
    order,
    normed,
    branch,
    out_part,
    grad_part,
    mixes,
    backs,
    carried,
    local_maps,
    full_maps,
    fc1_bias,
    gain,
    ln_bias,
    *rest,
):
    refs, rest = split_refs(rest, counts)
    if resumed:
        local_before, full_before = rest[9:11]
        rest = rest[11:]
    outs, grads = rest[0:4], rest[4:8]
    row_sums, grad_local, grad_full = rest[8:11]
    w1, w2, active, hidden_grad, sem = rest[11:]

    @pl.when(pl.program_id(0) == 0)
    def _():
        sems = [sem.at[i] for i in range(sem.shape[0])]
        run_copies(mlp_copies(refs[0], refs[1], order, w1, w2, sems))
        if resumed:
            grad_local[...] = local_before[...]
            grad_full[...] = full_before[...]
        else:
            grad_local[...] = jnp.zeros_like(grad_local)
            grad_full[...] = jnp.zeros_like(grad_full)

    member = meta[0]
    d = normed.shape[1]
    fh = w1.shape[1]
    fc1_at = d
    fc2_at = fc1_at + 2 * fh
    mix_fc1 = mixes[:, RANK : 2 * RANK].astype(BF16)
    back_fc2 = backs[:, RANK : 2 * RANK].astype(BF16)
    mix_fc2, back_fc1 = mlp_half(
        normed,
        branch,
        mix_fc1,
        back_fc2,
        w1,
        w2,
        local_maps[:, fc1_at + fh : fc1_at + 2 * fh],
        local_maps[:, fc2_at + fh : fc2_at + 2 * fh],
        fc1_bias,
        active,
        hidden_grad,
        (grad_local.at[:, 0:fh], grad_local.at[:, fh : 2 * fh]),
    )
    mix_fc2 = (mix_fc2 + carried[:, RANK : 2 * RANK]).astype(BF16)
    back_fc1 = (back_fc1 + carried[:, 3 * RANK : 4 * RANK]).astype(BF16)
    grad_full[:, d : 2 * d] += mm_tn(mix_fc2, branch[...])
    grad_full[:, 0:d] += mm_tn(back_fc1, normed[...])
    out_mix = jnp.concatenate([carried[:, 0:RANK].astype(BF16), mix_fc2], 1)
    in_mix = jnp.concatenate([carried[:, 2 * RANK : 3 * RANK].astype(BF16), back_fc1], 1)
    rows = normed.shape[0]
    first = jnp.zeros((rows, 1), F32)
    second = jnp.zeros((rows, 1), F32)
    width = d // 4
    for r in range(4):
        offset = pl.multiple_of((member ^ r) * width, width)
        lanes = pl.ds(offset, width)

        def maps(i, offset=offset):
            return full_maps[:, pl.ds(pl.multiple_of(i * d + offset, width), width)]

        out = out_part[:, lanes].astype(F32) + mm(active[...], w2[:, lanes])
        out += mm(out_mix, jnp.concatenate([maps(2), maps(3)], 0))
        outs[r][...] = out.astype(BF16)
        total = grad_part[:, lanes].astype(F32) + mm_nt(hidden_grad[...], w1[lanes, :])
        total += mm(in_mix, jnp.concatenate([maps(0), maps(1)], 0))
        grads[r][...] = total.astype(BF16)
        first += jnp.sum(total * gain[:, lanes], -1, keepdims=True)
        second += jnp.sum(
            total * (normed[:, lanes].astype(F32) - ln_bias[:, lanes]), -1, keepdims=True
        )
    lane = lax.broadcasted_iota(jnp.int32, (rows, 128), 1)
    row_sums[...] = jnp.transpose(jnp.where(lane == 0, first, second))[0:8, :]


def kept_rows(length, rows):
    slot = pl.program_id(0) * rows + lax.broadcasted_iota(jnp.int32, (rows, 1), 0)
    return (slot < length).astype(F32)


def out_kernel(seq, meta, x, part, first, second, bias, out):
    rows, share = part.shape
    total = part[...].astype(F32) + first[...].astype(F32) + second[...].astype(F32)
    value = x[:, 0].reshape(rows, share).astype(F32) + total + bias[...]
    value = value * kept_rows(meta[1 + seq], rows)
    out[...] = value.astype(BF16).reshape(out.shape)


def grad_kernel(seq, d, meta, x, cot, part, first, second, stats, row_sums, gain, out):
    rows, share = part.shape
    total = part[...].astype(F32) + first[...].astype(F32) + second[...].astype(F32)
    mean, scale = stats[:, 0:1], stats[:, 1:2]
    unit = (x[:, 0].reshape(rows, share).astype(F32) - mean) * scale
    sums = jnp.transpose(
        jnp.concatenate([row_sums[...], jnp.zeros((120, rows), F32)], 0)
    ) * (1.0 / d)
    value = scale * (total * gain[...] - sums[:, 0:1] - unit * sums[:, 1:2])
    value += kept_rows(meta[1 + seq], rows) * cot[:, 0].reshape(rows, share).astype(F32)
    out[...] = value.astype(BF16).reshape(out.shape)


def local(
    tokens,
    cotangent,
    lengths,
    adapter_index,
    ln_gain,
    ln_bias,
    w_qkv,
    qkv_bias,
    w_dense,
    w_fc1,
    fc1_bias,
    w_fc2,
    out_bias,
    qkv_down,
    qkv_up,
    dense_down,
    dense_up,
    fc1_down,
    fc1_up,
    fc2_down,
    fc2_up,
):
    groups = lax.axis_size("dp")
    members = lax.axis_size("mp")
    group = lax.axis_index("dp")
    member = lax.axis_index("mp")
    seqs = tokens.shape[0] // groups
    block, share = tokens.shape[1], tokens.shape[2]
    d = share * members
    ff = w_fc1.shape[1]
    tiles = SLOT // TILE
    per_tile = TILE // block
    count_rows = seqs * SLOT
    permutation, dealt_lengths, dealt_adapters = deal(lengths, adapter_index, groups, seqs)
    my_lengths = lax.dynamic_slice_in_dim(dealt_lengths, group * seqs, seqs)
    my_adapters = lax.dynamic_slice_in_dim(dealt_adapters, group * seqs, seqs)
    meta = jnp.concatenate([member[None].astype(jnp.int32), my_lengths, my_adapters])

    def near(value):
        return lax.ppermute(value, "mp", [(i, i ^ 1) for i in range(members)])

    def far(value):
        return lax.ppermute(value, "mp", [(i, i ^ 2) for i in range(members)])

    def hop(value):
        return near(value[0:8])

    def dealt(values):
        return move_rows(gather_rows_kernel, permutation, (values,), "gather_rows")

    def entered(values):
        return lax.all_to_all(values, "dp", split_axis=0, concat_axis=0, tiled=True)

    def widened(mine, across):
        shape = (groups, seqs, block, share)
        return tuple(a.reshape(shape) for a in (mine, near(mine), across, near(across)))

    dealt_tokens = dealt(tokens)
    my_tokens = entered(dealt_tokens)
    far_tokens = far(my_tokens)

    wide = (d // groups) % 128 == 0
    inner = 2
    outer = groups // inner
    place_out, place_in = group // inner, group % inner

    def gathered(weight, axis):
        if wide:
            return (lax.all_gather(weight, "dp", axis=0, tiled=False),)
        return (lax.all_gather(weight, "dp", axis=axis, tiled=True)[None],)

    def beside(value):
        return lax.ppermute(value, "dp", [(i, i ^ 1) for i in range(groups)])

    def onward(value):
        return lax.ppermute(value, "dp", [(i, (i + inner) % groups) for i in range(groups)])

    def ring(weight, axis, *waits):
        if not wide:
            return gathered(weight, axis), ()
        held = [weight]
        crossed = []
        for k in range(outer - 1):
            step = after(held[k], *waits, *crossed[-1:])
            crossed.append(beside(held[k]))
            held.append(onward(step))
            waits = ()
        done = tuple(held) + tuple(crossed)
        crossed.append(beside(held[-1]))
        return tuple(a for pair in zip(held, crossed, strict=True) for a in pair), done

    order = jnp.stack(
        [
            (place_out - k) % outer * inner + (place_in + j) % inner
            for k in range(outer)
            for j in range(inner)
        ]
    ).astype(jnp.int32)
    all_qkv, ring_early = ring(w_qkv, 1, my_tokens)
    rows_in = widened(my_tokens, after(far_tokens, *ring_early))
    cos, up, down = rotary_tables()
    gain_row = ln_gain[None, :]
    bias_row = ln_bias[None, :]

    piece = pl.BlockSpec((per_tile, 1, block, share), lambda s, t, *_: (t, s, 0, 0))
    wide_row = pl.BlockSpec((TILE, d), lambda s, t, *_: (s * tiles + t, 0))
    share_row = pl.BlockSpec((TILE, share), lambda s, t, *_: (s * tiles + t, 0))
    stat_row = pl.BlockSpec((TILE, 128), lambda s, t, *_: (s * tiles + t, 0))
    table_row = pl.BlockSpec((TILE, 128), lambda s, t, *_: (t, 0))
    cols = 4 * share + 2 * ff
    local_map = pl.BlockSpec((RANK, cols), lambda s, t, meta, *_: (meta[1 + seqs + s], 0))
    full_map = pl.BlockSpec((RANK, 4 * d), lambda s, t, *_: (s, 0))

    def whole(shape):
        return pl.BlockSpec(shape, lambda s, t, *_: tuple(0 for _ in shape))

    def shaped(*shape, dtype=BF16):
        return jax.ShapeDtypeStruct(shape, dtype)

    def cost(flops, nbytes, exps=0):
        return pl.CostEstimate(
            flops=int(flops * COST), transcendentals=int(exps * COST), bytes_accessed=int(nbytes * COST)
        )

    limit = pltpu.CompilerParams(vmem_limit_bytes=58 * 1024 * 1024)

    normed, stats = pl.pallas_call(
        norm_kernel,
        out_shape=(shaped(count_rows, d), shaped(count_rows, 128, dtype=F32)),
        grid_spec=pltpu.PrefetchScalarGridSpec(
            num_scalar_prefetch=1,
            grid=(seqs, tiles),
            in_specs=[piece] * 4 + [whole((1, d))] * 2,
            out_specs=[wide_row, stat_row],
            scratch_shapes=[pltpu.VMEM((TILE, d), F32)],
        ),
        compiler_params=limit,
        cost_estimate=cost(10 * count_rows * d, 4 * count_rows * d),
        name="norm_rows",
    )(meta, *rows_in, gain_row, bias_row)

    my_cotangent = entered(after(dealt(cotangent), *ring_early, *rows_in))
    fh = ff // 2
    local_part = jnp.concatenate(
        [qkv_up[0], qkv_up[1], qkv_up[2], dense_down, fc1_up, fc2_down], 1
    ).astype(BF16)
    cols = local_part.shape[1]
    full_rows = qkv_down.shape[0]
    full_part = jnp.stack([qkv_down, fc1_down, dense_up, fc2_up], 1).astype(BF16)
    full_part = after(full_part, dealt_tokens)
    full_part = jnp.transpose(full_part.reshape(full_rows, 4, members, share), (2, 0, 1, 3))
    full_part = lax.all_to_all(
        full_part.reshape(members, full_rows, 4 * share),
        "mp",
        split_axis=0,
        concat_axis=0,
        tiled=True,
    )
    all_part = jnp.concatenate(
        [local_part, full_part.reshape(members * full_rows, 4 * share)], 1
    )
    all_part = after(all_part, my_tokens)
    local_maps = lax.all_gather(all_part, "dp", axis=0, tiled=True)
    my_maps = jnp.stack(
        [
            lax.dynamic_slice(
                local_maps, (my_adapters[s] * RANK, cols), (RANK, 4 * share)
            )
            for s in range(seqs)
        ]
    ).reshape(seqs * RANK, 4, share)
    full_maps = jnp.transpose(lax.all_gather(my_maps, "mp", axis=0, tiled=False), (1, 2, 0, 3))
    full_maps = full_maps.reshape(seqs * RANK, 4 * d)
    all_dense = gathered(after(w_dense, local_maps), 1)
    w_fc1, w_fc2 = after(w_fc1, my_cotangent), after(w_fc2, my_cotangent)
    my_cotangent = after(my_cotangent, full_maps, *all_qkv)
    far_cotangent = far(my_cotangent)

    def mlp_weights(j):
        first, second = w_fc1[:, j * fh : (j + 1) * fh], w_fc2[j * fh : (j + 1) * fh, :]
        if not wide:
            return gathered(first, 0), gathered(second, 1)
        width = second.shape[1]
        parts = [second[i : i + width] for i in range(0, fh, width)]
        packed = jnp.concatenate([first, jnp.concatenate(parts, 1)], 0)
        return (lax.all_gather(packed, "dp", axis=0, tiled=False),), ()

    halves_fc = [mlp_weights(j) for j in range(2)]
    slots = groups
    dense_at = 3 * share

    queries, keys, values, mixes = pl.pallas_call(
        functools.partial(qkv_kernel, len(all_qkv) == 1, len(all_qkv)),
        out_shape=(
            shaped(count_rows, share),
            shaped(count_rows, share),
            shaped(count_rows, share),
            shaped(count_rows, 128, dtype=F32),
        ),
        grid_spec=pltpu.PrefetchScalarGridSpec(
            num_scalar_prefetch=2,
            grid=(seqs, tiles),
            in_specs=[wide_row, local_map, full_map, whole((3, share))]
            + [table_row] * 3
            + [ANY] * len(all_qkv),
            out_specs=[share_row, share_row, share_row, stat_row],
            scratch_shapes=[
                pltpu.VMEM((3, d, share), BF16),
                pltpu.SemaphoreType.DMA((slots,)),
            ],
        ),
        compiler_params=limit,
        cost_estimate=cost(6 * count_rows * d * share, 16 * 2**20),
        name="project_rows",
    )(meta, order, normed, local_maps, full_maps, qkv_bias.astype(F32), cos, up, down, *all_qkv)

    projected = hop(mixes)
    grads_in = widened(my_cotangent, after(far_cotangent, projected))
    branch, attn_grad, backs = pl.pallas_call(
        functools.partial(branch_kernel, len(all_dense) == 1, len(all_dense), dense_at),
        out_shape=(
            shaped(count_rows, d),
            shaped(count_rows, share),
            shaped(count_rows, 128, dtype=F32),
        ),
        grid_spec=pltpu.PrefetchScalarGridSpec(
            num_scalar_prefetch=2,
            grid=(seqs, tiles),
            in_specs=[piece] * 4 + [local_map, full_map] + [ANY] * (1 + len(all_dense)),
            out_specs=[wide_row, share_row, stat_row],
            scratch_shapes=[
                pltpu.VMEM((TILE, d), BF16),
                pltpu.VMEM((share, d), BF16),
                pltpu.SemaphoreType.DMA((slots,)),
            ],
        ),
        compiler_params=limit,
        cost_estimate=cost(2 * count_rows * d * share, 20 * 2**20),
        name="branch_rows",
    )(meta, order, *grads_in, local_maps, full_maps, projected, *all_dense)

    pair = pl.BlockSpec((SLOT, 128), lambda s, h, *_: (s, h))
    attended, dq, dk, dv = pl.pallas_call(
        attention_kernel,
        out_shape=(shaped(count_rows, share),) * 4,
        grid_spec=pltpu.PrefetchScalarGridSpec(
            num_scalar_prefetch=1,
            grid=(seqs, share // 128),
            in_specs=[pair] * 4 + [whole((SLOT, 128))] * 3,
            out_specs=[pair] * 4,
            scratch_shapes=[
                pltpu.VMEM((SLOT, 128), F32),
                pltpu.VMEM((SLOT, 128), F32),
                pltpu.VMEM((SLOT, 128), F32),
            ],
        ),
        compiler_params=limit,
        cost_estimate=cost(
            6 * 4 * count_rows * SLOT * share, 16 * 2**20, count_rows * SLOT * share // HD
        ),
        name="attend_rows",
    )(meta, queries, keys, values, attn_grad, cos, up, down)

    big = BIG
    big_tiles = SLOT // big

    def big_row(width):
        return pl.BlockSpec((big, width), lambda s, t, *_: (s * big_tiles + t, 0))

    def per_seq(*shape):
        return pl.BlockSpec((1,) + shape, lambda s, t, *_: (s,) + tuple(0 for _ in shape))

    first_weights = (all_qkv, all_dense) + halves_fc[0]
    counts = tuple(len(w) for w in first_weights)
    first_cols = 4 * share + 2 * fh
    bias_all = fc1_bias.astype(F32)[None, :]
    out_part, grad_part, carried, local_first, full_first = pl.pallas_call(
        functools.partial(first_kernel, tuple(c == 1 for c in counts), counts),
        out_shape=(
            shaped(count_rows, d),
            shaped(count_rows, d),
            shaped(count_rows, 128, dtype=F32),
            shaped(seqs, RANK, first_cols, dtype=F32),
            shaped(seqs, RANK, 2 * d, dtype=F32),
        ),
        grid_spec=pltpu.PrefetchScalarGridSpec(
            num_scalar_prefetch=2,
            grid=(seqs, big_tiles),
            in_specs=[big_row(d)] * 2
            + [big_row(share)] * 4
            + [big_row(128)] * 2
            + [local_map, full_map, whole((1, fh))]
            + [ANY] * sum(counts),
            out_specs=[
                big_row(d),
                big_row(d),
                big_row(128),
                per_seq(RANK, first_cols),
                per_seq(RANK, 2 * d),
            ],
            scratch_shapes=[
                pltpu.VMEM((3, d, share), BF16),
                pltpu.VMEM((share, d), BF16),
                pltpu.VMEM((d, fh), BF16),
                pltpu.VMEM((fh, d), BF16),
                pltpu.VMEM((big, fh), BF16),
                pltpu.VMEM((big, fh), BF16),
                pltpu.SemaphoreType.DMA((3 + fh // (d // slots), slots)),
            ],
        ),
        compiler_params=limit,
        cost_estimate=cost(
            8 * count_rows * d * fh + 8 * count_rows * d * share, 80 * 2**20, count_rows * fh
        ),
        name="first_half",
    )(
        meta,
        order,
        normed,
        branch,
        attended,
        dq,
        dk,
        dv,
        mixes,
        backs,
        local_maps,
        full_maps,
        bias_all[:, :fh],
        *[a for w in first_weights for a in w],
    )

    def add_low(left, right):
        return (left.astype(F32) + right.astype(F32)).astype(BF16)

    def half_reduced(parts):
        return add_low(parts[2], near(parts[3]))

    def reduced(parts, half):
        return parts[0], near(parts[1]), far(half)

    adapters = qkv_down.shape[0] * groups * members // RANK
    owned = adapters * RANK // groups

    blocks = RANK // owned
    each = owned // members

    def spread_sums(local_grad, full_grad):
        width = full_grad.shape[2]
        rows = full_grad.astype(BF16).reshape(seqs, blocks, members, each, width)
        rows = jnp.transpose(rows, (2, 0, 1, 3, 4)).reshape(members, seqs * blocks * each, width)
        traded = lax.all_to_all(rows, "mp", split_axis=0, concat_axis=0, tiled=True)
        mine = jnp.sum(traded.astype(F32), 0).reshape(seqs, blocks * each * members, width // members)
        update = jnp.concatenate([local_grad, mine], 2)
        spread = jnp.zeros((adapters,) + update.shape[1:], F32)
        for s in range(seqs):
            here = jnp.arange(adapters, dtype=jnp.int32) == my_adapters[s]
            spread = spread + jnp.where(here[:, None, None], update[s][None], 0.0)
        return spread.astype(BF16).reshape(groups, owned, update.shape[2])

    def owned_sums(arrived, width):
        summed = jnp.sum(arrived.astype(F32), 0)
        mine = summed[:, width:].reshape(each, -1, d)
        return summed, jnp.transpose(mine, (1, 0, 2))

    sent_first = spread_sums(local_first, full_first)
    arrived_first = entered(sent_first)
    last_weights = halves_fc[1]
    counts = tuple(len(w) for w in last_weights)
    my_gain = lax.dynamic_slice_in_dim(gain_row, member * share, share, 1)
    def last_call(seq, first_tile, count, token, given):
        def rows_of(width):
            return pl.BlockSpec((big, width), lambda t, *_: (seq * big_tiles + first_tile + t, 0))

        def fixed(shape, first=0):
            return pl.BlockSpec(shape, lambda t, *_: (first,) + (0,) * (len(shape) - 1))

        def own(width):
            return pl.BlockSpec((big, width), lambda t, *_: (first_tile + t, 0))

        sum_block = pl.BlockSpec((8, big), lambda t, *_: (0, first_tile + t))
        own_map = pl.BlockSpec((RANK, cols), lambda t, meta, *_: (meta[1 + seqs + seq], 0))
        operands = (
            token,
            order,
            normed,
            branch,
            out_part,
            grad_part,
            mixes,
            backs,
            carried,
            local_maps,
            full_maps,
            bias_all[:, fh:],
            gain_row,
            bias_row,
            *[a for w in last_weights for a in w],
        )
        given = tuple(given)
        return pl.pallas_call(
            functools.partial(
                last_kernel, tuple(c == 1 for c in counts), counts, len(given) > 0
            ),
            out_shape=(shaped(SLOT, share),) * 8
            + (
                shaped(8, SLOT, dtype=F32),
                shaped(RANK, 2 * fh, dtype=F32),
                shaped(RANK, 2 * d, dtype=F32),
            ),
            grid_spec=pltpu.PrefetchScalarGridSpec(
                num_scalar_prefetch=2,
                grid=(count,),
                in_specs=[rows_of(d)] * 4
                + [rows_of(128)] * 3
                + [own_map, fixed((RANK, 4 * d), seq)]
                + [fixed((1, fh)), fixed((1, d)), fixed((1, d))]
                + [ANY] * (sum(counts) + 9 * (len(given) > 0))
                + [fixed((RANK, 2 * fh)), fixed((RANK, 2 * d))] * (len(given) > 0),
                out_specs=[own(share)] * 8
                + [sum_block, fixed((RANK, 2 * fh)), fixed((RANK, 2 * d))],
                scratch_shapes=[
                    pltpu.VMEM((d, fh), BF16),
                    pltpu.VMEM((fh, d), BF16),
                    pltpu.VMEM((big, fh), BF16),
                    pltpu.VMEM((big, fh), BF16),
                    pltpu.SemaphoreType.DMA((1 + fh // (d // slots), slots)),
                ],
            ),
            input_output_aliases={len(operands) + i: i for i in range(len(given))},
            compiler_params=limit,
            cost_estimate=cost(
                8 * count * big * d * fh, 10 * count * 2**20, count * big * fh
            ),
            name="last_half",
        )(*operands, *given)

    def out_call(seq, parts):
        return pl.pallas_call(
            functools.partial(out_kernel, seq),
            out_shape=shaped(groups, block, share),
            grid_spec=pltpu.PrefetchScalarGridSpec(
                num_scalar_prefetch=1,
                grid=(tiles,),
                in_specs=[piece_of(seq)] + [own_row] * 3 + [row_block],
                out_specs=back_block,
            ),
            compiler_params=limit,
            cost_estimate=cost(6 * SLOT * share, 10 * SLOT * share),
            name="output_rows",
        )(meta, rows_in[0], *parts, out_bias.astype(F32)[None, :])

    def grad_call(seq, parts, totals):
        return pl.pallas_call(
            functools.partial(grad_kernel, seq, d),
            out_shape=shaped(groups, block, share),
            grid_spec=pltpu.PrefetchScalarGridSpec(
                num_scalar_prefetch=1,
                grid=(tiles,),
                in_specs=[piece_of(seq)] * 2
                + [own_row] * 3
                + [
                    pl.BlockSpec((TILE, 128), lambda t, *_: (seq * tiles + t, 0)),
                    pl.BlockSpec((8, TILE), lambda t, *_: (0, t)),
                    row_block,
                ],
                out_specs=back_block,
            ),
            compiler_params=limit,
            cost_estimate=cost(10 * SLOT * share, 12 * SLOT * share),
            name="input_grad_rows",
        )(meta, rows_in[0], grads_in[0], *parts, stats, totals, my_gain)

    def piece_of(seq):
        return pl.BlockSpec((per_tile, 1, block, share), lambda t, *_: (t, seq, 0, 0))

    own_row = pl.BlockSpec((TILE, share), lambda t, *_: (t, 0))
    row_block = pl.BlockSpec((1, share), lambda t, *_: (0, 0))
    back_block = pl.BlockSpec((per_tile, block, share), lambda t, *_: (t, 0, 0))

    def near_sums(results, *waits):
        parts = [after(results[r], *waits) if r in (2, 6) else results[r] for r in range(8)]
        half_sums = results[8] + near(results[8])
        return parts, half_reduced(parts[0:4]), half_reduced(parts[4:8]), half_sums

    def far_sums(parts, half_out, half_grad, half_sums):
        return (
            reduced(parts[0:4], half_out),
            reduced(parts[4:8], half_grad),
            half_sums + far(half_sums),
        )

    back_outs = []
    back_grads = []
    local_last = []
    full_last = []
    waits = (arrived_first,)
    token = after(meta, sent_first)
    for seq in range(seqs):
        if seq == 0:
            results = last_call(seq, 0, big_tiles, token, ())
        else:
            results = last_call(seq, 0, big_tiles // 2, token, ())
            out_rows = out_call(seq - 1, after(out_parts, results[9]))
            results = last_call(
                seq, big_tiles // 2, big_tiles // 2, after(meta, out_rows), results
            )
            back_outs.append(entered(after(out_rows, *back_grads)))
        local_last.append(results[9])
        full_last.append(results[10])
        halves = near_sums(results, *waits)
        if seq > 0:
            grad_rows = grad_call(seq - 1, after(grad_parts, results[9]), row_totals)
            back_grads.append(entered(after(grad_rows, back_outs[-1])))
        out_parts, grad_parts, row_totals = far_sums(*halves)
        token = after(meta, *halves[1:])
        waits = (out_parts[2], grad_parts[2])
    sent_last = spread_sums(jnp.stack(local_last), after(jnp.stack(full_last), *halves[1:]))
    out_rows = out_call(seqs - 1, out_parts)
    back_outs.append(entered(after(out_rows, *back_grads)))
    grad_rows = grad_call(seqs - 1, grad_parts, row_totals)
    arrived_last = entered(after(sent_last, grad_rows, back_outs[-1]))
    back_grads.append(entered(after(grad_rows, arrived_last)))
    output = move_rows(scatter_rows_kernel, permutation, back_outs, "scatter_rows")
    input_grad = move_rows(scatter_rows_kernel, permutation, back_grads, "scatter_rows")

    first_sums, first_full = owned_sums(arrived_first, first_cols)
    last_sums, last_full = owned_sums(arrived_last, 2 * fh)
    fc1_at = 4 * share
    return (
        output,
        input_grad,
        first_full[0],
        jnp.stack([first_sums[:, c * share : (c + 1) * share] for c in range(3)], 0),
        first_sums[:, dense_at:fc1_at],
        first_full[1],
        last_full[0],
        jnp.concatenate([first_sums[:, fc1_at : fc1_at + fh], last_sums[:, 0:fh]], 1),
        jnp.concatenate(
            [first_sums[:, fc1_at + fh : fc1_at + 2 * fh], last_sums[:, fh : 2 * fh]], 1
        ),
        last_full[1],
    )


def solution(mesh):
    return jax.shard_map(
        local,
        mesh=mesh,
        in_specs=(
            P(None, "dp", "mp"),
            P(None, "dp", "mp"),
            P(),
            P(),
            P(),
            P(),
            P(None, "dp", "mp"),
            P(None, "mp"),
            P("mp", "dp"),
            P("dp", "mp"),
            P("mp"),
            P("mp", "dp"),
            P("mp"),
            P(("dp", "mp"), None),
            P(None, "dp", "mp"),
            P("dp", "mp"),
            P(("dp", "mp"), None),
            P(("dp", "mp"), None),
            P("dp", "mp"),
            P("dp", "mp"),
            P(("dp", "mp"), None),
        ),
        out_specs=(
            P(None, "dp", "mp"),
            P(None, "dp", "mp"),
            P(("dp", "mp"), None),
            P(None, "dp", "mp"),
            P("dp", "mp"),
            P(("dp", "mp"), None),
            P(("dp", "mp"), None),
            P("dp", "mp"),
            P("dp", "mp"),
            P(("dp", "mp"), None),
        ),
        check_vma=False,
    )
```

```python
import functools

import jax
import jax.numpy as jnp
import numpy as np
from jax import lax
from jax.experimental import pallas as pl
from jax.experimental.pallas import tpu as pltpu
from jax.sharding import PartitionSpec as P

HD = 64
ROT = 32
RANK = 16
SLOT = 1024
EPSILON = 1e-05
MASKED = -1e30
BF16 = jnp.bfloat16
F32 = jnp.float32
ANY = pl.BlockSpec(memory_space=pl.ANY)
TILE = 256
BIG = 256
FIRST = 5
COST = 1.0


def after(value, *others):
    return lax.optimization_barrier((value,) + others)[0] if others else value


def mm(left, right):
    return jnp.dot(left, right, preferred_element_type=F32)


def mm_nt(left, right):
    return lax.dot_general(left, right, (((1,), (1,)), ((), ())), preferred_element_type=F32)


def mm_tn(left, right):
    return lax.dot_general(left, right, (((0,), (0,)), ((), ())), preferred_element_type=F32)


def rotary_tables():
    half = ROT // 2
    places = np.arange(SLOT, dtype=np.float32)
    frequency = np.float32(1.0) / np.float32(10000.0) ** (
        np.arange(half, dtype=np.float32) * np.float32(2.0) / np.float32(ROT)
    )
    phases = (places[:, None] * frequency[None, :]).astype(np.float32)
    cosine, sine = np.cos(phases), np.sin(phases)
    zero = np.zeros_like(sine)
    rest = np.zeros((SLOT, HD - ROT), np.float32)
    cos_head = np.concatenate([cosine, cosine, rest + 1.0], 1)
    up_head = np.concatenate([-sine, zero, rest], 1)
    down_head = np.concatenate([zero, sine, rest], 1)
    return tuple(
        jnp.asarray(np.concatenate([t, t], 1), F32) for t in (cos_head, up_head, down_head)
    )


def rotate(value, cos, up, down):
    return (
        value * cos
        + pltpu.roll(value, 128 - ROT // 2, axis=1) * up
        + pltpu.roll(value, ROT // 2, axis=1) * down
    )


def deal(lengths, adapter_index, groups, local_seqs):
    count = lengths.shape[0]
    pos = jnp.arange(count, dtype=jnp.int32)
    ranking = lengths * count + pos
    rank = jnp.sum((ranking[None, :] > ranking[:, None]).astype(jnp.int32), 1)
    round_num = rank // groups
    within = rank % groups
    target = jnp.where(round_num % 2 == 0, within, groups - 1 - within)
    place = target * local_seqs + round_num
    chosen = (place[None, :] == pos[:, None]).astype(jnp.int32)

    def pick(values):
        return jnp.sum(chosen * values[None, :], 1).astype(jnp.int32)

    return pick(pos), pick(lengths), pick(adapter_index)


def gather_rows_kernel(order, source, target, held, sem_in, sem_out):
    count = source.shape[0]
    fetch = [
        pltpu.make_async_copy(source.at[order[i]], held.at[i], sem_in.at[i]) for i in range(count)
    ]
    store = [pltpu.make_async_copy(held.at[i], target.at[i], sem_out.at[i]) for i in range(count)]
    for copy in fetch:
        copy.start()
    for i in range(count):
        fetch[i].wait()
        store[i].start()
    for copy in store:
        copy.wait()


def scatter_rows_kernel(order, *refs):
    seqs = len(refs) - 4
    sources, (target, held, sem_in, sem_out) = refs[:seqs], refs[seqs:]
    groups = sources[0].shape[0]
    fetch = []
    store = []
    for g in range(groups):
        for s in range(seqs):
            i = g * seqs + s
            fetch.append(pltpu.make_async_copy(sources[s].at[g], held.at[i], sem_in.at[i]))
            store.append(pltpu.make_async_copy(held.at[i], target.at[order[i]], sem_out.at[i]))
    for copy in fetch:
        copy.start()
    for take, put in zip(fetch, store, strict=True):
        take.wait()
        put.start()
    for copy in store:
        copy.wait()


def move_rows(kernel, order, arrays, name):
    count = sum(a.shape[0] for a in arrays)
    rest = arrays[0].shape[1:]
    size = sum(a.size for a in arrays)
    return pl.pallas_call(
        kernel,
        out_shape=jax.ShapeDtypeStruct((count,) + rest, BF16),
        grid_spec=pltpu.PrefetchScalarGridSpec(
            num_scalar_prefetch=1,
            grid=(1,),
            in_specs=[ANY] * len(arrays),
            out_specs=ANY,
            scratch_shapes=[
                pltpu.VMEM((count,) + rest, BF16),
                pltpu.SemaphoreType.DMA((count,)),
                pltpu.SemaphoreType.DMA((count,)),
            ],
        ),
        compiler_params=pltpu.CompilerParams(vmem_limit_bytes=16 * 1024 * 1024),
        cost_estimate=pl.CostEstimate(flops=0, transcendentals=0, bytes_accessed=int(4 * size * COST)),
        name=name,
    )(order, *arrays)


def weight_copies(kind, refs, order, target, sem, stacked):
    count = refs[0].shape[0] if stacked else len(refs)
    rows = target.shape[1 if kind in ("q", "lane") else 0]
    width = rows // count
    copies = []
    for s in range(count):
        source = refs[0].at[s] if stacked else refs[s]
        offset = s * width if stacked else pl.multiple_of(order[s] * width, width)
        if kind == "q":
            place = target.at[:, pl.ds(offset, width), :]
        elif kind == "row":
            place = target.at[pl.ds(offset, width), :]
        else:
            place = target.at[:, pl.ds(offset, width)]
        copies.append(pltpu.make_async_copy(source, place, sem.at[s]))
    return copies


def ring_copies(refs, order, sems, wq, wd):
    copies = []
    if len(refs[0].shape) > 2:
        for i, target in ((0, wq), (3, wd)):
            if target is not None:
                source = refs[min(i, 1)].at[0]
                copies.append(pltpu.make_async_copy(source, target, sems.at[i, 0]))
        return copies
    width = refs[0].shape[0] // 4
    for s, ref in enumerate(refs):
        place = pl.ds(pl.multiple_of(order[s] * width, width), width)
        for c in range(3):
            if wq is not None:
                source = ref.at[c * width : (c + 1) * width, :]
                copies.append(
                    pltpu.make_async_copy(source, wq.at[c, place, :], sems.at[c, s])
                )
        for i in range(ref.shape[1] // width):
            if wd is not None:
                lanes = slice(i * width, (i + 1) * width)
                source = ref.at[3 * width : 4 * width, lanes]
                copies.append(
                    pltpu.make_async_copy(source, wd.at[lanes, place], sems.at[3 + i, s])
                )
    return copies


def mlp_copies(first, second, order, w1, w2, sems):
    if second:
        copies = weight_copies("row", first, order, w1, sems[0], True)
        return copies + weight_copies("lane", second, order, w2, sems[1], True)
    packed = first[0]
    count = packed.shape[0]
    width = w1.shape[0] // count
    copies = []
    for s in range(count):
        lanes = pl.ds(s * width, width)
        copies.append(
            pltpu.make_async_copy(packed.at[s, 0:width, :], w1.at[lanes, :], sems[0].at[s])
        )
        for i in range(0, w2.shape[0], width):
            copies.append(
                pltpu.make_async_copy(
                    packed.at[s, width : 2 * width, i : i + width],
                    w2.at[i : i + width, lanes],
                    sems[1 + i // width].at[s],
                )
            )
    return copies


def first_step():
    return (pl.program_id(0) == 0) & (pl.program_id(1) == 0)


def norm_kernel(meta, a0, a1, a2, a3, gain, bias, normed, stats, row):
    member = meta[0]
    share = a0.shape[-1]
    for r, ref in enumerate((a0, a1, a2, a3)):
        offset = pl.multiple_of((member ^ r) * share, share)
        row[:, pl.ds(offset, share)] = ref[:, 0].reshape(row.shape[0], share).astype(F32)
    value = row[...]
    mean = jnp.mean(value, -1, keepdims=True)
    centred = value - mean
    scale = lax.rsqrt(jnp.mean(centred * centred, -1, keepdims=True) + EPSILON)
    normed[...] = (centred * scale * gain[...] + bias[...]).astype(BF16)
    lane = lax.broadcasted_iota(jnp.int32, stats.shape, 1)
    stats[...] = jnp.where(lane == 0, mean, scale)


def qkv_kernel(
    count, meta, order, normed, local_maps, full_maps, bias, cos, up, down, *rest
):
    weights, rest = rest[:count], rest[count:]
    queries, keys, values, mixes, w, sem = rest

    @pl.when(first_step())
    def _():
        run_copies(ring_copies(weights, order, sem, w, None))

    x = normed[...]
    d = x.shape[1]
    share = queries.shape[1]
    maps = jnp.concatenate([full_maps[:, 0:d], full_maps[:, d : 2 * d]], 0)
    mix = mm_nt(x, maps)
    mixes[:, : 2 * RANK] = mix
    mix_low = mix[:, :RANK].astype(BF16)
    for c, out in enumerate((queries, keys, values)):
        value = mm(x, w[c]) + bias[c : c + 1, :] + mm(
            mix_low, local_maps[:, c * share : (c + 1) * share]
        )
        if c == 2:
            out[...] = value.astype(BF16)
        else:
            for j in range(share // 128):
                part = value[:, j * 128 : (j + 1) * 128]
                out[:, j * 128 : (j + 1) * 128] = rotate(
                    part, cos[...], up[...], down[...]
                ).astype(BF16)


def branch_kernel(
    count, places, meta, order, a0, a1, a2, a3, local_maps, full_maps, token, *rest
):
    weights, rest = rest[:count], rest[count:]
    branch, attn_grad, backs, row, w, sem = rest

    @pl.when(first_step())
    def _():
        run_copies(ring_copies(weights, order, sem, None, w))

    member = meta[0]
    length = meta[1 + pl.program_id(0)]
    share = a0.shape[-1]
    d = row.shape[1]
    dense_at = places
    for r, ref in enumerate((a0, a1, a2, a3)):
        offset = pl.multiple_of((member ^ r) * share, share)
        row[:, pl.ds(offset, share)] = ref[:, 0].reshape(row.shape[0], share)
    slot = pl.program_id(1) * row.shape[0] + lax.broadcasted_iota(jnp.int32, (row.shape[0], 1), 0)
    keep = (slot < length).astype(F32)
    value = (row[...].astype(F32) * keep).astype(BF16)
    branch[...] = value
    maps = jnp.concatenate([full_maps[:, 2 * d : 3 * d], full_maps[:, 3 * d : 4 * d]], 0)
    back = mm_nt(value, maps)
    backs[:, : 2 * RANK] = back
    attn_grad[...] = (
        mm_nt(value, w[...])
        + mm(back[:, :RANK].astype(BF16), local_maps[:, dense_at : dense_at + share])
    ).astype(BF16)


def attention_kernel(
    meta,
    queries,
    keys,
    values,
    out_grad,
    cos,
    up,
    down,
    attended,
    dq,
    dk,
    dv,
    dk_sum,
    dv_sum,
    outside,
):
    length = meta[1 + pl.program_id(0)]
    rows = 512
    heads = 128 // HD

    @pl.when(pl.program_id(1) == 0)
    def _():
        place = lax.broadcasted_iota(jnp.int32, outside.shape, 0)
        outside[...] = jnp.where(place < length, 0.0, MASKED)

    zero = jnp.zeros((), BF16)
    head_of = lax.broadcasted_iota(jnp.int32, (SLOT, 128), 1) // HD
    own_keys = [jnp.where(head_of == h, keys[...], zero) for h in range(heads)]
    own_values = [jnp.where(head_of == h, values[...], zero) for h in range(heads)]
    below = lax.broadcasted_iota(jnp.int32, (rows, rows), 0) <= lax.broadcasted_iota(
        jnp.int32, (rows, rows), 1
    )
    dk_sum[...] = jnp.zeros_like(dk_sum)
    dv_sum[...] = jnp.zeros_like(dv_sum)
    for at in range(0, SLOT, rows):
        n = at + rows
        all_q = queries[at:n, :] * jnp.asarray(0.125, BF16)
        all_g = out_grad[at:n, :]
        out = jnp.zeros((128, rows), F32)
        dq_sum = jnp.zeros((128, rows), F32)
        for h in range(heads):
            q = jnp.where(head_of[:rows] == h, all_q, zero)
            g = jnp.where(head_of[:rows] == h, all_g, zero)
            score = mm_nt(keys[0:n, :], q)
            score = score + jnp.concatenate([outside[0:n, :]] * (rows // 128), 1)
            corner = jnp.where(below, score[at:n], MASKED)
            score = jnp.concatenate([score[0:at], corner], 0) if at else corner
            weight = jnp.exp(score - jnp.max(score, 0, keepdims=True))
            probs = weight * (1.0 / jnp.sum(weight, 0, keepdims=True))
            low = probs.astype(BF16)
            prob_grad = mm_nt(values[0:n, :], g)
            inner = jnp.sum(probs * prob_grad, 0, keepdims=True)
            score_grad = (probs * (prob_grad - inner)).astype(BF16)
            out += mm_tn(own_values[h][0:n], low)
            dq_sum += mm_tn(own_keys[h][0:n], score_grad)
            dk_sum[0:n, :] += mm(score_grad, q)
            dv_sum[0:n, :] += mm(low, g)
        attended[at:n, :] = jnp.transpose(out).astype(BF16)
        dq[at:n, :] = rotate(
            jnp.transpose(dq_sum) * 0.125, cos[at:n, :], -up[at:n, :], -down[at:n, :]
        ).astype(BF16)
    dk[...] = rotate(dk_sum[...], cos[...], -up[...], -down[...]).astype(BF16)
    dv[...] = dv_sum[...].astype(BF16)


def mlp_half(
    x, b, mix_fc1, back_fc2, w1, w2, up_maps, down_maps, fc1_bias, active, hidden_grad, grads
):
    step = 512
    for at in range(0, w1.shape[1], step):
        lanes = slice(at, min(at + step, w1.shape[1]))
        v = mm(x[...], w1[:, lanes]) + fc1_bias[:, lanes] + mm(mix_fc1, up_maps[:, lanes])
        square = v * v
        t = jnp.tanh(0.7978845608028654 * (v + 0.044715 * v * square))
        half = 0.5 * (1.0 + t)
        slope = half + (0.5 * 0.7978845608028654) * v * (1.0 - t * t) * (
            1.0 + (3.0 * 0.044715) * square
        )
        active[:, lanes] = (v * half).astype(BF16)
        pull = mm_nt(b[...], w2[lanes, :]) + mm(back_fc2, down_maps[:, lanes])
        hidden_grad[:, lanes] = (pull * slope).astype(BF16)
    grads[0][...] += mm_tn(mix_fc1, hidden_grad[...])
    grads[1][...] += mm_tn(back_fc2, active[...])
    return mm_nt(active[...], down_maps), mm_nt(hidden_grad[...], up_maps)


def run_copies(copies):
    for c in copies:
        c.start()
    for c in copies:
        c.wait()


def split_refs(rest, counts):
    refs = []
    for count in counts:
        refs.append(rest[:count])
        rest = rest[count:]
    return refs, rest


def first_kernel(
    ff,
    counts,
    meta,
    order,
    normed,
    branch,
    attended,
    dq,
    dk,
    dv,
    mixes,
    backs,
    local_maps,
    full_maps,
    fc1_bias,
    *rest,
):
    refs, rest = split_refs(rest, counts)
    out_sum, grad_sum, carried, grad_local, grad_full = rest[0:5]
    wq, wd, w1, w2, active, hidden_grad, sem, fc_sem = rest[5:]

    @pl.when(first_step())
    def _():
        copies = ring_copies(refs[0], order, sem, wq, wd)
        sems = [fc_sem.at[i] for i in range(fc_sem.shape[0])]
        run_copies(copies + mlp_copies(refs[1], refs[2], order, w1, w2, sems))

    @pl.when(pl.program_id(1) == 0)
    def _():
        grad_local[...] = jnp.zeros_like(grad_local)
        grad_full[...] = jnp.zeros_like(grad_full)

    d = normed.shape[1]
    share = attended.shape[1]
    fh = w1.shape[1]
    dense_at = 3 * share
    fc1_at = dense_at + share
    fc2_at = fc1_at + ff
    att = attended[...]
    mix = mixes[:, : 2 * RANK].astype(BF16)
    back = backs[:, : 2 * RANK].astype(BF16)
    mix_qkv, mix_fc1 = mix[:, :RANK], mix[:, RANK:]
    back_dense, back_fc2 = back[:, :RANK], back[:, RANK:]
    mix_dense = mm_nt(att, local_maps[:, dense_at:fc1_at])
    grad_local[0, :, dense_at:fc1_at] += mm_tn(back_dense, att)
    grad_full[0, :, d : 2 * d] += mm_tn(mix_dense.astype(BF16), branch[...])
    back_qkv = jnp.zeros(mix_dense.shape, F32)
    for c, part in enumerate((dq, dk, dv)):
        lanes = slice(c * share, (c + 1) * share)
        back_qkv += mm_nt(part[...], local_maps[:, lanes])
        grad_local[0, :, lanes] += mm_tn(mix_qkv, part[...])
    grad_full[0, :, 0:d] += mm_tn(back_qkv.astype(BF16), normed[...])
    mix_fc2, back_fc1 = mlp_half(
        normed,
        branch,
        mix_fc1,
        back_fc2,
        w1,
        w2,
        local_maps[:, fc1_at : fc1_at + fh],
        local_maps[:, fc2_at : fc2_at + fh],
        fc1_bias,
        active,
        hidden_grad,
        (
            grad_local.at[0, :, fc1_at : fc1_at + fh],
            grad_local.at[0, :, fc1_at + fh : fc1_at + 2 * fh],
        ),
    )
    for at in range(0, d, 512):
        lanes = slice(at, at + 512)
        total = mm(att, wd[:, lanes]) + mm(active[...], w2[:, lanes])
        out_sum[:, lanes] = total.astype(BF16)
        total = mm_nt(hidden_grad[...], w1[lanes, :])
        for c, part in enumerate((dq, dk, dv)):
            total += mm_nt(part[...], wq[c, lanes, :])
        grad_sum[:, lanes] = total.astype(BF16)
    carried[:, 0:RANK] = mix_dense
    carried[:, RANK : 2 * RANK] = mix_fc2
    carried[:, 2 * RANK : 3 * RANK] = back_qkv
    carried[:, 3 * RANK : 4 * RANK] = back_fc1


def last_kernel(
    ff,
    counts,
    resumed,
    meta,
    order,
    normed,
    branch,
    out_part,
    grad_part,
    mixes,
    backs,
    carried,
    local_maps,
    full_maps,
    fc1_bias,
    gain,
    ln_bias,
    *rest,
):
    refs, rest = split_refs(rest, counts)
    if resumed:
        local_before, full_before = rest[9:11]
        rest = rest[11:]
    outs, grads = rest[0:4], rest[4:8]
    row_sums, grad_local, grad_full = rest[8:11]
    w1, w2, active, hidden_grad, sem = rest[11:]

    @pl.when(pl.program_id(0) == 0)
    def _():
        sems = [sem.at[i] for i in range(sem.shape[0])]
        run_copies(mlp_copies(refs[0], refs[1], order, w1, w2, sems))
        if resumed:
            grad_local[...] = local_before[...]
            grad_full[...] = full_before[...]
        else:
            grad_local[...] = jnp.zeros_like(grad_local)
            grad_full[...] = jnp.zeros_like(grad_full)

    member = meta[0]
    d = normed.shape[1]
    fh = w1.shape[1]
    fc1_at = d
    fc2_at = fc1_at + ff
    start = ff - fh
    mix_fc1 = mixes[:, RANK : 2 * RANK].astype(BF16)
    back_fc2 = backs[:, RANK : 2 * RANK].astype(BF16)
    mix_fc2, back_fc1 = mlp_half(
        normed,
        branch,
        mix_fc1,
        back_fc2,
        w1,
        w2,
        local_maps[:, fc1_at + start : fc1_at + ff],
        local_maps[:, fc2_at + start : fc2_at + ff],
        fc1_bias,
        active,
        hidden_grad,
        (grad_local.at[:, 0:fh], grad_local.at[:, fh : 2 * fh]),
    )
    mix_fc2 = (mix_fc2 + carried[:, RANK : 2 * RANK]).astype(BF16)
    back_fc1 = (back_fc1 + carried[:, 3 * RANK : 4 * RANK]).astype(BF16)
    grad_full[:, d : 2 * d] += mm_tn(mix_fc2, branch[...])
    grad_full[:, 0:d] += mm_tn(back_fc1, normed[...])
    out_mix = jnp.concatenate([carried[:, 0:RANK].astype(BF16), mix_fc2], 1)
    in_mix = jnp.concatenate([carried[:, 2 * RANK : 3 * RANK].astype(BF16), back_fc1], 1)
    rows = normed.shape[0]
    first = jnp.zeros((rows, 1), F32)
    second = jnp.zeros((rows, 1), F32)
    width = d // 4
    for r in range(4):
        offset = pl.multiple_of((member ^ r) * width, width)
        lanes = pl.ds(offset, width)

        def maps(i, offset=offset):
            return full_maps[:, pl.ds(pl.multiple_of(i * d + offset, width), width)]

        out = out_part[:, lanes].astype(F32) + mm(active[...], w2[:, lanes])
        out += mm(out_mix, jnp.concatenate([maps(2), maps(3)], 0))
        outs[r][...] = out.astype(BF16)
        total = grad_part[:, lanes].astype(F32) + mm_nt(hidden_grad[...], w1[lanes, :])
        total += mm(in_mix, jnp.concatenate([maps(0), maps(1)], 0))
        grads[r][...] = total.astype(BF16)
        first += jnp.sum(total * gain[:, lanes], -1, keepdims=True)
        second += jnp.sum(
            total * (normed[:, lanes].astype(F32) - ln_bias[:, lanes]), -1, keepdims=True
        )
    lane = lax.broadcasted_iota(jnp.int32, (rows, 128), 1)
    row_sums[...] = jnp.transpose(jnp.where(lane == 0, first, second))[0:8, :]


def kept_rows(length, rows):
    slot = pl.program_id(0) * rows + lax.broadcasted_iota(jnp.int32, (rows, 1), 0)
    return (slot < length).astype(F32)


def out_kernel(seq, meta, x, part, first, second, bias, out):
    rows, share = part.shape
    total = part[...].astype(F32) + first[...].astype(F32) + second[...].astype(F32)
    value = x[:, 0].reshape(rows, share).astype(F32) + total + bias[...]
    value = value * kept_rows(meta[1 + seq], rows)
    out[...] = value.astype(BF16).reshape(out.shape)


def grad_kernel(seq, d, meta, x, cot, part, first, second, stats, row_sums, gain, out):
    rows, share = part.shape
    total = part[...].astype(F32) + first[...].astype(F32) + second[...].astype(F32)
    mean, scale = stats[:, 0:1], stats[:, 1:2]
    unit = (x[:, 0].reshape(rows, share).astype(F32) - mean) * scale
    sums = jnp.transpose(
        jnp.concatenate([row_sums[...], jnp.zeros((120, rows), F32)], 0)
    ) * (1.0 / d)
    value = scale * (total * gain[...] - sums[:, 0:1] - unit * sums[:, 1:2])
    value += kept_rows(meta[1 + seq], rows) * cot[:, 0].reshape(rows, share).astype(F32)
    out[...] = value.astype(BF16).reshape(out.shape)


def local(
    tokens,
    cotangent,
    lengths,
    adapter_index,
    ln_gain,
    ln_bias,
    w_qkv,
    qkv_bias,
    w_dense,
    w_fc1,
    fc1_bias,
    w_fc2,
    out_bias,
    qkv_down,
    qkv_up,
    dense_down,
    dense_up,
    fc1_down,
    fc1_up,
    fc2_down,
    fc2_up,
):
    groups = lax.axis_size("dp")
    members = lax.axis_size("mp")
    group = lax.axis_index("dp")
    member = lax.axis_index("mp")
    seqs = tokens.shape[0] // groups
    block, share = tokens.shape[1], tokens.shape[2]
    d = share * members
    ff = w_fc1.shape[1]
    tiles = SLOT // TILE
    per_tile = TILE // block
    count_rows = seqs * SLOT
    permutation, dealt_lengths, dealt_adapters = deal(lengths, adapter_index, groups, seqs)
    my_lengths = lax.dynamic_slice_in_dim(dealt_lengths, group * seqs, seqs)
    my_adapters = lax.dynamic_slice_in_dim(dealt_adapters, group * seqs, seqs)
    meta = jnp.concatenate([member[None].astype(jnp.int32), my_lengths, my_adapters])

    def near(value):
        return lax.ppermute(value, "mp", [(i, i ^ 1) for i in range(members)])

    def far(value):
        return lax.ppermute(value, "mp", [(i, i ^ 2) for i in range(members)])

    def hop(value):
        return near(value[0:8])

    def dealt(values):
        return move_rows(gather_rows_kernel, permutation, (values,), "gather_rows")

    def entered(values):
        return lax.all_to_all(values, "dp", split_axis=0, concat_axis=0, tiled=True)

    def widened(mine, across):
        shape = (groups, seqs, block, share)
        return tuple(a.reshape(shape) for a in (mine, near(mine), across, near(across)))

    dealt_tokens = dealt(tokens)
    my_tokens = entered(dealt_tokens)
    far_tokens = far(my_tokens)

    wide = (d // groups) % 128 == 0
    inner = 2
    outer = groups // inner
    place_out, place_in = group // inner, group % inner

    def gathered(weight, axis):
        if wide:
            return (lax.all_gather(weight, "dp", axis=0, tiled=False),)
        return (lax.all_gather(weight, "dp", axis=axis, tiled=True)[None],)

    def beside(value):
        return lax.ppermute(value, "dp", [(i, i ^ 1) for i in range(groups)])

    def onward(value):
        return lax.ppermute(value, "dp", [(i, (i + inner) % groups) for i in range(groups)])

    def ring(weight, *waits):
        held = [weight]
        crossed = []
        for k in range(outer - 1):
            step = after(held[k], *waits, *crossed[-1:])
            crossed.append(beside(held[k]))
            held.append(onward(step))
            waits = ()
        done = tuple(held) + tuple(crossed)
        crossed.append(beside(held[-1]))
        return tuple(a for pair in zip(held, crossed, strict=True) for a in pair), done

    pieces = share // w_dense.shape[1]
    ring_sems = pltpu.SemaphoreType.DMA((3 + pieces, groups))
    order = jnp.stack(
        [
            (place_out - k) % outer * inner + (place_in + j) % inner
            for k in range(outer)
            for j in range(inner)
        ]
    ).astype(jnp.int32)
    if wide:
        rows = [w_dense[i * w_dense.shape[1] : (i + 1) * w_dense.shape[1]] for i in range(pieces)]
        packed = jnp.concatenate([w_qkv.reshape(-1, share), jnp.concatenate(rows, 1)], 0)
        ring_slots, ring_early = ring(packed, my_tokens)
    else:
        ring_slots, ring_early = gathered(w_qkv, 1) + gathered(w_dense, 1), ()
    rows_in = widened(my_tokens, after(far_tokens, *ring_early))
    cos, up, down = rotary_tables()
    gain_row = ln_gain[None, :]
    bias_row = ln_bias[None, :]

    piece = pl.BlockSpec((per_tile, 1, block, share), lambda s, t, *_: (t, s, 0, 0))
    wide_row = pl.BlockSpec((TILE, d), lambda s, t, *_: (s * tiles + t, 0))
    share_row = pl.BlockSpec((TILE, share), lambda s, t, *_: (s * tiles + t, 0))
    stat_row = pl.BlockSpec((TILE, 128), lambda s, t, *_: (s * tiles + t, 0))
    table_row = pl.BlockSpec((TILE, 128), lambda s, t, *_: (t, 0))
    cols = 4 * share + 2 * ff
    local_map = pl.BlockSpec((RANK, cols), lambda s, t, meta, *_: (meta[1 + seqs + s], 0))
    full_map = pl.BlockSpec((RANK, 4 * d), lambda s, t, *_: (s, 0))

    def whole(shape):
        return pl.BlockSpec(shape, lambda s, t, *_: tuple(0 for _ in shape))

    def shaped(*shape, dtype=BF16):
        return jax.ShapeDtypeStruct(shape, dtype)

    def cost(flops, nbytes, exps=0):
        return pl.CostEstimate(
            flops=int(flops * COST), transcendentals=int(exps * COST), bytes_accessed=int(nbytes * COST)
        )

    limit = pltpu.CompilerParams(vmem_limit_bytes=58 * 1024 * 1024)

    normed, stats = pl.pallas_call(
        norm_kernel,
        out_shape=(shaped(count_rows, d), shaped(count_rows, 128, dtype=F32)),
        grid_spec=pltpu.PrefetchScalarGridSpec(
            num_scalar_prefetch=1,
            grid=(seqs, tiles),
            in_specs=[piece] * 4 + [whole((1, d))] * 2,
            out_specs=[wide_row, stat_row],
            scratch_shapes=[pltpu.VMEM((TILE, d), F32)],
        ),
        compiler_params=limit,
        cost_estimate=cost(10 * count_rows * d, 4 * count_rows * d),
        name="norm_rows",
    )(meta, *rows_in, gain_row, bias_row)

    my_cotangent = entered(after(dealt(cotangent), *ring_early, *rows_in))
    fh = ff * FIRST // 8
    fl = ff - fh
    local_part = jnp.concatenate(
        [qkv_up[0], qkv_up[1], qkv_up[2], dense_down, fc1_up, fc2_down], 1
    ).astype(BF16)
    cols = local_part.shape[1]
    full_rows = qkv_down.shape[0]
    full_part = jnp.stack([qkv_down, fc1_down, dense_up, fc2_up], 1).astype(BF16)
    full_part = after(full_part, dealt_tokens)
    full_part = jnp.transpose(full_part.reshape(full_rows, 4, members, share), (2, 0, 1, 3))
    full_part = lax.all_to_all(
        full_part.reshape(members, full_rows, 4 * share),
        "mp",
        split_axis=0,
        concat_axis=0,
        tiled=True,
    )
    all_part = jnp.concatenate(
        [local_part, full_part.reshape(members * full_rows, 4 * share)], 1
    )
    all_part = after(all_part, my_tokens)
    local_maps = lax.all_gather(all_part, "dp", axis=0, tiled=True)
    my_maps = jnp.stack(
        [
            lax.dynamic_slice(
                local_maps, (my_adapters[s] * RANK, cols), (RANK, 4 * share)
            )
            for s in range(seqs)
        ]
    ).reshape(seqs * RANK, 4, share)
    full_maps = jnp.transpose(lax.all_gather(my_maps, "mp", axis=0, tiled=False), (1, 2, 0, 3))
    full_maps = full_maps.reshape(seqs * RANK, 4 * d)
    w_fc1, w_fc2 = after(w_fc1, my_cotangent), after(w_fc2, my_cotangent)
    my_cotangent = after(my_cotangent, full_maps, *ring_slots)
    far_cotangent = far(my_cotangent)

    def mlp_weights(j):
        start, stop = (0, fh) if j == 0 else (fh, ff)
        first, second = w_fc1[:, start:stop], w_fc2[start:stop, :]
        if not wide:
            return gathered(first, 0), gathered(second, 1)
        width = second.shape[1]
        parts = [second[i : i + width] for i in range(0, stop - start, width)]
        packed = jnp.concatenate([first, jnp.concatenate(parts, 1)], 0)
        return (lax.all_gather(packed, "dp", axis=0, tiled=False),), ()

    halves_fc = [mlp_weights(j) for j in range(2)]
    slots = groups
    dense_at = 3 * share

    queries, keys, values, mixes = pl.pallas_call(
        functools.partial(qkv_kernel, len(ring_slots)),
        out_shape=(
            shaped(count_rows, share),
            shaped(count_rows, share),
            shaped(count_rows, share),
            shaped(count_rows, 128, dtype=F32),
        ),
        grid_spec=pltpu.PrefetchScalarGridSpec(
            num_scalar_prefetch=2,
            grid=(seqs, tiles),
            in_specs=[wide_row, local_map, full_map, whole((3, share))]
            + [table_row] * 3
            + [ANY] * len(ring_slots),
            out_specs=[share_row, share_row, share_row, stat_row],
            scratch_shapes=[
                pltpu.VMEM((3, d, share), BF16),
                ring_sems,
            ],
        ),
        compiler_params=limit,
        cost_estimate=cost(6 * count_rows * d * share, 16 * 2**20),
        name="project_rows",
    )(meta, order, normed, local_maps, full_maps, qkv_bias.astype(F32), cos, up, down, *ring_slots)

    projected = hop(mixes)
    grads_in = widened(my_cotangent, after(far_cotangent, projected))
    branch, attn_grad, backs = pl.pallas_call(
        functools.partial(branch_kernel, len(ring_slots), dense_at),
        out_shape=(
            shaped(count_rows, d),
            shaped(count_rows, share),
            shaped(count_rows, 128, dtype=F32),
        ),
        grid_spec=pltpu.PrefetchScalarGridSpec(
            num_scalar_prefetch=2,
            grid=(seqs, tiles),
            in_specs=[piece] * 4 + [local_map, full_map] + [ANY] * (1 + len(ring_slots)),
            out_specs=[wide_row, share_row, stat_row],
            scratch_shapes=[
                pltpu.VMEM((TILE, d), BF16),
                pltpu.VMEM((share, d), BF16),
                ring_sems,
            ],
        ),
        compiler_params=limit,
        cost_estimate=cost(2 * count_rows * d * share, 20 * 2**20),
        name="branch_rows",
    )(meta, order, *grads_in, local_maps, full_maps, projected, *ring_slots)

    pair = pl.BlockSpec((SLOT, 128), lambda s, h, *_: (s, h))
    attended, dq, dk, dv = pl.pallas_call(
        attention_kernel,
        out_shape=(shaped(count_rows, share),) * 4,
        grid_spec=pltpu.PrefetchScalarGridSpec(
            num_scalar_prefetch=1,
            grid=(seqs, share // 128),
            in_specs=[pair] * 4 + [whole((SLOT, 128))] * 3,
            out_specs=[pair] * 4,
            scratch_shapes=[
                pltpu.VMEM((SLOT, 128), F32),
                pltpu.VMEM((SLOT, 128), F32),
                pltpu.VMEM((SLOT, 128), F32),
            ],
        ),
        compiler_params=limit,
        cost_estimate=cost(
            6 * 4 * count_rows * SLOT * share, 16 * 2**20, count_rows * SLOT * share // HD
        ),
        name="attend_rows",
    )(meta, queries, keys, values, attn_grad, cos, up, down)

    big = BIG
    big_tiles = SLOT // big

    def big_row(width):
        return pl.BlockSpec((big, width), lambda s, t, *_: (s * big_tiles + t, 0))

    def per_seq(*shape):
        return pl.BlockSpec((1,) + shape, lambda s, t, *_: (s,) + tuple(0 for _ in shape))

    first_weights = (ring_slots,) + halves_fc[0]
    counts = tuple(len(w) for w in first_weights)
    first_cols = 4 * share + 2 * fh
    bias_all = fc1_bias.astype(F32)[None, :]
    out_part, grad_part, carried, local_first, full_first = pl.pallas_call(
        functools.partial(first_kernel, ff, counts),
        out_shape=(
            shaped(count_rows, d),
            shaped(count_rows, d),
            shaped(count_rows, 128, dtype=F32),
            shaped(seqs, RANK, first_cols, dtype=F32),
            shaped(seqs, RANK, 2 * d, dtype=F32),
        ),
        grid_spec=pltpu.PrefetchScalarGridSpec(
            num_scalar_prefetch=2,
            grid=(seqs, big_tiles),
            in_specs=[big_row(d)] * 2
            + [big_row(share)] * 4
            + [big_row(128)] * 2
            + [local_map, full_map, whole((1, fh))]
            + [ANY] * sum(counts),
            out_specs=[
                big_row(d),
                big_row(d),
                big_row(128),
                per_seq(RANK, first_cols),
                per_seq(RANK, 2 * d),
            ],
            scratch_shapes=[
                pltpu.VMEM((3, d, share), BF16),
                pltpu.VMEM((share, d), BF16),
                pltpu.VMEM((d, fh), BF16),
                pltpu.VMEM((fh, d), BF16),
                pltpu.VMEM((big, fh), BF16),
                pltpu.VMEM((big, fh), BF16),
                ring_sems,
                pltpu.SemaphoreType.DMA((1 + fh // (d // slots), slots)),
            ],
        ),
        compiler_params=limit,
        cost_estimate=cost(
            8 * count_rows * d * fh + 8 * count_rows * d * share, 80 * 2**20, count_rows * fh
        ),
        name="first_half",
    )(
        meta,
        order,
        normed,
        branch,
        attended,
        dq,
        dk,
        dv,
        mixes,
        backs,
        local_maps,
        full_maps,
        bias_all[:, :fh],
        *[a for w in first_weights for a in w],
    )

    def add_low(left, right):
        return (left.astype(F32) + right.astype(F32)).astype(BF16)

    def half_reduced(parts):
        return add_low(parts[2], near(parts[3]))

    def reduced(parts, half):
        return parts[0], near(parts[1]), far(half)

    adapters = qkv_down.shape[0] * groups * members // RANK
    owned = adapters * RANK // groups

    blocks = RANK // owned
    each = owned // members

    def spread_sums(local_grad, full_grad):
        width = full_grad.shape[2]
        rows = full_grad.astype(BF16).reshape(seqs, blocks, members, each, width)
        rows = jnp.transpose(rows, (2, 0, 1, 3, 4)).reshape(members, seqs * blocks * each, width)
        traded = lax.all_to_all(rows, "mp", split_axis=0, concat_axis=0, tiled=True)
        mine = jnp.sum(traded.astype(F32), 0).reshape(seqs, blocks * each * members, width // members)
        update = jnp.concatenate([local_grad, mine], 2)
        spread = jnp.zeros((adapters,) + update.shape[1:], F32)
        for s in range(seqs):
            here = jnp.arange(adapters, dtype=jnp.int32) == my_adapters[s]
            spread = spread + jnp.where(here[:, None, None], update[s][None], 0.0)
        return spread.astype(BF16).reshape(groups, owned, update.shape[2])

    def owned_sums(arrived, width):
        summed = jnp.sum(arrived.astype(F32), 0)
        mine = summed[:, width:].reshape(each, -1, d)
        return summed, jnp.transpose(mine, (1, 0, 2))

    sent_first = spread_sums(local_first, full_first)
    arrived_first = entered(sent_first)
    last_weights = halves_fc[1]
    counts = tuple(len(w) for w in last_weights)
    my_gain = lax.dynamic_slice_in_dim(gain_row, member * share, share, 1)
    def last_call(seq, first_tile, count, token, given):
        def rows_of(width):
            return pl.BlockSpec((big, width), lambda t, *_: (seq * big_tiles + first_tile + t, 0))

        def fixed(shape, first=0):
            return pl.BlockSpec(shape, lambda t, *_: (first,) + (0,) * (len(shape) - 1))

        def own(width):
            return pl.BlockSpec((big, width), lambda t, *_: (first_tile + t, 0))

        sum_block = pl.BlockSpec((8, big), lambda t, *_: (0, first_tile + t))
        own_map = pl.BlockSpec((RANK, cols), lambda t, meta, *_: (meta[1 + seqs + seq], 0))
        operands = (
            token,
            order,
            normed,
            branch,
            out_part,
            grad_part,
            mixes,
            backs,
            carried,
            local_maps,
            full_maps,
            bias_all[:, fh:],
            gain_row,
            bias_row,
            *[a for w in last_weights for a in w],
        )
        given = tuple(given)
        return pl.pallas_call(
            functools.partial(
                last_kernel, ff, counts, len(given) > 0
            ),
            out_shape=(shaped(SLOT, share),) * 8
            + (
                shaped(8, SLOT, dtype=F32),
                shaped(RANK, 2 * fl, dtype=F32),
                shaped(RANK, 2 * d, dtype=F32),
            ),
            grid_spec=pltpu.PrefetchScalarGridSpec(
                num_scalar_prefetch=2,
                grid=(count,),
                in_specs=[rows_of(d)] * 4
                + [rows_of(128)] * 3
                + [own_map, fixed((RANK, 4 * d), seq)]
                + [fixed((1, fl)), fixed((1, d)), fixed((1, d))]
                + [ANY] * (sum(counts) + 9 * (len(given) > 0))
                + [fixed((RANK, 2 * fl)), fixed((RANK, 2 * d))] * (len(given) > 0),
                out_specs=[own(share)] * 8
                + [sum_block, fixed((RANK, 2 * fl)), fixed((RANK, 2 * d))],
                scratch_shapes=[
                    pltpu.VMEM((d, fl), BF16),
                    pltpu.VMEM((fl, d), BF16),
                    pltpu.VMEM((big, fl), BF16),
                    pltpu.VMEM((big, fl), BF16),
                    pltpu.SemaphoreType.DMA((1 + fl // (d // slots), slots)),
                ],
            ),
            input_output_aliases={len(operands) + i: i for i in range(len(given))},
            compiler_params=limit,
            cost_estimate=cost(
                8 * count * big * d * fl, 10 * count * 2**20, count * big * fl
            ),
            name="last_half",
        )(*operands, *given)

    def out_call(seq, parts):
        return pl.pallas_call(
            functools.partial(out_kernel, seq),
            out_shape=shaped(groups, block, share),
            grid_spec=pltpu.PrefetchScalarGridSpec(
                num_scalar_prefetch=1,
                grid=(tiles,),
                in_specs=[piece_of(seq)] + [own_row] * 3 + [row_block],
                out_specs=back_block,
            ),
            compiler_params=limit,
            cost_estimate=cost(6 * SLOT * share, 10 * SLOT * share),
            name="output_rows",
        )(meta, rows_in[0], *parts, out_bias.astype(F32)[None, :])

    def grad_call(seq, parts, totals):
        return pl.pallas_call(
            functools.partial(grad_kernel, seq, d),
            out_shape=shaped(groups, block, share),
            grid_spec=pltpu.PrefetchScalarGridSpec(
                num_scalar_prefetch=1,
                grid=(tiles,),
                in_specs=[piece_of(seq)] * 2
                + [own_row] * 3
                + [
                    pl.BlockSpec((TILE, 128), lambda t, *_: (seq * tiles + t, 0)),
                    pl.BlockSpec((8, TILE), lambda t, *_: (0, t)),
                    row_block,
                ],
                out_specs=back_block,
            ),
            compiler_params=limit,
            cost_estimate=cost(10 * SLOT * share, 12 * SLOT * share),
            name="input_grad_rows",
        )(meta, rows_in[0], grads_in[0], *parts, stats, totals, my_gain)

    def piece_of(seq):
        return pl.BlockSpec((per_tile, 1, block, share), lambda t, *_: (t, seq, 0, 0))

    own_row = pl.BlockSpec((TILE, share), lambda t, *_: (t, 0))
    row_block = pl.BlockSpec((1, share), lambda t, *_: (0, 0))
    back_block = pl.BlockSpec((per_tile, block, share), lambda t, *_: (t, 0, 0))

    def near_sums(results, *waits):
        parts = [after(results[r], *waits) if r in (2, 6) else results[r] for r in range(8)]
        half_sums = results[8] + near(results[8])
        return parts, half_reduced(parts[0:4]), half_reduced(parts[4:8]), half_sums

    def far_sums(parts, half_out, half_grad, half_sums):
        return (
            reduced(parts[0:4], half_out),
            reduced(parts[4:8], half_grad),
            half_sums + far(half_sums),
        )

    back_outs = []
    back_grads = []
    local_last = []
    full_last = []
    waits = (arrived_first,)
    token = after(meta, sent_first)
    for seq in range(seqs):
        if seq == 0:
            results = last_call(seq, 0, big_tiles, token, ())
        else:
            results = last_call(seq, 0, big_tiles // 2, token, ())
            out_rows = out_call(seq - 1, after(out_parts, results[9]))
            results = last_call(
                seq, big_tiles // 2, big_tiles // 2, after(meta, out_rows), results
            )
            back_outs.append(entered(after(out_rows, *back_grads)))
        local_last.append(results[9])
        full_last.append(results[10])
        halves = near_sums(results, *waits)
        if seq > 0:
            grad_rows = grad_call(seq - 1, after(grad_parts, results[9]), row_totals)
            back_grads.append(entered(after(grad_rows, back_outs[-1])))
        out_parts, grad_parts, row_totals = far_sums(*halves)
        token = after(meta, *halves[1:])
        waits = (out_parts[2], grad_parts[2])
    sent_last = spread_sums(jnp.stack(local_last), after(jnp.stack(full_last), *halves[1:]))
    out_rows = out_call(seqs - 1, out_parts)
    back_outs.append(entered(after(out_rows, *back_grads)))
    grad_rows = grad_call(seqs - 1, grad_parts, row_totals)
    arrived_last = entered(after(sent_last, grad_rows, back_outs[-1]))
    back_grads.append(entered(after(grad_rows, arrived_last)))
    output = move_rows(scatter_rows_kernel, permutation, back_outs, "scatter_rows")
    input_grad = move_rows(scatter_rows_kernel, permutation, back_grads, "scatter_rows")

    first_sums, first_full = owned_sums(arrived_first, first_cols)
    last_sums, last_full = owned_sums(arrived_last, 2 * fl)
    fc1_at = 4 * share
    return (
        output,
        input_grad,
        first_full[0],
        jnp.stack([first_sums[:, c * share : (c + 1) * share] for c in range(3)], 0),
        first_sums[:, dense_at:fc1_at],
        first_full[1],
        last_full[0],
        jnp.concatenate([first_sums[:, fc1_at : fc1_at + fh], last_sums[:, 0:fl]], 1),
        jnp.concatenate(
            [first_sums[:, fc1_at + fh : fc1_at + 2 * fh], last_sums[:, fl : 2 * fl]], 1
        ),
        last_full[1],
    )


def solution(mesh):
    return jax.shard_map(
        local,
        mesh=mesh,
        in_specs=(
            P(None, "dp", "mp"),
            P(None, "dp", "mp"),
            P(),
            P(),
            P(),
            P(),
            P(None, "dp", "mp"),
            P(None, "mp"),
            P("mp", "dp"),
            P("dp", "mp"),
            P("mp"),
            P("mp", "dp"),
            P("mp"),
            P(("dp", "mp"), None),
            P(None, "dp", "mp"),
            P("dp", "mp"),
            P(("dp", "mp"), None),
            P(("dp", "mp"), None),
            P("dp", "mp"),
            P("dp", "mp"),
            P(("dp", "mp"), None),
        ),
        out_specs=(
            P(None, "dp", "mp"),
            P(None, "dp", "mp"),
            P(("dp", "mp"), None),
            P(None, "dp", "mp"),
            P("dp", "mp"),
            P(("dp", "mp"), None),
            P(("dp", "mp"), None),
            P("dp", "mp"),
            P("dp", "mp"),
            P(("dp", "mp"), None),
        ),
        check_vma=False,
    )
```

```python
import functools

import jax
import jax.numpy as jnp
import numpy as np
from jax import lax
from jax.experimental import pallas as pl
from jax.experimental.pallas import tpu as pltpu
from jax.sharding import PartitionSpec as P

HD = 64
ROT = 32
RANK = 16
SLOT = 1024
EPSILON = 1e-05
MASKED = -1e30
BF16 = jnp.bfloat16
F32 = jnp.float32
ANY = pl.BlockSpec(memory_space=pl.ANY)
TILE = 256
BIG = 256
FIRST = 5
COST = 1.0


def after(value, *others):
    return lax.optimization_barrier((value,) + others)[0] if others else value


def mm(left, right):
    return jnp.dot(left, right, preferred_element_type=F32)


def mm_nt(left, right):
    return lax.dot_general(left, right, (((1,), (1,)), ((), ())), preferred_element_type=F32)


def mm_tn(left, right):
    return lax.dot_general(left, right, (((0,), (0,)), ((), ())), preferred_element_type=F32)


def rotary_tables():
    half = ROT // 2
    places = np.arange(SLOT, dtype=np.float32)
    frequency = np.float32(1.0) / np.float32(10000.0) ** (
        np.arange(half, dtype=np.float32) * np.float32(2.0) / np.float32(ROT)
    )
    phases = (places[:, None] * frequency[None, :]).astype(np.float32)
    cosine, sine = np.cos(phases), np.sin(phases)
    zero = np.zeros_like(sine)
    rest = np.zeros((SLOT, HD - ROT), np.float32)
    cos_head = np.concatenate([cosine, cosine, rest + 1.0], 1)
    up_head = np.concatenate([-sine, zero, rest], 1)
    down_head = np.concatenate([zero, sine, rest], 1)
    return tuple(
        jnp.asarray(np.concatenate([t, t], 1), F32) for t in (cos_head, up_head, down_head)
    )


def rotate(value, cos, up, down):
    return (
        value * cos
        + pltpu.roll(value, 128 - ROT // 2, axis=1) * up
        + pltpu.roll(value, ROT // 2, axis=1) * down
    )


def deal(lengths, adapter_index, groups, local_seqs):
    count = lengths.shape[0]
    pos = jnp.arange(count, dtype=jnp.int32)
    ranking = lengths * count + pos
    rank = jnp.sum((ranking[None, :] > ranking[:, None]).astype(jnp.int32), 1)
    round_num = rank // groups
    within = rank % groups
    target = jnp.where(round_num % 2 == 0, within, groups - 1 - within)
    place = target * local_seqs + round_num
    chosen = (place[None, :] == pos[:, None]).astype(jnp.int32)

    def pick(values):
        return jnp.sum(chosen * values[None, :], 1).astype(jnp.int32)

    return pick(pos), pick(lengths), pick(adapter_index)


def gather_rows_kernel(order, source, target, held, sem_in, sem_out):
    count = source.shape[0]
    fetch = [
        pltpu.make_async_copy(source.at[order[i]], held.at[i], sem_in.at[i]) for i in range(count)
    ]
    store = [pltpu.make_async_copy(held.at[i], target.at[i], sem_out.at[i]) for i in range(count)]
    for copy in fetch:
        copy.start()
    for i in range(count):
        fetch[i].wait()
        store[i].start()
    for copy in store:
        copy.wait()


def scatter_rows_kernel(order, *refs):
    seqs = len(refs) - 4
    sources, (target, held, sem_in, sem_out) = refs[:seqs], refs[seqs:]
    groups = sources[0].shape[0]
    fetch = []
    store = []
    for g in range(groups):
        for s in range(seqs):
            i = g * seqs + s
            source = sources[s].at[g, 0 : held.shape[1]]
            fetch.append(pltpu.make_async_copy(source, held.at[i], sem_in.at[i]))
            store.append(pltpu.make_async_copy(held.at[i], target.at[order[i]], sem_out.at[i]))
    for copy in fetch:
        copy.start()
    for take, put in zip(fetch, store, strict=True):
        take.wait()
        put.start()
    for copy in store:
        copy.wait()


def move_rows(kernel, order, arrays, name):
    count = sum(a.shape[0] for a in arrays)
    rest = arrays[0].shape[1:]
    size = sum(a.size for a in arrays)
    return pl.pallas_call(
        kernel,
        out_shape=jax.ShapeDtypeStruct((count,) + rest, BF16),
        grid_spec=pltpu.PrefetchScalarGridSpec(
            num_scalar_prefetch=1,
            grid=(1,),
            in_specs=[ANY] * len(arrays),
            out_specs=ANY,
            scratch_shapes=[
                pltpu.VMEM((count,) + rest, BF16),
                pltpu.SemaphoreType.DMA((count,)),
                pltpu.SemaphoreType.DMA((count,)),
            ],
        ),
        compiler_params=pltpu.CompilerParams(vmem_limit_bytes=16 * 1024 * 1024),
        cost_estimate=pl.CostEstimate(flops=0, transcendentals=0, bytes_accessed=int(4 * size * COST)),
        name=name,
    )(order, *arrays)


def weight_copies(kind, refs, order, target, sem, stacked):
    count = refs[0].shape[0] if stacked else len(refs)
    rows = target.shape[1 if kind in ("q", "lane") else 0]
    width = rows // count
    copies = []
    for s in range(count):
        source = refs[0].at[s] if stacked else refs[s]
        offset = s * width if stacked else pl.multiple_of(order[s] * width, width)
        if kind == "q":
            place = target.at[:, pl.ds(offset, width), :]
        elif kind == "row":
            place = target.at[pl.ds(offset, width), :]
        else:
            place = target.at[:, pl.ds(offset, width)]
        copies.append(pltpu.make_async_copy(source, place, sem.at[s]))
    return copies


def ring_copies(refs, order, sems, wq, wd):
    copies = []
    if len(refs[0].shape) > 2:
        for i, target in ((0, wq), (3, wd)):
            if target is not None:
                source = refs[min(i, 1)].at[0]
                copies.append(pltpu.make_async_copy(source, target, sems.at[i, 0]))
        return copies
    width = refs[0].shape[0] // 4
    for s, ref in enumerate(refs):
        place = pl.ds(pl.multiple_of(order[s] * width, width), width)
        for c in range(3):
            if wq is not None:
                source = ref.at[c * width : (c + 1) * width, :]
                copies.append(
                    pltpu.make_async_copy(source, wq.at[c, place, :], sems.at[c, s])
                )
        for i in range(ref.shape[1] // width):
            if wd is not None:
                lanes = slice(i * width, (i + 1) * width)
                source = ref.at[3 * width : 4 * width, lanes]
                copies.append(
                    pltpu.make_async_copy(source, wd.at[lanes, place], sems.at[3 + i, s])
                )
    return copies


def mlp_copies(first, second, order, w1, w2, sems):
    if second:
        copies = weight_copies("row", first, order, w1, sems[0], True)
        return copies + weight_copies("lane", second, order, w2, sems[1], True)
    packed = first[0]
    count = packed.shape[0]
    width = w1.shape[0] // count
    copies = []
    for s in range(count):
        lanes = pl.ds(s * width, width)
        copies.append(
            pltpu.make_async_copy(packed.at[s, 0:width, :], w1.at[lanes, :], sems[0].at[s])
        )
        for i in range(0, w2.shape[0], width):
            copies.append(
                pltpu.make_async_copy(
                    packed.at[s, width : 2 * width, i : i + width],
                    w2.at[i : i + width, lanes],
                    sems[1 + i // width].at[s],
                )
            )
    return copies


def first_step():
    return (pl.program_id(0) == 0) & (pl.program_id(1) == 0)


def norm_kernel(meta, a0, a1, a2, a3, gain, bias, normed, stats, row):
    member = meta[0]
    share = a0.shape[-1]
    for r, ref in enumerate((a0, a1, a2, a3)):
        offset = pl.multiple_of((member ^ r) * share, share)
        row[:, pl.ds(offset, share)] = ref[:, 0].reshape(row.shape[0], share).astype(F32)
    value = row[...]
    mean = jnp.mean(value, -1, keepdims=True)
    centred = value - mean
    scale = lax.rsqrt(jnp.mean(centred * centred, -1, keepdims=True) + EPSILON)
    normed[...] = (centred * scale * gain[...] + bias[...]).astype(BF16)
    lane = lax.broadcasted_iota(jnp.int32, stats.shape, 1)
    stats[...] = jnp.where(lane == 0, mean, scale)


def qkv_kernel(
    count, meta, order, normed, local_maps, full_maps, bias, cos, up, down, *rest
):
    weights, rest = rest[:count], rest[count:]
    queries, keys, values, mixes, w, sem = rest

    @pl.when(first_step())
    def _():
        run_copies(ring_copies(weights, order, sem, w, None))

    x = normed[...]
    d = x.shape[1]
    share = queries.shape[1]
    maps = jnp.concatenate([full_maps[:, 0:d], full_maps[:, d : 2 * d]], 0)
    mix = mm_nt(x, maps)
    mixes[:, : 2 * RANK] = mix
    mix_low = mix[:, :RANK].astype(BF16)
    for c, out in enumerate((queries, keys, values)):
        value = mm(x, w[c]) + bias[c : c + 1, :] + mm(
            mix_low, local_maps[:, c * share : (c + 1) * share]
        )
        if c == 2:
            out[...] = value.astype(BF16)
        else:
            for j in range(share // 128):
                part = value[:, j * 128 : (j + 1) * 128]
                out[:, j * 128 : (j + 1) * 128] = rotate(
                    part, cos[...], up[...], down[...]
                ).astype(BF16)


def branch_kernel(
    count, places, meta, order, a0, a1, a2, a3, local_maps, full_maps, token, *rest
):
    weights, rest = rest[:count], rest[count:]
    branch, attn_grad, backs, row, w, sem = rest

    @pl.when(first_step())
    def _():
        run_copies(ring_copies(weights, order, sem, None, w))

    member = meta[0]
    length = meta[1 + pl.program_id(0)]
    share = a0.shape[-1]
    d = row.shape[1]
    dense_at = places
    for r, ref in enumerate((a0, a1, a2, a3)):
        offset = pl.multiple_of((member ^ r) * share, share)
        row[:, pl.ds(offset, share)] = ref[:, 0].reshape(row.shape[0], share)
    slot = pl.program_id(1) * row.shape[0] + lax.broadcasted_iota(jnp.int32, (row.shape[0], 1), 0)
    keep = (slot < length).astype(F32)
    value = (row[...].astype(F32) * keep).astype(BF16)
    branch[...] = value
    maps = jnp.concatenate([full_maps[:, 2 * d : 3 * d], full_maps[:, 3 * d : 4 * d]], 0)
    back = mm_nt(value, maps)
    backs[:, : 2 * RANK] = back
    attn_grad[...] = (
        mm_nt(value, w[...])
        + mm(back[:, :RANK].astype(BF16), local_maps[:, dense_at : dense_at + share])
    ).astype(BF16)


def attention_kernel(
    meta,
    queries,
    keys,
    values,
    out_grad,
    cos,
    up,
    down,
    attended,
    dq,
    dk,
    dv,
    dk_sum,
    dv_sum,
    outside,
):
    length = meta[1 + pl.program_id(0)]
    rows = 512
    heads = 128 // HD

    @pl.when(pl.program_id(1) == 0)
    def _():
        place = lax.broadcasted_iota(jnp.int32, outside.shape, 0)
        outside[...] = jnp.where(place < length, 0.0, MASKED)

    zero = jnp.zeros((), BF16)
    head_of = lax.broadcasted_iota(jnp.int32, (SLOT, 128), 1) // HD
    own_keys = [jnp.where(head_of == h, keys[...], zero) for h in range(heads)]
    own_values = [jnp.where(head_of == h, values[...], zero) for h in range(heads)]
    below = lax.broadcasted_iota(jnp.int32, (rows, rows), 0) <= lax.broadcasted_iota(
        jnp.int32, (rows, rows), 1
    )
    dk_sum[...] = jnp.zeros_like(dk_sum)
    dv_sum[...] = jnp.zeros_like(dv_sum)
    for at in range(0, SLOT, rows):
        n = at + rows
        all_q = queries[at:n, :] * jnp.asarray(0.125, BF16)
        all_g = out_grad[at:n, :]
        out = jnp.zeros((128, rows), F32)
        dq_sum = jnp.zeros((128, rows), F32)
        for h in range(heads):
            q = jnp.where(head_of[:rows] == h, all_q, zero)
            g = jnp.where(head_of[:rows] == h, all_g, zero)
            score = mm_nt(keys[0:n, :], q)
            score = score + jnp.concatenate([outside[0:n, :]] * (rows // 128), 1)
            corner = jnp.where(below, score[at:n], MASKED)
            score = jnp.concatenate([score[0:at], corner], 0) if at else corner
            weight = jnp.exp(score - jnp.max(score, 0, keepdims=True))
            probs = weight * (1.0 / jnp.sum(weight, 0, keepdims=True))
            low = probs.astype(BF16)
            prob_grad = mm_nt(values[0:n, :], g)
            inner = jnp.sum(probs * prob_grad, 0, keepdims=True)
            score_grad = (probs * (prob_grad - inner)).astype(BF16)
            out += mm_tn(own_values[h][0:n], low)
            dq_sum += mm_tn(own_keys[h][0:n], score_grad)
            dk_sum[0:n, :] += mm(score_grad, q)
            dv_sum[0:n, :] += mm(low, g)
        attended[at:n, :] = jnp.transpose(out).astype(BF16)
        dq[at:n, :] = rotate(
            jnp.transpose(dq_sum) * 0.125, cos[at:n, :], -up[at:n, :], -down[at:n, :]
        ).astype(BF16)
    dk[...] = rotate(dk_sum[...], cos[...], -up[...], -down[...]).astype(BF16)
    dv[...] = dv_sum[...].astype(BF16)


def mlp_half(
    x, b, mix_fc1, back_fc2, w1, w2, up_maps, down_maps, fc1_bias, active, hidden_grad, grads
):
    step = 512
    for at in range(0, w1.shape[1], step):
        lanes = slice(at, min(at + step, w1.shape[1]))
        v = mm(x[...], w1[:, lanes]) + fc1_bias[:, lanes] + mm(mix_fc1, up_maps[:, lanes])
        square = v * v
        t = jnp.tanh(0.7978845608028654 * (v + 0.044715 * v * square))
        half = 0.5 * (1.0 + t)
        slope = half + (0.5 * 0.7978845608028654) * v * (1.0 - t * t) * (
            1.0 + (3.0 * 0.044715) * square
        )
        active[:, lanes] = (v * half).astype(BF16)
        pull = mm_nt(b[...], w2[lanes, :]) + mm(back_fc2, down_maps[:, lanes])
        hidden_grad[:, lanes] = (pull * slope).astype(BF16)
    grads[0][...] += mm_tn(mix_fc1, hidden_grad[...])
    grads[1][...] += mm_tn(back_fc2, active[...])
    return mm_nt(active[...], down_maps), mm_nt(hidden_grad[...], up_maps)


def run_copies(copies):
    for c in copies:
        c.start()
    for c in copies:
        c.wait()


def split_refs(rest, counts):
    refs = []
    for count in counts:
        refs.append(rest[:count])
        rest = rest[count:]
    return refs, rest


def first_kernel(
    ff,
    counts,
    meta,
    order,
    normed,
    branch,
    attended,
    dq,
    dk,
    dv,
    mixes,
    backs,
    local_maps,
    full_maps,
    fc1_bias,
    *rest,
):
    refs, rest = split_refs(rest, counts)
    out_sum, grad_sum, carried, grad_local, grad_full = rest[0:5]
    wq, wd, w1, w2, active, hidden_grad, sem, fc_sem = rest[5:]

    @pl.when(first_step())
    def _():
        copies = ring_copies(refs[0], order, sem, wq, wd)
        sems = [fc_sem.at[i] for i in range(fc_sem.shape[0])]
        run_copies(copies + mlp_copies(refs[1], refs[2], order, w1, w2, sems))

    @pl.when(pl.program_id(1) == 0)
    def _():
        grad_local[...] = jnp.zeros_like(grad_local)
        grad_full[...] = jnp.zeros_like(grad_full)

    d = normed.shape[1]
    share = attended.shape[1]
    fh = w1.shape[1]
    dense_at = 3 * share
    fc1_at = dense_at + share
    fc2_at = fc1_at + ff
    att = attended[...]
    mix = mixes[:, : 2 * RANK].astype(BF16)
    back = backs[:, : 2 * RANK].astype(BF16)
    mix_qkv, mix_fc1 = mix[:, :RANK], mix[:, RANK:]
    back_dense, back_fc2 = back[:, :RANK], back[:, RANK:]
    mix_dense = mm_nt(att, local_maps[:, dense_at:fc1_at])
    grad_local[0, :, dense_at:fc1_at] += mm_tn(back_dense, att)
    grad_full[0, :, d : 2 * d] += mm_tn(mix_dense.astype(BF16), branch[...])
    back_qkv = jnp.zeros(mix_dense.shape, F32)
    for c, part in enumerate((dq, dk, dv)):
        lanes = slice(c * share, (c + 1) * share)
        back_qkv += mm_nt(part[...], local_maps[:, lanes])
        grad_local[0, :, lanes] += mm_tn(mix_qkv, part[...])
    grad_full[0, :, 0:d] += mm_tn(back_qkv.astype(BF16), normed[...])
    mix_fc2, back_fc1 = mlp_half(
        normed,
        branch,
        mix_fc1,
        back_fc2,
        w1,
        w2,
        local_maps[:, fc1_at : fc1_at + fh],
        local_maps[:, fc2_at : fc2_at + fh],
        fc1_bias,
        active,
        hidden_grad,
        (
            grad_local.at[0, :, fc1_at : fc1_at + fh],
            grad_local.at[0, :, fc1_at + fh : fc1_at + 2 * fh],
        ),
    )
    for at in range(0, d, 512):
        lanes = slice(at, at + 512)
        total = mm(att, wd[:, lanes]) + mm(active[...], w2[:, lanes])
        out_sum[:, lanes] = total.astype(BF16)
        total = mm_nt(hidden_grad[...], w1[lanes, :])
        for c, part in enumerate((dq, dk, dv)):
            total += mm_nt(part[...], wq[c, lanes, :])
        grad_sum[:, lanes] = total.astype(BF16)
    carried[:, 0:RANK] = mix_dense
    carried[:, RANK : 2 * RANK] = mix_fc2
    carried[:, 2 * RANK : 3 * RANK] = back_qkv
    carried[:, 3 * RANK : 4 * RANK] = back_fc1


def last_kernel(
    ff,
    counts,
    resumed,
    meta,
    order,
    normed,
    branch,
    out_part,
    grad_part,
    mixes,
    backs,
    carried,
    local_maps,
    full_maps,
    fc1_bias,
    gain,
    ln_bias,
    *rest,
):
    refs, rest = split_refs(rest, counts)
    if resumed:
        local_before, full_before = rest[9:11]
        rest = rest[11:]
    outs, grads = rest[0:4], rest[4:8]
    row_sums, grad_local, grad_full = rest[8:11]
    w1, w2, active, hidden_grad, sem = rest[11:]

    @pl.when(pl.program_id(0) == 0)
    def _():
        sems = [sem.at[i] for i in range(sem.shape[0])]
        run_copies(mlp_copies(refs[0], refs[1], order, w1, w2, sems))
        if resumed:
            grad_local[...] = local_before[...]
            grad_full[...] = full_before[...]
        else:
            grad_local[...] = jnp.zeros_like(grad_local)
            grad_full[...] = jnp.zeros_like(grad_full)

    member = meta[0]
    d = normed.shape[1]
    fh = w1.shape[1]
    fc1_at = d
    fc2_at = fc1_at + ff
    start = ff - fh
    mix_fc1 = mixes[:, RANK : 2 * RANK].astype(BF16)
    back_fc2 = backs[:, RANK : 2 * RANK].astype(BF16)
    mix_fc2, back_fc1 = mlp_half(
        normed,
        branch,
        mix_fc1,
        back_fc2,
        w1,
        w2,
        local_maps[:, fc1_at + start : fc1_at + ff],
        local_maps[:, fc2_at + start : fc2_at + ff],
        fc1_bias,
        active,
        hidden_grad,
        (grad_local.at[:, 0:fh], grad_local.at[:, fh : 2 * fh]),
    )
    mix_fc2 = (mix_fc2 + carried[:, RANK : 2 * RANK]).astype(BF16)
    back_fc1 = (back_fc1 + carried[:, 3 * RANK : 4 * RANK]).astype(BF16)
    grad_full[:, d : 2 * d] += mm_tn(mix_fc2, branch[...])
    grad_full[:, 0:d] += mm_tn(back_fc1, normed[...])
    out_mix = jnp.concatenate([carried[:, 0:RANK].astype(BF16), mix_fc2], 1)
    in_mix = jnp.concatenate([carried[:, 2 * RANK : 3 * RANK].astype(BF16), back_fc1], 1)
    rows = normed.shape[0]
    first = jnp.zeros((rows, 1), F32)
    second = jnp.zeros((rows, 1), F32)
    width = d // 4
    for r in range(4):
        offset = pl.multiple_of((member ^ r) * width, width)
        lanes = pl.ds(offset, width)

        def maps(i, offset=offset):
            return full_maps[:, pl.ds(pl.multiple_of(i * d + offset, width), width)]

        out = out_part[:, lanes].astype(F32) + mm(active[...], w2[:, lanes])
        out += mm(out_mix, jnp.concatenate([maps(2), maps(3)], 0))
        outs[r][...] = out.astype(BF16)
        total = grad_part[:, lanes].astype(F32) + mm_nt(hidden_grad[...], w1[lanes, :])
        total += mm(in_mix, jnp.concatenate([maps(0), maps(1)], 0))
        grads[r][...] = total.astype(BF16)
        first += jnp.sum(total * gain[:, lanes], -1, keepdims=True)
        second += jnp.sum(
            total * (normed[:, lanes].astype(F32) - ln_bias[:, lanes]), -1, keepdims=True
        )
    lane = lax.broadcasted_iota(jnp.int32, (rows, 128), 1)
    row_sums[...] = jnp.transpose(jnp.where(lane == 0, first, second))[0:8, :]


def kept_rows(length, rows):
    slot = pl.program_id(0) * rows + lax.broadcasted_iota(jnp.int32, (rows, 1), 0)
    return (slot < length).astype(F32)


def out_kernel(seq, meta, x, part, first, second, bias, out):
    rows, share = part.shape
    total = part[...].astype(F32) + first[...].astype(F32) + second[...].astype(F32)
    value = x[:, 0].reshape(rows, share).astype(F32) + total + bias[...]
    value = value * kept_rows(meta[1 + seq], rows)
    out[...] = value.astype(BF16).reshape(out.shape)


def grad_kernel(seq, d, meta, x, cot, part, first, second, stats, row_sums, gain, out):
    rows, share = part.shape
    total = part[...].astype(F32) + first[...].astype(F32) + second[...].astype(F32)
    mean, scale = stats[:, 0:1], stats[:, 1:2]
    unit = (x[:, 0].reshape(rows, share).astype(F32) - mean) * scale
    sums = jnp.transpose(
        jnp.concatenate([row_sums[...], jnp.zeros((120, rows), F32)], 0)
    ) * (1.0 / d)
    value = scale * (total * gain[...] - sums[:, 0:1] - unit * sums[:, 1:2])
    value += kept_rows(meta[1 + seq], rows) * cot[:, 0].reshape(rows, share).astype(F32)
    out[...] = value.astype(BF16).reshape(out.shape)


def local(
    tokens,
    cotangent,
    lengths,
    adapter_index,
    ln_gain,
    ln_bias,
    w_qkv,
    qkv_bias,
    w_dense,
    w_fc1,
    fc1_bias,
    w_fc2,
    out_bias,
    qkv_down,
    qkv_up,
    dense_down,
    dense_up,
    fc1_down,
    fc1_up,
    fc2_down,
    fc2_up,
):
    groups = lax.axis_size("dp")
    members = lax.axis_size("mp")
    group = lax.axis_index("dp")
    member = lax.axis_index("mp")
    seqs = tokens.shape[0] // groups
    block, share = tokens.shape[1], tokens.shape[2]
    d = share * members
    ff = w_fc1.shape[1]
    tiles = SLOT // TILE
    per_tile = TILE // block
    count_rows = seqs * SLOT
    permutation, dealt_lengths, dealt_adapters = deal(lengths, adapter_index, groups, seqs)
    my_lengths = lax.dynamic_slice_in_dim(dealt_lengths, group * seqs, seqs)
    my_adapters = lax.dynamic_slice_in_dim(dealt_adapters, group * seqs, seqs)
    meta = jnp.concatenate([member[None].astype(jnp.int32), my_lengths, my_adapters])

    def near(value):
        return lax.ppermute(value, "mp", [(i, i ^ 1) for i in range(members)])

    def far(value):
        return lax.ppermute(value, "mp", [(i, i ^ 2) for i in range(members)])

    def hop(value):
        return near(value[0:8])

    def dealt(values):
        return move_rows(gather_rows_kernel, permutation, (values,), "gather_rows")

    def entered(values):
        return lax.all_to_all(values, "dp", split_axis=0, concat_axis=0, tiled=True)

    def widened(mine, across):
        shape = (groups, seqs, block, share)
        return tuple(a.reshape(shape) for a in (mine, near(mine), across, near(across)))

    dealt_tokens = dealt(tokens)
    my_tokens = entered(dealt_tokens)
    far_tokens = far(my_tokens)

    wide = (d // groups) % 128 == 0
    inner = 2
    outer = groups // inner
    place_out, place_in = group // inner, group % inner

    def gathered(weight, axis):
        if wide:
            return (lax.all_gather(weight, "dp", axis=0, tiled=False),)
        return (lax.all_gather(weight, "dp", axis=axis, tiled=True)[None],)

    def beside(value):
        return lax.ppermute(value, "dp", [(i, i ^ 1) for i in range(groups)])

    def onward(value):
        return lax.ppermute(value, "dp", [(i, (i + inner) % groups) for i in range(groups)])

    def ring(weight, *waits):
        held = [weight]
        crossed = []
        for k in range(outer - 1):
            step = after(held[k], *waits, *crossed[-1:])
            crossed.append(beside(held[k]))
            held.append(onward(step))
            waits = ()
        done = tuple(held) + tuple(crossed)
        crossed.append(beside(held[-1]))
        return tuple(a for pair in zip(held, crossed, strict=True) for a in pair), done

    pieces = share // w_dense.shape[1]
    ring_sems = pltpu.SemaphoreType.DMA((3 + pieces, groups))
    order = jnp.stack(
        [
            (place_out - k) % outer * inner + (place_in + j) % inner
            for k in range(outer)
            for j in range(inner)
        ]
    ).astype(jnp.int32)
    if wide:
        rows = [w_dense[i * w_dense.shape[1] : (i + 1) * w_dense.shape[1]] for i in range(pieces)]
        packed = jnp.concatenate([w_qkv.reshape(-1, share), jnp.concatenate(rows, 1)], 0)
        ring_slots, ring_early = ring(packed, my_tokens)
    else:
        ring_slots, ring_early = gathered(w_qkv, 1) + gathered(w_dense, 1), ()
    rows_in = widened(my_tokens, after(far_tokens, *ring_early))
    cos, up, down = rotary_tables()
    gain_row = ln_gain[None, :]
    bias_row = ln_bias[None, :]

    piece = pl.BlockSpec((per_tile, 1, block, share), lambda s, t, *_: (t, s, 0, 0))
    wide_row = pl.BlockSpec((TILE, d), lambda s, t, *_: (s * tiles + t, 0))
    share_row = pl.BlockSpec((TILE, share), lambda s, t, *_: (s * tiles + t, 0))
    stat_row = pl.BlockSpec((TILE, 128), lambda s, t, *_: (s * tiles + t, 0))
    table_row = pl.BlockSpec((TILE, 128), lambda s, t, *_: (t, 0))
    cols = 4 * share + 2 * ff
    local_map = pl.BlockSpec((RANK, cols), lambda s, t, meta, *_: (meta[1 + seqs + s], 0))
    full_map = pl.BlockSpec((RANK, 4 * d), lambda s, t, *_: (s, 0))

    def whole(shape):
        return pl.BlockSpec(shape, lambda s, t, *_: tuple(0 for _ in shape))

    def shaped(*shape, dtype=BF16):
        return jax.ShapeDtypeStruct(shape, dtype)

    def cost(flops, nbytes, exps=0):
        return pl.CostEstimate(
            flops=int(flops * COST), transcendentals=int(exps * COST), bytes_accessed=int(nbytes * COST)
        )

    limit = pltpu.CompilerParams(vmem_limit_bytes=58 * 1024 * 1024)

    normed, stats = pl.pallas_call(
        norm_kernel,
        out_shape=(shaped(count_rows, d), shaped(count_rows, 128, dtype=F32)),
        grid_spec=pltpu.PrefetchScalarGridSpec(
            num_scalar_prefetch=1,
            grid=(seqs, tiles),
            in_specs=[piece] * 4 + [whole((1, d))] * 2,
            out_specs=[wide_row, stat_row],
            scratch_shapes=[pltpu.VMEM((TILE, d), F32)],
        ),
        compiler_params=limit,
        cost_estimate=cost(10 * count_rows * d, 4 * count_rows * d),
        name="norm_rows",
    )(meta, *rows_in, gain_row, bias_row)

    my_cotangent = entered(after(dealt(cotangent), *ring_early, *rows_in))
    fh = ff * FIRST // 8
    fl = ff - fh
    local_part = jnp.concatenate(
        [qkv_up[0], qkv_up[1], qkv_up[2], dense_down, fc1_up, fc2_down], 1
    ).astype(BF16)
    cols = local_part.shape[1]
    full_rows = qkv_down.shape[0]
    full_part = jnp.stack([qkv_down, fc1_down, dense_up, fc2_up], 1).astype(BF16)
    full_part = after(full_part, dealt_tokens)
    full_part = jnp.transpose(full_part.reshape(full_rows, 4, members, share), (2, 0, 1, 3))
    full_part = lax.all_to_all(
        full_part.reshape(members, full_rows, 4 * share),
        "mp",
        split_axis=0,
        concat_axis=0,
        tiled=True,
    )
    all_part = jnp.concatenate(
        [local_part, full_part.reshape(members * full_rows, 4 * share)], 1
    )
    all_part = after(all_part, my_tokens)
    local_maps = lax.all_gather(all_part, "dp", axis=0, tiled=True)
    my_maps = jnp.stack(
        [
            lax.dynamic_slice(
                local_maps, (my_adapters[s] * RANK, cols), (RANK, 4 * share)
            )
            for s in range(seqs)
        ]
    ).reshape(seqs * RANK, 4, share)
    full_maps = jnp.transpose(lax.all_gather(my_maps, "mp", axis=0, tiled=False), (1, 2, 0, 3))
    full_maps = full_maps.reshape(seqs * RANK, 4 * d)
    w_fc1, w_fc2 = after(w_fc1, my_cotangent), after(w_fc2, my_cotangent)
    my_cotangent = after(my_cotangent, full_maps)
    far_cotangent = far(my_cotangent)

    def mlp_weights(j):
        start, stop = (0, fh) if j == 0 else (fh, ff)
        first, second = w_fc1[:, start:stop], w_fc2[start:stop, :]
        if not wide:
            return gathered(first, 0), gathered(second, 1)
        width = second.shape[1]
        parts = [second[i : i + width] for i in range(0, stop - start, width)]
        packed = jnp.concatenate([first, jnp.concatenate(parts, 1)], 0)
        return (lax.all_gather(packed, "dp", axis=0, tiled=False),), ()

    halves_fc = [mlp_weights(j) for j in range(2)]
    slots = groups
    dense_at = 3 * share

    queries, keys, values, mixes = pl.pallas_call(
        functools.partial(qkv_kernel, len(ring_slots)),
        out_shape=(
            shaped(count_rows, share),
            shaped(count_rows, share),
            shaped(count_rows, share),
            shaped(count_rows, 128, dtype=F32),
        ),
        grid_spec=pltpu.PrefetchScalarGridSpec(
            num_scalar_prefetch=2,
            grid=(seqs, tiles),
            in_specs=[wide_row, local_map, full_map, whole((3, share))]
            + [table_row] * 3
            + [ANY] * len(ring_slots),
            out_specs=[share_row, share_row, share_row, stat_row],
            scratch_shapes=[
                pltpu.VMEM((3, d, share), BF16),
                ring_sems,
            ],
        ),
        compiler_params=limit,
        cost_estimate=cost(6 * count_rows * d * share, 16 * 2**20),
        name="project_rows",
    )(meta, order, normed, local_maps, full_maps, qkv_bias.astype(F32), cos, up, down, *ring_slots)

    projected = hop(mixes)
    grads_in = widened(my_cotangent, after(far_cotangent, projected))
    branch, attn_grad, backs = pl.pallas_call(
        functools.partial(branch_kernel, len(ring_slots), dense_at),
        out_shape=(
            shaped(count_rows, d),
            shaped(count_rows, share),
            shaped(count_rows, 128, dtype=F32),
        ),
        grid_spec=pltpu.PrefetchScalarGridSpec(
            num_scalar_prefetch=2,
            grid=(seqs, tiles),
            in_specs=[piece] * 4 + [local_map, full_map] + [ANY] * (1 + len(ring_slots)),
            out_specs=[wide_row, share_row, stat_row],
            scratch_shapes=[
                pltpu.VMEM((TILE, d), BF16),
                pltpu.VMEM((share, d), BF16),
                ring_sems,
            ],
        ),
        compiler_params=limit,
        cost_estimate=cost(2 * count_rows * d * share, 20 * 2**20),
        name="branch_rows",
    )(meta, order, *grads_in, local_maps, full_maps, projected, *ring_slots)

    pair = pl.BlockSpec((SLOT, 128), lambda s, h, *_: (s, h))
    attended, dq, dk, dv = pl.pallas_call(
        attention_kernel,
        out_shape=(shaped(count_rows, share),) * 4,
        grid_spec=pltpu.PrefetchScalarGridSpec(
            num_scalar_prefetch=1,
            grid=(seqs, share // 128),
            in_specs=[pair] * 4 + [whole((SLOT, 128))] * 3,
            out_specs=[pair] * 4,
            scratch_shapes=[
                pltpu.VMEM((SLOT, 128), F32),
                pltpu.VMEM((SLOT, 128), F32),
                pltpu.VMEM((SLOT, 128), F32),
            ],
        ),
        compiler_params=limit,
        cost_estimate=cost(
            6 * 4 * count_rows * SLOT * share, 16 * 2**20, count_rows * SLOT * share // HD
        ),
        name="attend_rows",
    )(meta, queries, keys, values, attn_grad, cos, up, down)

    big = BIG
    big_tiles = SLOT // big

    def big_row(width):
        return pl.BlockSpec((big, width), lambda s, t, *_: (s * big_tiles + t, 0))

    def per_seq(*shape):
        return pl.BlockSpec((1,) + shape, lambda s, t, *_: (s,) + tuple(0 for _ in shape))

    first_weights = (ring_slots,) + halves_fc[0]
    counts = tuple(len(w) for w in first_weights)
    first_cols = 4 * share + 2 * fh
    bias_all = fc1_bias.astype(F32)[None, :]
    out_part, grad_part, carried, local_first, full_first = pl.pallas_call(
        functools.partial(first_kernel, ff, counts),
        out_shape=(
            shaped(count_rows, d),
            shaped(count_rows, d),
            shaped(count_rows, 128, dtype=F32),
            shaped(seqs, RANK, first_cols, dtype=F32),
            shaped(seqs, RANK, 2 * d, dtype=F32),
        ),
        grid_spec=pltpu.PrefetchScalarGridSpec(
            num_scalar_prefetch=2,
            grid=(seqs, big_tiles),
            in_specs=[big_row(d)] * 2
            + [big_row(share)] * 4
            + [big_row(128)] * 2
            + [local_map, full_map, whole((1, fh))]
            + [ANY] * sum(counts),
            out_specs=[
                big_row(d),
                big_row(d),
                big_row(128),
                per_seq(RANK, first_cols),
                per_seq(RANK, 2 * d),
            ],
            scratch_shapes=[
                pltpu.VMEM((3, d, share), BF16),
                pltpu.VMEM((share, d), BF16),
                pltpu.VMEM((d, fh), BF16),
                pltpu.VMEM((fh, d), BF16),
                pltpu.VMEM((big, fh), BF16),
                pltpu.VMEM((big, fh), BF16),
                ring_sems,
                pltpu.SemaphoreType.DMA((1 + fh // (d // slots), slots)),
            ],
        ),
        compiler_params=limit,
        cost_estimate=cost(
            8 * count_rows * d * fh + 8 * count_rows * d * share, 80 * 2**20, count_rows * fh
        ),
        name="first_half",
    )(
        meta,
        order,
        normed,
        branch,
        attended,
        dq,
        dk,
        dv,
        mixes,
        backs,
        local_maps,
        full_maps,
        bias_all[:, :fh],
        *[a for w in first_weights for a in w],
    )

    def add_low(left, right):
        return (left.astype(F32) + right.astype(F32)).astype(BF16)

    def half_reduced(parts):
        return add_low(parts[2], near(parts[3]))

    def reduced(parts, half):
        return parts[0], near(parts[1]), far(half)

    adapters = qkv_down.shape[0] * groups * members // RANK
    owned = adapters * RANK // groups

    blocks = RANK // owned
    each = owned // members

    def spread_sums(local_grad, full_grad):
        width = full_grad.shape[2]
        rows = full_grad.astype(BF16).reshape(seqs, blocks, members, each, width)
        rows = jnp.transpose(rows, (2, 0, 1, 3, 4)).reshape(members, seqs * blocks * each, width)
        parts = [
            lax.dynamic_index_in_dim(rows, member ^ r, 0, keepdims=False) for r in range(members)
        ]
        total, beside_part, across_part = reduced(parts, half_reduced(parts))
        mine = total.astype(F32) + beside_part.astype(F32) + across_part.astype(F32)
        mine = mine.reshape(seqs, blocks * each * members, width // members)
        update = jnp.concatenate([local_grad, mine], 2)
        spread = jnp.zeros((adapters,) + update.shape[1:], F32)
        for s in range(seqs):
            here = jnp.arange(adapters, dtype=jnp.int32) == my_adapters[s]
            spread = spread + jnp.where(here[:, None, None], update[s][None], 0.0)
        return spread.astype(BF16).reshape(groups, owned, update.shape[2])

    def owned_sums(arrived, width):
        summed = jnp.sum(arrived.astype(F32), 0)
        mine = summed[:, width:].reshape(each, -1, d)
        return summed, jnp.transpose(mine, (1, 0, 2))

    sent_first = spread_sums(local_first, full_first)
    arrived_first = entered(sent_first)
    last_weights = halves_fc[1]
    counts = tuple(len(w) for w in last_weights)
    my_gain = lax.dynamic_slice_in_dim(gain_row, member * share, share, 1)
    def last_call(seq, first_tile, count, token, given):
        def rows_of(width):
            return pl.BlockSpec((big, width), lambda t, *_: (seq * big_tiles + first_tile + t, 0))

        def fixed(shape, first=0):
            return pl.BlockSpec(shape, lambda t, *_: (first,) + (0,) * (len(shape) - 1))

        def own(width):
            return pl.BlockSpec((big, width), lambda t, *_: (first_tile + t, 0))

        sum_block = pl.BlockSpec((8, big), lambda t, *_: (0, first_tile + t))
        own_map = pl.BlockSpec((RANK, cols), lambda t, meta, *_: (meta[1 + seqs + seq], 0))
        operands = (
            token,
            order,
            normed,
            branch,
            out_part,
            grad_part,
            mixes,
            backs,
            carried,
            local_maps,
            full_maps,
            bias_all[:, fh:],
            gain_row,
            bias_row,
            *[a for w in last_weights for a in w],
        )
        given = tuple(given)
        return pl.pallas_call(
            functools.partial(
                last_kernel, ff, counts, len(given) > 0
            ),
            out_shape=(shaped(SLOT, share),) * 8
            + (
                shaped(8, SLOT, dtype=F32),
                shaped(RANK, 2 * fl, dtype=F32),
                shaped(RANK, 2 * d, dtype=F32),
            ),
            grid_spec=pltpu.PrefetchScalarGridSpec(
                num_scalar_prefetch=2,
                grid=(count,),
                in_specs=[rows_of(d)] * 4
                + [rows_of(128)] * 3
                + [own_map, fixed((RANK, 4 * d), seq)]
                + [fixed((1, fl)), fixed((1, d)), fixed((1, d))]
                + [ANY] * (sum(counts) + 9 * (len(given) > 0))
                + [fixed((RANK, 2 * fl)), fixed((RANK, 2 * d))] * (len(given) > 0),
                out_specs=[own(share)] * 8
                + [sum_block, fixed((RANK, 2 * fl)), fixed((RANK, 2 * d))],
                scratch_shapes=[
                    pltpu.VMEM((d, fl), BF16),
                    pltpu.VMEM((fl, d), BF16),
                    pltpu.VMEM((big, fl), BF16),
                    pltpu.VMEM((big, fl), BF16),
                    pltpu.SemaphoreType.DMA((1 + fl // (d // slots), slots)),
                ],
            ),
            input_output_aliases={len(operands) + i: i for i in range(len(given))},
            compiler_params=limit,
            cost_estimate=cost(
                8 * count * big * d * fl, 10 * count * 2**20, count * big * fl
            ),
            name="last_half",
        )(*operands, *given)

    def out_call(seq, parts):
        return pl.pallas_call(
            functools.partial(out_kernel, seq),
            out_shape=shaped(groups, block, share),
            grid_spec=pltpu.PrefetchScalarGridSpec(
                num_scalar_prefetch=1,
                grid=(tiles,),
                in_specs=[piece_of(seq)] + [own_row] * 3 + [row_block],
                out_specs=back_block,
            ),
            compiler_params=limit,
            cost_estimate=cost(6 * SLOT * share, 10 * SLOT * share),
            name="output_rows",
        )(meta, rows_in[0], *parts, out_bias.astype(F32)[None, :])

    def grad_call(seq, parts, totals):
        return pl.pallas_call(
            functools.partial(grad_kernel, seq, d),
            out_shape=shaped(groups, block, share),
            grid_spec=pltpu.PrefetchScalarGridSpec(
                num_scalar_prefetch=1,
                grid=(tiles,),
                in_specs=[piece_of(seq)] * 2
                + [own_row] * 3
                + [
                    pl.BlockSpec((TILE, 128), lambda t, *_: (seq * tiles + t, 0)),
                    pl.BlockSpec((8, TILE), lambda t, *_: (0, t)),
                    row_block,
                ],
                out_specs=back_block,
            ),
            compiler_params=limit,
            cost_estimate=cost(10 * SLOT * share, 12 * SLOT * share),
            name="input_grad_rows",
        )(meta, rows_in[0], grads_in[0], *parts, stats, totals, my_gain)

    def piece_of(seq):
        return pl.BlockSpec((per_tile, 1, block, share), lambda t, *_: (t, seq, 0, 0))

    own_row = pl.BlockSpec((TILE, share), lambda t, *_: (t, 0))
    row_block = pl.BlockSpec((1, share), lambda t, *_: (0, 0))
    back_block = pl.BlockSpec((per_tile, block, share), lambda t, *_: (t, 0, 0))

    def near_sums(results, *waits):
        parts = [after(results[r], *waits) if r in (2, 6) else results[r] for r in range(8)]
        half_sums = results[8] + near(results[8])
        return parts, half_reduced(parts[0:4]), half_reduced(parts[4:8]), half_sums

    def far_sums(parts, half_out, half_grad, half_sums):
        return (
            reduced(parts[0:4], half_out),
            reduced(parts[4:8], half_grad),
            half_sums + far(half_sums),
        )

    back_outs = []
    back_grads = []
    local_last = []
    full_last = []
    waits = (arrived_first,)
    token = after(meta, sent_first)
    for seq in range(seqs):
        if seq == 0:
            results = last_call(seq, 0, big_tiles, token, ())
        else:
            results = last_call(seq, 0, big_tiles // 2, token, ())
            out_rows = out_call(seq - 1, after(out_parts, results[9]))
            results = last_call(
                seq, big_tiles // 2, big_tiles // 2, after(meta, out_rows), results
            )
            back_outs.append(entered(after(out_rows, *back_grads)))
        local_last.append(results[9])
        full_last.append(results[10])
        halves = near_sums(results, *waits)
        if seq > 0:
            grad_rows = grad_call(seq - 1, after(grad_parts, results[9]), row_totals)
            back_grads.append(entered(after(grad_rows, back_outs[-1])))
        out_parts, grad_parts, row_totals = far_sums(*halves)
        token = after(meta, *halves[1:])
        waits = (out_parts[2], grad_parts[2])
    sent_last = spread_sums(jnp.stack(local_last), after(jnp.stack(full_last), *halves[1:]))
    out_rows = out_call(seqs - 1, out_parts)
    merged = jnp.concatenate([out_rows, sent_last.reshape(groups, -1, share)], 1)
    merged = entered(after(merged, *back_grads))
    back_outs.append(merged)
    arrived_last = merged[:, block:].reshape(sent_last.shape)
    grad_rows = grad_call(seqs - 1, grad_parts, row_totals)
    back_grads.append(entered(after(grad_rows, merged)))
    output = move_rows(scatter_rows_kernel, permutation, back_outs, "scatter_rows")
    input_grad = move_rows(scatter_rows_kernel, permutation, back_grads, "scatter_rows")

    first_sums, first_full = owned_sums(arrived_first, first_cols)
    last_sums, last_full = owned_sums(arrived_last, 2 * fl)
    fc1_at = 4 * share
    return (
        output,
        input_grad,
        first_full[0],
        jnp.stack([first_sums[:, c * share : (c + 1) * share] for c in range(3)], 0),
        first_sums[:, dense_at:fc1_at],
        first_full[1],
        last_full[0],
        jnp.concatenate([first_sums[:, fc1_at : fc1_at + fh], last_sums[:, 0:fl]], 1),
        jnp.concatenate(
            [first_sums[:, fc1_at + fh : fc1_at + 2 * fh], last_sums[:, fl : 2 * fl]], 1
        ),
        last_full[1],
    )


def solution(mesh):
    return jax.shard_map(
        local,
        mesh=mesh,
        in_specs=(
            P(None, "dp", "mp"),
            P(None, "dp", "mp"),
            P(),
            P(),
            P(),
            P(),
            P(None, "dp", "mp"),
            P(None, "mp"),
            P("mp", "dp"),
            P("dp", "mp"),
            P("mp"),
            P("mp", "dp"),
            P("mp"),
            P(("dp", "mp"), None),
            P(None, "dp", "mp"),
            P("dp", "mp"),
            P(("dp", "mp"), None),
            P(("dp", "mp"), None),
            P("dp", "mp"),
            P("dp", "mp"),
            P(("dp", "mp"), None),
        ),
        out_specs=(
            P(None, "dp", "mp"),
            P(None, "dp", "mp"),
            P(("dp", "mp"), None),
            P(None, "dp", "mp"),
            P("dp", "mp"),
            P(("dp", "mp"), None),
            P(("dp", "mp"), None),
            P("dp", "mp"),
            P("dp", "mp"),
            P(("dp", "mp"), None),
        ),
        check_vma=False,
    )
```

```python
import functools

import jax
import jax.numpy as jnp
import numpy as np
from jax import lax
from jax.experimental import pallas as pl
from jax.experimental.pallas import tpu as pltpu
from jax.sharding import PartitionSpec as P

HD = 64
ROT = 32
RANK = 16
SLOT = 1024
EPSILON = 1e-05
MASKED = -1e30
BF16 = jnp.bfloat16
F32 = jnp.float32
ANY = pl.BlockSpec(memory_space=pl.ANY)
TILE = 256
BIG = 256
FIRST = 5
COST = 1.0


def after(value, *others):
    return lax.optimization_barrier((value,) + others)[0] if others else value


def mm(left, right):
    return jnp.dot(left, right, preferred_element_type=F32)


def mm_nt(left, right):
    return lax.dot_general(left, right, (((1,), (1,)), ((), ())), preferred_element_type=F32)


def mm_tn(left, right):
    return lax.dot_general(left, right, (((0,), (0,)), ((), ())), preferred_element_type=F32)


def rotary_tables():
    half = ROT // 2
    places = np.arange(SLOT, dtype=np.float32)
    frequency = np.float32(1.0) / np.float32(10000.0) ** (
        np.arange(half, dtype=np.float32) * np.float32(2.0) / np.float32(ROT)
    )
    phases = (places[:, None] * frequency[None, :]).astype(np.float32)
    cosine, sine = np.cos(phases), np.sin(phases)
    zero = np.zeros_like(sine)
    rest = np.zeros((SLOT, HD - ROT), np.float32)
    cos_head = np.concatenate([cosine, cosine, rest + 1.0], 1)
    up_head = np.concatenate([-sine, zero, rest], 1)
    down_head = np.concatenate([zero, sine, rest], 1)
    return tuple(
        jnp.asarray(np.concatenate([t, t], 1), F32) for t in (cos_head, up_head, down_head)
    )


def rotate(value, cos, up, down):
    return (
        value * cos
        + pltpu.roll(value, 128 - ROT // 2, axis=1) * up
        + pltpu.roll(value, ROT // 2, axis=1) * down
    )


def deal(lengths, adapter_index, groups, local_seqs):
    count = lengths.shape[0]
    pos = jnp.arange(count, dtype=jnp.int32)
    ranking = lengths * count + pos
    rank = jnp.sum((ranking[None, :] > ranking[:, None]).astype(jnp.int32), 1)
    round_num = rank // groups
    within = rank % groups
    target = jnp.where(round_num % 2 == 0, within, groups - 1 - within)
    place = target * local_seqs + round_num
    chosen = (place[None, :] == pos[:, None]).astype(jnp.int32)

    def pick(values):
        return jnp.sum(chosen * values[None, :], 1).astype(jnp.int32)

    return pick(pos), pick(lengths), pick(adapter_index)


def gather_rows_kernel(order, source, target, held, sem_in, sem_out):
    count = source.shape[0]
    fetch = [
        pltpu.make_async_copy(source.at[order[i]], held.at[i], sem_in.at[i]) for i in range(count)
    ]
    store = [pltpu.make_async_copy(held.at[i], target.at[i], sem_out.at[i]) for i in range(count)]
    for copy in fetch:
        copy.start()
    for i in range(count):
        fetch[i].wait()
        store[i].start()
    for copy in store:
        copy.wait()


def scatter_rows_kernel(order, *refs):
    seqs = len(refs) - 4
    sources, (target, held, sem_in, sem_out) = refs[:seqs], refs[seqs:]
    groups = sources[0].shape[0]
    fetch = []
    store = []
    for g in range(groups):
        for s in range(seqs):
            i = g * seqs + s
            source = sources[s].at[g, 0 : held.shape[1]]
            fetch.append(pltpu.make_async_copy(source, held.at[i], sem_in.at[i]))
            store.append(pltpu.make_async_copy(held.at[i], target.at[order[i]], sem_out.at[i]))
    for copy in fetch:
        copy.start()
    for take, put in zip(fetch, store, strict=True):
        take.wait()
        put.start()
    for copy in store:
        copy.wait()


def move_rows(kernel, order, arrays, name):
    count = sum(a.shape[0] for a in arrays)
    rest = arrays[0].shape[1:]
    size = sum(a.size for a in arrays)
    return pl.pallas_call(
        kernel,
        out_shape=jax.ShapeDtypeStruct((count,) + rest, BF16),
        grid_spec=pltpu.PrefetchScalarGridSpec(
            num_scalar_prefetch=1,
            grid=(1,),
            in_specs=[ANY] * len(arrays),
            out_specs=ANY,
            scratch_shapes=[
                pltpu.VMEM((count,) + rest, BF16),
                pltpu.SemaphoreType.DMA((count,)),
                pltpu.SemaphoreType.DMA((count,)),
            ],
        ),
        compiler_params=pltpu.CompilerParams(vmem_limit_bytes=16 * 1024 * 1024),
        cost_estimate=pl.CostEstimate(flops=0, transcendentals=0, bytes_accessed=int(4 * size * COST)),
        name=name,
    )(order, *arrays)


def weight_copies(kind, refs, order, target, sem, stacked):
    count = refs[0].shape[0] if stacked else len(refs)
    rows = target.shape[1 if kind in ("q", "lane") else 0]
    width = rows // count
    copies = []
    for s in range(count):
        source = refs[0].at[s] if stacked else refs[s]
        offset = s * width if stacked else pl.multiple_of(order[s] * width, width)
        if kind == "q":
            place = target.at[:, pl.ds(offset, width), :]
        elif kind == "row":
            place = target.at[pl.ds(offset, width), :]
        else:
            place = target.at[:, pl.ds(offset, width)]
        copies.append(pltpu.make_async_copy(source, place, sem.at[s]))
    return copies


def ring_copies(refs, order, sems, wq, wd):
    copies = []
    if len(refs[0].shape) > 2:
        for i, target in ((0, wq), (3, wd)):
            if target is not None:
                source = refs[min(i, 1)].at[0]
                copies.append(pltpu.make_async_copy(source, target, sems.at[i, 0]))
        return copies
    width = refs[0].shape[0] // 4
    for s, ref in enumerate(refs):
        place = pl.ds(pl.multiple_of(order[s] * width, width), width)
        for c in range(3):
            if wq is not None:
                source = ref.at[c * width : (c + 1) * width, :]
                copies.append(
                    pltpu.make_async_copy(source, wq.at[c, place, :], sems.at[c, s])
                )
        for i in range(ref.shape[1] // width):
            if wd is not None:
                lanes = slice(i * width, (i + 1) * width)
                source = ref.at[3 * width : 4 * width, lanes]
                copies.append(
                    pltpu.make_async_copy(source, wd.at[lanes, place], sems.at[3 + i, s])
                )
    return copies


def mlp_copies(first, second, order, w1, w2, sems):
    if second:
        copies = weight_copies("row", first, order, w1, sems[0], True)
        return copies + weight_copies("lane", second, order, w2, sems[1], True)
    packed = first[0]
    count = packed.shape[0]
    width = w1.shape[0] // count
    copies = []
    for s in range(count):
        lanes = pl.ds(s * width, width)
        copies.append(
            pltpu.make_async_copy(packed.at[s, 0:width, :], w1.at[lanes, :], sems[0].at[s])
        )
        for i in range(0, w2.shape[0], width):
            copies.append(
                pltpu.make_async_copy(
                    packed.at[s, width : 2 * width, i : i + width],
                    w2.at[i : i + width, lanes],
                    sems[1 + i // width].at[s],
                )
            )
    return copies


def first_step():
    return (pl.program_id(0) == 0) & (pl.program_id(1) == 0)


def norm_kernel(meta, a0, a1, a2, a3, gain, bias, normed, stats, row):
    member = meta[0]
    share = a0.shape[-1]
    for r, ref in enumerate((a0, a1, a2, a3)):
        offset = pl.multiple_of((member ^ r) * share, share)
        row[:, pl.ds(offset, share)] = ref[:, 0].reshape(row.shape[0], share).astype(F32)
    value = row[...]
    mean = jnp.mean(value, -1, keepdims=True)
    centred = value - mean
    scale = lax.rsqrt(jnp.mean(centred * centred, -1, keepdims=True) + EPSILON)
    normed[...] = (centred * scale * gain[...] + bias[...]).astype(BF16)
    lane = lax.broadcasted_iota(jnp.int32, stats.shape, 1)
    stats[...] = jnp.where(lane == 0, mean, scale)


def qkv_kernel(
    count, meta, order, normed, local_maps, full_maps, bias, cos, up, down, *rest
):
    weights, rest = rest[:count], rest[count:]
    queries, keys, values, mixes, w, sem = rest

    @pl.when(first_step())
    def _():
        run_copies(ring_copies(weights, order, sem, w, None))

    x = normed[...]
    d = x.shape[1]
    share = queries.shape[1]
    maps = jnp.concatenate([full_maps[:, 0:d], full_maps[:, d : 2 * d]], 0)
    mix = mm_nt(x, maps)
    mixes[:, : 2 * RANK] = mix
    mix_low = mix[:, :RANK].astype(BF16)
    for c, out in enumerate((queries, keys, values)):
        value = mm(x, w[c]) + bias[c : c + 1, :] + mm(
            mix_low, local_maps[:, c * share : (c + 1) * share]
        )
        if c == 2:
            out[...] = value.astype(BF16)
        else:
            for j in range(share // 128):
                part = value[:, j * 128 : (j + 1) * 128]
                out[:, j * 128 : (j + 1) * 128] = rotate(
                    part, cos[...], up[...], down[...]
                ).astype(BF16)


def branch_kernel(
    count, places, meta, order, a0, a1, a2, a3, local_maps, full_maps, token, *rest
):
    weights, rest = rest[:count], rest[count:]
    branch, attn_grad, backs, row, w, sem = rest

    @pl.when(first_step())
    def _():
        run_copies(ring_copies(weights, order, sem, None, w))

    member = meta[0]
    length = meta[1 + pl.program_id(0)]
    share = a0.shape[-1]
    d = row.shape[1]
    dense_at = places
    for r, ref in enumerate((a0, a1, a2, a3)):
        offset = pl.multiple_of((member ^ r) * share, share)
        row[:, pl.ds(offset, share)] = ref[:, 0].reshape(row.shape[0], share)
    slot = pl.program_id(1) * row.shape[0] + lax.broadcasted_iota(jnp.int32, (row.shape[0], 1), 0)
    keep = (slot < length).astype(F32)
    value = (row[...].astype(F32) * keep).astype(BF16)
    branch[...] = value
    maps = jnp.concatenate([full_maps[:, 2 * d : 3 * d], full_maps[:, 3 * d : 4 * d]], 0)
    back = mm_nt(value, maps)
    backs[:, : 2 * RANK] = back
    attn_grad[...] = (
        mm_nt(value, w[...])
        + mm(back[:, :RANK].astype(BF16), local_maps[:, dense_at : dense_at + share])
    ).astype(BF16)


def attention_kernel(
    meta,
    queries,
    keys,
    values,
    out_grad,
    cos,
    up,
    down,
    attended,
    dq,
    dk,
    dv,
    dk_sum,
    dv_sum,
    outside,
):
    length = meta[1 + pl.program_id(0)]
    rows = 512
    heads = 128 // HD

    @pl.when(pl.program_id(1) == 0)
    def _():
        place = lax.broadcasted_iota(jnp.int32, outside.shape, 0)
        outside[...] = jnp.where(place < length, 0.0, MASKED)

    zero = jnp.zeros((), BF16)
    head_of = lax.broadcasted_iota(jnp.int32, (SLOT, 128), 1) // HD
    own_keys = [jnp.where(head_of == h, keys[...], zero) for h in range(heads)]
    own_values = [jnp.where(head_of == h, values[...], zero) for h in range(heads)]
    below = lax.broadcasted_iota(jnp.int32, (rows, rows), 0) <= lax.broadcasted_iota(
        jnp.int32, (rows, rows), 1
    )
    dk_sum[...] = jnp.zeros_like(dk_sum)
    dv_sum[...] = jnp.zeros_like(dv_sum)
    for at in range(0, SLOT, rows):
        n = at + rows
        all_q = queries[at:n, :] * jnp.asarray(0.125, BF16)
        all_g = out_grad[at:n, :]
        out = jnp.zeros((128, rows), F32)
        dq_sum = jnp.zeros((128, rows), F32)
        for h in range(heads):
            q = jnp.where(head_of[:rows] == h, all_q, zero)
            g = jnp.where(head_of[:rows] == h, all_g, zero)
            score = mm_nt(keys[0:n, :], q)
            score = score + jnp.concatenate([outside[0:n, :]] * (rows // 128), 1)
            corner = jnp.where(below, score[at:n], MASKED)
            score = jnp.concatenate([score[0:at], corner], 0) if at else corner
            weight = jnp.exp(score - jnp.max(score, 0, keepdims=True))
            probs = weight * (1.0 / jnp.sum(weight, 0, keepdims=True))
            low = probs.astype(BF16)
            prob_grad = mm_nt(values[0:n, :], g)
            inner = jnp.sum(probs * prob_grad, 0, keepdims=True)
            score_grad = (probs * (prob_grad - inner)).astype(BF16)
            out += mm_tn(own_values[h][0:n], low)
            dq_sum += mm_tn(own_keys[h][0:n], score_grad)
            dk_sum[0:n, :] += mm(score_grad, q)
            dv_sum[0:n, :] += mm(low, g)
        attended[at:n, :] = jnp.transpose(out).astype(BF16)
        dq[at:n, :] = rotate(
            jnp.transpose(dq_sum) * 0.125, cos[at:n, :], -up[at:n, :], -down[at:n, :]
        ).astype(BF16)
    dk[...] = rotate(dk_sum[...], cos[...], -up[...], -down[...]).astype(BF16)
    dv[...] = dv_sum[...].astype(BF16)


def mlp_half(
    x, b, mix_fc1, back_fc2, w1, w2, up_maps, down_maps, fc1_bias, active, hidden_grad, grads
):
    step = 512
    for at in range(0, w1.shape[1], step):
        lanes = slice(at, min(at + step, w1.shape[1]))
        v = mm(x[...], w1[:, lanes]) + fc1_bias[:, lanes] + mm(mix_fc1, up_maps[:, lanes])
        square = v * v
        t = jnp.tanh(0.7978845608028654 * (v + 0.044715 * v * square))
        half = 0.5 * (1.0 + t)
        slope = half + (0.5 * 0.7978845608028654) * v * (1.0 - t * t) * (
            1.0 + (3.0 * 0.044715) * square
        )
        active[:, lanes] = (v * half).astype(BF16)
        pull = mm_nt(b[...], w2[lanes, :]) + mm(back_fc2, down_maps[:, lanes])
        hidden_grad[:, lanes] = (pull * slope).astype(BF16)
    grads[0][...] += mm_tn(mix_fc1, hidden_grad[...])
    grads[1][...] += mm_tn(back_fc2, active[...])
    return mm_nt(active[...], down_maps), mm_nt(hidden_grad[...], up_maps)


def run_copies(copies):
    for c in copies:
        c.start()
    for c in copies:
        c.wait()


def split_refs(rest, counts):
    refs = []
    for count in counts:
        refs.append(rest[:count])
        rest = rest[count:]
    return refs, rest


def heads_kernel(
    meta, order, normed, branch, attended, dq, dk, dv, mixes, backs, local_maps, *rest
):
    refs, rest = rest[:-8], rest[-8:]
    out_sum, grad_sum, carried, grad_local, grad_full, wq, wd, sem = rest

    @pl.when(first_step())
    def _():
        run_copies(ring_copies(refs, order, sem, wq, wd))

    @pl.when(pl.program_id(1) == 0)
    def _():
        grad_local[...] = jnp.zeros_like(grad_local)
        grad_full[...] = jnp.zeros_like(grad_full)

    d = normed.shape[1]
    share = attended.shape[1]
    dense_at = 3 * share
    fc1_at = dense_at + share
    att = attended[...]
    mix_qkv = mixes[:, :RANK].astype(BF16)
    back_dense = backs[:, :RANK].astype(BF16)
    mix_dense = mm_nt(att, local_maps[:, dense_at:fc1_at])
    grad_local[0, :, dense_at:fc1_at] += mm_tn(back_dense, att)
    grad_full[0, :, d : 2 * d] += mm_tn(mix_dense.astype(BF16), branch[...])
    back_qkv = jnp.zeros(mix_dense.shape, F32)
    for c, part in enumerate((dq, dk, dv)):
        lanes = slice(c * share, (c + 1) * share)
        back_qkv += mm_nt(part[...], local_maps[:, lanes])
        grad_local[0, :, lanes] += mm_tn(mix_qkv, part[...])
    grad_full[0, :, 0:d] += mm_tn(back_qkv.astype(BF16), normed[...])
    for at in range(0, d, 512):
        lanes = slice(at, at + 512)
        out_sum[:, lanes] = mm(att, wd[:, lanes]).astype(BF16)
        total = mm_nt(dq[...], wq[0, lanes, :])
        for c, part in ((1, dk), (2, dv)):
            total += mm_nt(part[...], wq[c, lanes, :])
        grad_sum[:, lanes] = total.astype(BF16)
    carried[:, 0:RANK] = mix_dense
    carried[:, 2 * RANK : 3 * RANK] = back_qkv


def first_kernel(
    ff,
    counts,
    meta,
    order,
    normed,
    branch,
    out_part,
    grad_part,
    mixes,
    backs,
    heads,
    local_maps,
    fc1_bias,
    *rest,
):
    refs, rest = split_refs(rest, counts)
    out_sum, grad_sum, carried, grad_local = rest[0:4]
    w1, w2, active, hidden_grad, fc_sem = rest[4:]

    @pl.when(first_step())
    def _():
        sems = [fc_sem.at[i] for i in range(fc_sem.shape[0])]
        run_copies(mlp_copies(refs[0], refs[1], order, w1, w2, sems))

    @pl.when(pl.program_id(1) == 0)
    def _():
        grad_local[...] = jnp.zeros_like(grad_local)

    d = normed.shape[1]
    fh = w1.shape[1]
    fc1_at = d
    fc2_at = fc1_at + ff
    mix_fc2, back_fc1 = mlp_half(
        normed,
        branch,
        mixes[:, RANK : 2 * RANK].astype(BF16),
        backs[:, RANK : 2 * RANK].astype(BF16),
        w1,
        w2,
        local_maps[:, fc1_at : fc1_at + fh],
        local_maps[:, fc2_at : fc2_at + fh],
        fc1_bias,
        active,
        hidden_grad,
        (grad_local.at[0, :, 0:fh], grad_local.at[0, :, fh : 2 * fh]),
    )
    for at in range(0, d, 512):
        lanes = slice(at, at + 512)
        total = out_part[:, lanes].astype(F32) + mm(active[...], w2[:, lanes])
        out_sum[:, lanes] = total.astype(BF16)
        total = grad_part[:, lanes].astype(F32) + mm_nt(hidden_grad[...], w1[lanes, :])
        grad_sum[:, lanes] = total.astype(BF16)
    carried[:, 0:RANK] = heads[:, 0:RANK]
    carried[:, RANK : 2 * RANK] = mix_fc2
    carried[:, 2 * RANK : 3 * RANK] = heads[:, 2 * RANK : 3 * RANK]
    carried[:, 3 * RANK : 4 * RANK] = back_fc1


def last_kernel(
    ff,
    counts,
    resumed,
    meta,
    order,
    normed,
    branch,
    out_part,
    grad_part,
    mixes,
    backs,
    carried,
    local_maps,
    full_maps,
    fc1_bias,
    gain,
    ln_bias,
    *rest,
):
    refs, rest = split_refs(rest, counts)
    if resumed:
        local_before, full_before = rest[9:11]
        rest = rest[11:]
    outs, grads = rest[0:4], rest[4:8]
    row_sums, grad_local, grad_full = rest[8:11]
    w1, w2, active, hidden_grad, sem = rest[11:]

    @pl.when(pl.program_id(0) == 0)
    def _():
        sems = [sem.at[i] for i in range(sem.shape[0])]
        run_copies(mlp_copies(refs[0], refs[1], order, w1, w2, sems))
        if resumed:
            grad_local[...] = local_before[...]
            grad_full[...] = full_before[...]
        else:
            grad_local[...] = jnp.zeros_like(grad_local)
            grad_full[...] = jnp.zeros_like(grad_full)

    member = meta[0]
    d = normed.shape[1]
    fh = w1.shape[1]
    fc1_at = d
    fc2_at = fc1_at + ff
    start = ff - fh
    mix_fc1 = mixes[:, RANK : 2 * RANK].astype(BF16)
    back_fc2 = backs[:, RANK : 2 * RANK].astype(BF16)
    mix_fc2, back_fc1 = mlp_half(
        normed,
        branch,
        mix_fc1,
        back_fc2,
        w1,
        w2,
        local_maps[:, fc1_at + start : fc1_at + ff],
        local_maps[:, fc2_at + start : fc2_at + ff],
        fc1_bias,
        active,
        hidden_grad,
        (grad_local.at[:, 0:fh], grad_local.at[:, fh : 2 * fh]),
    )
    mix_fc2 = (mix_fc2 + carried[:, RANK : 2 * RANK]).astype(BF16)
    back_fc1 = (back_fc1 + carried[:, 3 * RANK : 4 * RANK]).astype(BF16)
    grad_full[:, d : 2 * d] += mm_tn(mix_fc2, branch[...])
    grad_full[:, 0:d] += mm_tn(back_fc1, normed[...])
    out_mix = jnp.concatenate([carried[:, 0:RANK].astype(BF16), mix_fc2], 1)
    in_mix = jnp.concatenate([carried[:, 2 * RANK : 3 * RANK].astype(BF16), back_fc1], 1)
    rows = normed.shape[0]
    first = jnp.zeros((rows, 1), F32)
    second = jnp.zeros((rows, 1), F32)
    width = d // 4
    for r in range(4):
        offset = pl.multiple_of((member ^ r) * width, width)
        lanes = pl.ds(offset, width)

        def maps(i, offset=offset):
            return full_maps[:, pl.ds(pl.multiple_of(i * d + offset, width), width)]

        out = out_part[:, lanes].astype(F32) + mm(active[...], w2[:, lanes])
        out += mm(out_mix, jnp.concatenate([maps(2), maps(3)], 0))
        outs[r][...] = out.astype(BF16)
        total = grad_part[:, lanes].astype(F32) + mm_nt(hidden_grad[...], w1[lanes, :])
        total += mm(in_mix, jnp.concatenate([maps(0), maps(1)], 0))
        grads[r][...] = total.astype(BF16)
        first += jnp.sum(total * gain[:, lanes], -1, keepdims=True)
        second += jnp.sum(
            total * (normed[:, lanes].astype(F32) - ln_bias[:, lanes]), -1, keepdims=True
        )
    lane = lax.broadcasted_iota(jnp.int32, (rows, 128), 1)
    row_sums[...] = jnp.transpose(jnp.where(lane == 0, first, second))[0:8, :]


def kept_rows(length, rows):
    slot = pl.program_id(0) * rows + lax.broadcasted_iota(jnp.int32, (rows, 1), 0)
    return (slot < length).astype(F32)


def out_kernel(seq, meta, x, part, first, second, bias, out):
    rows, share = part.shape
    total = part[...].astype(F32) + first[...].astype(F32) + second[...].astype(F32)
    value = x[:, 0].reshape(rows, share).astype(F32) + total + bias[...]
    value = value * kept_rows(meta[1 + seq], rows)
    out[...] = value.astype(BF16).reshape(out.shape)


def grad_kernel(seq, d, meta, x, cot, part, first, second, stats, row_sums, gain, out):
    rows, share = part.shape
    total = part[...].astype(F32) + first[...].astype(F32) + second[...].astype(F32)
    mean, scale = stats[:, 0:1], stats[:, 1:2]
    unit = (x[:, 0].reshape(rows, share).astype(F32) - mean) * scale
    sums = jnp.transpose(
        jnp.concatenate([row_sums[...], jnp.zeros((120, rows), F32)], 0)
    ) * (1.0 / d)
    value = scale * (total * gain[...] - sums[:, 0:1] - unit * sums[:, 1:2])
    value += kept_rows(meta[1 + seq], rows) * cot[:, 0].reshape(rows, share).astype(F32)
    out[...] = value.astype(BF16).reshape(out.shape)


def local(
    tokens,
    cotangent,
    lengths,
    adapter_index,
    ln_gain,
    ln_bias,
    w_qkv,
    qkv_bias,
    w_dense,
    w_fc1,
    fc1_bias,
    w_fc2,
    out_bias,
    qkv_down,
    qkv_up,
    dense_down,
    dense_up,
    fc1_down,
    fc1_up,
    fc2_down,
    fc2_up,
):
    groups = lax.axis_size("dp")
    members = lax.axis_size("mp")
    group = lax.axis_index("dp")
    member = lax.axis_index("mp")
    seqs = tokens.shape[0] // groups
    block, share = tokens.shape[1], tokens.shape[2]
    d = share * members
    ff = w_fc1.shape[1]
    tiles = SLOT // TILE
    per_tile = TILE // block
    count_rows = seqs * SLOT
    permutation, dealt_lengths, dealt_adapters = deal(lengths, adapter_index, groups, seqs)
    my_lengths = lax.dynamic_slice_in_dim(dealt_lengths, group * seqs, seqs)
    my_adapters = lax.dynamic_slice_in_dim(dealt_adapters, group * seqs, seqs)
    meta = jnp.concatenate([member[None].astype(jnp.int32), my_lengths, my_adapters])

    def near(value):
        return lax.ppermute(value, "mp", [(i, i ^ 1) for i in range(members)])

    def far(value):
        return lax.ppermute(value, "mp", [(i, i ^ 2) for i in range(members)])

    def hop(value):
        return near(value[0:8])

    def dealt(values):
        return move_rows(gather_rows_kernel, permutation, (values,), "gather_rows")

    def entered(values):
        return lax.all_to_all(values, "dp", split_axis=0, concat_axis=0, tiled=True)

    def widened(mine, across):
        shape = (groups, seqs, block, share)
        return tuple(a.reshape(shape) for a in (mine, near(mine), across, near(across)))

    dealt_tokens = dealt(tokens)
    my_tokens = entered(dealt_tokens)
    far_tokens = far(my_tokens)

    wide = (d // groups) % 128 == 0
    inner = 2
    outer = groups // inner
    place_out, place_in = group // inner, group % inner

    def gathered(weight, axis):
        if wide:
            return (lax.all_gather(weight, "dp", axis=0, tiled=False),)
        return (lax.all_gather(weight, "dp", axis=axis, tiled=True)[None],)

    def beside(value):
        return lax.ppermute(value, "dp", [(i, i ^ 1) for i in range(groups)])

    def onward(value):
        return lax.ppermute(value, "dp", [(i, (i + inner) % groups) for i in range(groups)])

    def ring(weight, *waits):
        held = [weight]
        crossed = []
        for k in range(outer - 1):
            step = after(held[k], *waits, *crossed[-1:])
            crossed.append(beside(held[k]))
            held.append(onward(step))
            waits = ()
        done = tuple(held) + tuple(crossed)
        crossed.append(beside(held[-1]))
        return tuple(a for pair in zip(held, crossed, strict=True) for a in pair), done

    pieces = share // w_dense.shape[1]
    ring_sems = pltpu.SemaphoreType.DMA((3 + pieces, groups))
    order = jnp.stack(
        [
            (place_out - k) % outer * inner + (place_in + j) % inner
            for k in range(outer)
            for j in range(inner)
        ]
    ).astype(jnp.int32)
    if wide:
        rows = [w_dense[i * w_dense.shape[1] : (i + 1) * w_dense.shape[1]] for i in range(pieces)]
        packed = jnp.concatenate([w_qkv.reshape(-1, share), jnp.concatenate(rows, 1)], 0)
        ring_slots, ring_early = ring(packed, my_tokens)
    else:
        ring_slots, ring_early = gathered(w_qkv, 1) + gathered(w_dense, 1), ()
    rows_in = widened(my_tokens, after(far_tokens, *ring_early))
    cos, up, down = rotary_tables()
    gain_row = ln_gain[None, :]
    bias_row = ln_bias[None, :]

    piece = pl.BlockSpec((per_tile, 1, block, share), lambda s, t, *_: (t, s, 0, 0))
    wide_row = pl.BlockSpec((TILE, d), lambda s, t, *_: (s * tiles + t, 0))
    share_row = pl.BlockSpec((TILE, share), lambda s, t, *_: (s * tiles + t, 0))
    stat_row = pl.BlockSpec((TILE, 128), lambda s, t, *_: (s * tiles + t, 0))
    table_row = pl.BlockSpec((TILE, 128), lambda s, t, *_: (t, 0))
    cols = 4 * share + 2 * ff
    local_map = pl.BlockSpec((RANK, cols), lambda s, t, meta, *_: (meta[1 + seqs + s], 0))
    full_map = pl.BlockSpec((RANK, 4 * d), lambda s, t, *_: (s, 0))

    def whole(shape):
        return pl.BlockSpec(shape, lambda s, t, *_: tuple(0 for _ in shape))

    def shaped(*shape, dtype=BF16):
        return jax.ShapeDtypeStruct(shape, dtype)

    def cost(flops, nbytes, exps=0):
        return pl.CostEstimate(
            flops=int(flops * COST), transcendentals=int(exps * COST), bytes_accessed=int(nbytes * COST)
        )

    limit = pltpu.CompilerParams(vmem_limit_bytes=58 * 1024 * 1024)

    normed, stats = pl.pallas_call(
        norm_kernel,
        out_shape=(shaped(count_rows, d), shaped(count_rows, 128, dtype=F32)),
        grid_spec=pltpu.PrefetchScalarGridSpec(
            num_scalar_prefetch=1,
            grid=(seqs, tiles),
            in_specs=[piece] * 4 + [whole((1, d))] * 2,
            out_specs=[wide_row, stat_row],
            scratch_shapes=[pltpu.VMEM((TILE, d), F32)],
        ),
        compiler_params=limit,
        cost_estimate=cost(10 * count_rows * d, 4 * count_rows * d),
        name="norm_rows",
    )(meta, *rows_in, gain_row, bias_row)

    my_cotangent = entered(after(dealt(cotangent), *ring_early, *rows_in))
    fh = ff * FIRST // 8
    fl = ff - fh
    local_part = jnp.concatenate(
        [qkv_up[0], qkv_up[1], qkv_up[2], dense_down, fc1_up, fc2_down], 1
    ).astype(BF16)
    cols = local_part.shape[1]
    full_rows = qkv_down.shape[0]
    full_part = jnp.stack([qkv_down, fc1_down, dense_up, fc2_up], 1).astype(BF16)
    full_part = after(full_part, dealt_tokens)
    full_part = jnp.transpose(full_part.reshape(full_rows, 4, members, share), (2, 0, 1, 3))
    full_part = lax.all_to_all(
        full_part.reshape(members, full_rows, 4 * share),
        "mp",
        split_axis=0,
        concat_axis=0,
        tiled=True,
    )
    all_part = jnp.concatenate(
        [local_part, full_part.reshape(members * full_rows, 4 * share)], 1
    )
    all_part = after(all_part, my_tokens)
    local_maps = lax.all_gather(all_part, "dp", axis=0, tiled=True)
    my_maps = jnp.stack(
        [
            lax.dynamic_slice(
                local_maps, (my_adapters[s] * RANK, cols), (RANK, 4 * share)
            )
            for s in range(seqs)
        ]
    ).reshape(seqs * RANK, 4, share)
    full_maps = jnp.transpose(lax.all_gather(my_maps, "mp", axis=0, tiled=False), (1, 2, 0, 3))
    full_maps = full_maps.reshape(seqs * RANK, 4 * d)
    w_fc1, w_fc2 = after(w_fc1, my_cotangent), after(w_fc2, my_cotangent)
    my_cotangent = after(my_cotangent, full_maps)
    far_cotangent = far(my_cotangent)

    def mlp_weights(j):
        start, stop = (0, fh) if j == 0 else (fh, ff)
        first, second = w_fc1[:, start:stop], w_fc2[start:stop, :]
        if not wide:
            return gathered(first, 0), gathered(second, 1)
        width = second.shape[1]
        parts = [second[i : i + width] for i in range(0, stop - start, width)]
        packed = jnp.concatenate([first, jnp.concatenate(parts, 1)], 0)
        return (lax.all_gather(packed, "dp", axis=0, tiled=False),), ()

    halves_fc = [mlp_weights(j) for j in range(2)]
    slots = groups
    dense_at = 3 * share

    queries, keys, values, mixes = pl.pallas_call(
        functools.partial(qkv_kernel, len(ring_slots)),
        out_shape=(
            shaped(count_rows, share),
            shaped(count_rows, share),
            shaped(count_rows, share),
            shaped(count_rows, 128, dtype=F32),
        ),
        grid_spec=pltpu.PrefetchScalarGridSpec(
            num_scalar_prefetch=2,
            grid=(seqs, tiles),
            in_specs=[wide_row, local_map, full_map, whole((3, share))]
            + [table_row] * 3
            + [ANY] * len(ring_slots),
            out_specs=[share_row, share_row, share_row, stat_row],
            scratch_shapes=[
                pltpu.VMEM((3, d, share), BF16),
                ring_sems,
            ],
        ),
        compiler_params=limit,
        cost_estimate=cost(6 * count_rows * d * share, 16 * 2**20),
        name="project_rows",
    )(meta, order, normed, local_maps, full_maps, qkv_bias.astype(F32), cos, up, down, *ring_slots)

    projected = hop(mixes)
    grads_in = widened(my_cotangent, after(far_cotangent, projected))
    branch, attn_grad, backs = pl.pallas_call(
        functools.partial(branch_kernel, len(ring_slots), dense_at),
        out_shape=(
            shaped(count_rows, d),
            shaped(count_rows, share),
            shaped(count_rows, 128, dtype=F32),
        ),
        grid_spec=pltpu.PrefetchScalarGridSpec(
            num_scalar_prefetch=2,
            grid=(seqs, tiles),
            in_specs=[piece] * 4 + [local_map, full_map] + [ANY] * (1 + len(ring_slots)),
            out_specs=[wide_row, share_row, stat_row],
            scratch_shapes=[
                pltpu.VMEM((TILE, d), BF16),
                pltpu.VMEM((share, d), BF16),
                ring_sems,
            ],
        ),
        compiler_params=limit,
        cost_estimate=cost(2 * count_rows * d * share, 20 * 2**20),
        name="branch_rows",
    )(meta, order, *grads_in, local_maps, full_maps, projected, *ring_slots)

    pair = pl.BlockSpec((SLOT, 128), lambda s, h, *_: (s, h))
    attended, dq, dk, dv = pl.pallas_call(
        attention_kernel,
        out_shape=(shaped(count_rows, share),) * 4,
        grid_spec=pltpu.PrefetchScalarGridSpec(
            num_scalar_prefetch=1,
            grid=(seqs, share // 128),
            in_specs=[pair] * 4 + [whole((SLOT, 128))] * 3,
            out_specs=[pair] * 4,
            scratch_shapes=[
                pltpu.VMEM((SLOT, 128), F32),
                pltpu.VMEM((SLOT, 128), F32),
                pltpu.VMEM((SLOT, 128), F32),
            ],
        ),
        compiler_params=limit,
        cost_estimate=cost(
            6 * 4 * count_rows * SLOT * share, 16 * 2**20, count_rows * SLOT * share // HD
        ),
        name="attend_rows",
    )(meta, queries, keys, values, attn_grad, cos, up, down)

    big = BIG
    big_tiles = SLOT // big

    def big_row(width):
        return pl.BlockSpec((big, width), lambda s, t, *_: (s * big_tiles + t, 0))

    def per_seq(*shape):
        return pl.BlockSpec((1,) + shape, lambda s, t, *_: (s,) + tuple(0 for _ in shape))

    bias_all = fc1_bias.astype(F32)[None, :]
    out_heads, grad_heads, heads, local_heads, full_heads = pl.pallas_call(
        heads_kernel,
        out_shape=(
            shaped(count_rows, d),
            shaped(count_rows, d),
            shaped(count_rows, 128, dtype=F32),
            shaped(seqs, RANK, 4 * share, dtype=F32),
            shaped(seqs, RANK, 2 * d, dtype=F32),
        ),
        grid_spec=pltpu.PrefetchScalarGridSpec(
            num_scalar_prefetch=2,
            grid=(seqs, big_tiles),
            in_specs=[big_row(d)] * 2
            + [big_row(share)] * 4
            + [big_row(128)] * 2
            + [local_map]
            + [ANY] * len(ring_slots),
            out_specs=[
                big_row(d),
                big_row(d),
                big_row(128),
                per_seq(RANK, 4 * share),
                per_seq(RANK, 2 * d),
            ],
            scratch_shapes=[
                pltpu.VMEM((3, d, share), BF16),
                pltpu.VMEM((share, d), BF16),
                ring_sems,
            ],
        ),
        compiler_params=limit,
        cost_estimate=cost(8 * count_rows * d * share, 48 * 2**20),
        name="head_sums",
    )(meta, order, normed, branch, attended, dq, dk, dv, mixes, backs, local_maps, *ring_slots)

    first_weights = halves_fc[0]
    counts = tuple(len(w) for w in first_weights)
    out_part, grad_part, carried, local_first = pl.pallas_call(
        functools.partial(first_kernel, ff, counts),
        out_shape=(
            shaped(count_rows, d),
            shaped(count_rows, d),
            shaped(count_rows, 128, dtype=F32),
            shaped(seqs, RANK, 2 * fh, dtype=F32),
        ),
        grid_spec=pltpu.PrefetchScalarGridSpec(
            num_scalar_prefetch=2,
            grid=(seqs, big_tiles),
            in_specs=[big_row(d)] * 4
            + [big_row(128)] * 3
            + [local_map, whole((1, fh))]
            + [ANY] * sum(counts),
            out_specs=[big_row(d), big_row(d), big_row(128), per_seq(RANK, 2 * fh)],
            scratch_shapes=[
                pltpu.VMEM((d, fh), BF16),
                pltpu.VMEM((fh, d), BF16),
                pltpu.VMEM((big, fh), BF16),
                pltpu.VMEM((big, fh), BF16),
                pltpu.SemaphoreType.DMA((1 + fh // (d // slots), slots)),
            ],
        ),
        compiler_params=limit,
        cost_estimate=cost(8 * count_rows * d * fh, 60 * 2**20, count_rows * fh),
        name="first_half",
    )(
        meta,
        order,
        normed,
        branch,
        out_heads,
        grad_heads,
        mixes,
        backs,
        heads,
        local_maps,
        bias_all[:, :fh],
        *[a for w in first_weights for a in w],
    )

    def add_low(left, right):
        return (left.astype(F32) + right.astype(F32)).astype(BF16)

    def half_reduced(parts):
        return add_low(parts[2], near(parts[3]))

    def reduced(parts, half):
        return parts[0], near(parts[1]), far(half)

    adapters = qkv_down.shape[0] * groups * members // RANK
    owned = adapters * RANK // groups

    blocks = RANK // owned
    each = owned // members

    def spread_sums(local_grad, full_grad):
        width = full_grad.shape[2]
        rows = full_grad.astype(BF16).reshape(seqs, blocks, members, each, width)
        rows = jnp.transpose(rows, (2, 0, 1, 3, 4)).reshape(members, seqs * blocks * each, width)
        parts = [
            lax.dynamic_index_in_dim(rows, member ^ r, 0, keepdims=False) for r in range(members)
        ]
        total, beside_part, across_part = reduced(parts, half_reduced(parts))
        mine = total.astype(F32) + beside_part.astype(F32) + across_part.astype(F32)
        mine = mine.reshape(seqs, blocks * each * members, width // members)
        update = jnp.concatenate([local_grad, mine], 2)
        spread = jnp.zeros((adapters,) + update.shape[1:], F32)
        for s in range(seqs):
            here = jnp.arange(adapters, dtype=jnp.int32) == my_adapters[s]
            spread = spread + jnp.where(here[:, None, None], update[s][None], 0.0)
        return spread.astype(BF16).reshape(groups, owned, update.shape[2])

    def owned_sums(arrived, width):
        summed = jnp.sum(arrived.astype(F32), 0)
        mine = summed[:, width:].reshape(each, -1, d)
        return summed, jnp.transpose(mine, (1, 0, 2))

    sent_first = spread_sums(
        jnp.concatenate([local_heads, local_first], 2), after(full_heads, carried)
    )
    arrived_first = entered(sent_first)
    last_weights = halves_fc[1]
    counts = tuple(len(w) for w in last_weights)
    my_gain = lax.dynamic_slice_in_dim(gain_row, member * share, share, 1)
    def last_call(seq, first_tile, count, token, given):
        def rows_of(width):
            return pl.BlockSpec((big, width), lambda t, *_: (seq * big_tiles + first_tile + t, 0))

        def fixed(shape, first=0):
            return pl.BlockSpec(shape, lambda t, *_: (first,) + (0,) * (len(shape) - 1))

        def own(width):
            return pl.BlockSpec((big, width), lambda t, *_: (first_tile + t, 0))

        sum_block = pl.BlockSpec((8, big), lambda t, *_: (0, first_tile + t))
        own_map = pl.BlockSpec((RANK, cols), lambda t, meta, *_: (meta[1 + seqs + seq], 0))
        operands = (
            token,
            order,
            normed,
            branch,
            out_part,
            grad_part,
            mixes,
            backs,
            carried,
            local_maps,
            full_maps,
            bias_all[:, fh:],
            gain_row,
            bias_row,
            *[a for w in last_weights for a in w],
        )
        given = tuple(given)
        return pl.pallas_call(
            functools.partial(
                last_kernel, ff, counts, len(given) > 0
            ),
            out_shape=(shaped(SLOT, share),) * 8
            + (
                shaped(8, SLOT, dtype=F32),
                shaped(RANK, 2 * fl, dtype=F32),
                shaped(RANK, 2 * d, dtype=F32),
            ),
            grid_spec=pltpu.PrefetchScalarGridSpec(
                num_scalar_prefetch=2,
                grid=(count,),
                in_specs=[rows_of(d)] * 4
                + [rows_of(128)] * 3
                + [own_map, fixed((RANK, 4 * d), seq)]
                + [fixed((1, fl)), fixed((1, d)), fixed((1, d))]
                + [ANY] * (sum(counts) + 9 * (len(given) > 0))
                + [fixed((RANK, 2 * fl)), fixed((RANK, 2 * d))] * (len(given) > 0),
                out_specs=[own(share)] * 8
                + [sum_block, fixed((RANK, 2 * fl)), fixed((RANK, 2 * d))],
                scratch_shapes=[
                    pltpu.VMEM((d, fl), BF16),
                    pltpu.VMEM((fl, d), BF16),
                    pltpu.VMEM((big, fl), BF16),
                    pltpu.VMEM((big, fl), BF16),
                    pltpu.SemaphoreType.DMA((1 + fl // (d // slots), slots)),
                ],
            ),
            input_output_aliases={len(operands) + i: i for i in range(len(given))},
            compiler_params=limit,
            cost_estimate=cost(
                8 * count * big * d * fl, 10 * count * 2**20, count * big * fl
            ),
            name="last_half",
        )(*operands, *given)

    def out_call(seq, parts):
        return pl.pallas_call(
            functools.partial(out_kernel, seq),
            out_shape=shaped(groups, block, share),
            grid_spec=pltpu.PrefetchScalarGridSpec(
                num_scalar_prefetch=1,
                grid=(tiles,),
                in_specs=[piece_of(seq)] + [own_row] * 3 + [row_block],
                out_specs=back_block,
            ),
            compiler_params=limit,
            cost_estimate=cost(6 * SLOT * share, 10 * SLOT * share),
            name="output_rows",
        )(meta, rows_in[0], *parts, out_bias.astype(F32)[None, :])

    def grad_call(seq, parts, totals):
        return pl.pallas_call(
            functools.partial(grad_kernel, seq, d),
            out_shape=shaped(groups, block, share),
            grid_spec=pltpu.PrefetchScalarGridSpec(
                num_scalar_prefetch=1,
                grid=(tiles,),
                in_specs=[piece_of(seq)] * 2
                + [own_row] * 3
                + [
                    pl.BlockSpec((TILE, 128), lambda t, *_: (seq * tiles + t, 0)),
                    pl.BlockSpec((8, TILE), lambda t, *_: (0, t)),
                    row_block,
                ],
                out_specs=back_block,
            ),
            compiler_params=limit,
            cost_estimate=cost(10 * SLOT * share, 12 * SLOT * share),
            name="input_grad_rows",
        )(meta, rows_in[0], grads_in[0], *parts, stats, totals, my_gain)

    def piece_of(seq):
        return pl.BlockSpec((per_tile, 1, block, share), lambda t, *_: (t, seq, 0, 0))

    own_row = pl.BlockSpec((TILE, share), lambda t, *_: (t, 0))
    row_block = pl.BlockSpec((1, share), lambda t, *_: (0, 0))
    back_block = pl.BlockSpec((per_tile, block, share), lambda t, *_: (t, 0, 0))

    def near_sums(results, *waits):
        parts = [after(results[r], *waits) if r in (2, 6) else results[r] for r in range(8)]
        half_sums = results[8] + near(results[8])
        return parts, half_reduced(parts[0:4]), half_reduced(parts[4:8]), half_sums

    def far_sums(parts, half_out, half_grad, half_sums):
        return (
            reduced(parts[0:4], half_out),
            reduced(parts[4:8], half_grad),
            half_sums + far(half_sums),
        )

    back_outs = []
    back_grads = []
    local_last = []
    full_last = []
    waits = (arrived_first,)
    token = after(meta, sent_first)
    for seq in range(seqs):
        if seq == 0:
            results = last_call(seq, 0, big_tiles, token, ())
        else:
            results = last_call(seq, 0, big_tiles // 2, token, ())
            out_rows = out_call(seq - 1, after(out_parts, results[9]))
            results = last_call(
                seq, big_tiles // 2, big_tiles // 2, after(meta, out_rows), results
            )
            back_outs.append(entered(after(out_rows, *back_grads)))
        local_last.append(results[9])
        full_last.append(results[10])
        halves = near_sums(results, *waits)
        if seq > 0:
            grad_rows = grad_call(seq - 1, after(grad_parts, results[9]), row_totals)
            back_grads.append(entered(after(grad_rows, back_outs[-1])))
        out_parts, grad_parts, row_totals = far_sums(*halves)
        token = after(meta, *halves[1:])
        waits = (out_parts[2], grad_parts[2])
    sent_last = spread_sums(jnp.stack(local_last), after(jnp.stack(full_last), *halves[1:]))
    out_rows = out_call(seqs - 1, out_parts)
    merged = jnp.concatenate([out_rows, sent_last.reshape(groups, -1, share)], 1)
    merged = entered(after(merged, *back_grads))
    back_outs.append(merged)
    arrived_last = merged[:, block:].reshape(sent_last.shape)
    grad_rows = grad_call(seqs - 1, grad_parts, row_totals)
    back_grads.append(entered(after(grad_rows, merged)))
    output = move_rows(scatter_rows_kernel, permutation, back_outs, "scatter_rows")
    input_grad = move_rows(scatter_rows_kernel, permutation, back_grads, "scatter_rows")

    head_sums, head_full = owned_sums(arrived_first, 4 * share + 2 * fh)
    first_sums = head_sums[:, 4 * share :]
    last_sums, last_full = owned_sums(arrived_last, 2 * fl)
    return (
        output,
        input_grad,
        head_full[0],
        jnp.stack([head_sums[:, c * share : (c + 1) * share] for c in range(3)], 0),
        head_sums[:, dense_at : dense_at + share],
        head_full[1],
        last_full[0],
        jnp.concatenate([first_sums[:, 0:fh], last_sums[:, 0:fl]], 1),
        jnp.concatenate(
            [first_sums[:, fh : 2 * fh], last_sums[:, fl : 2 * fl]], 1
        ),
        last_full[1],
    )


def solution(mesh):
    return jax.shard_map(
        local,
        mesh=mesh,
        in_specs=(
            P(None, "dp", "mp"),
            P(None, "dp", "mp"),
            P(),
            P(),
            P(),
            P(),
            P(None, "dp", "mp"),
            P(None, "mp"),
            P("mp", "dp"),
            P("dp", "mp"),
            P("mp"),
            P("mp", "dp"),
            P("mp"),
            P(("dp", "mp"), None),
            P(None, "dp", "mp"),
            P("dp", "mp"),
            P(("dp", "mp"), None),
            P(("dp", "mp"), None),
            P("dp", "mp"),
            P("dp", "mp"),
            P(("dp", "mp"), None),
        ),
        out_specs=(
            P(None, "dp", "mp"),
            P(None, "dp", "mp"),
            P(("dp", "mp"), None),
            P(None, "dp", "mp"),
            P("dp", "mp"),
            P(("dp", "mp"), None),
            P(("dp", "mp"), None),
            P("dp", "mp"),
            P("dp", "mp"),
            P(("dp", "mp"), None),
        ),
        check_vma=False,
    )
```

```python
import functools

import jax
import jax.numpy as jnp
import numpy as np
from jax import lax
from jax.experimental import pallas as pl
from jax.experimental.pallas import tpu as pltpu
from jax.sharding import PartitionSpec as P

HD = 64
ROT = 32
RANK = 16
SLOT = 1024
EPSILON = 1e-05
MASKED = -1e30
BF16 = jnp.bfloat16
F32 = jnp.float32
ANY = pl.BlockSpec(memory_space=pl.ANY)
TILE = 256
BIG = 256
FIRST = 5
COST = 1.0


def after(value, *others):
    return lax.optimization_barrier((value,) + others)[0] if others else value


def mm(left, right):
    return jnp.dot(left, right, preferred_element_type=F32)


def mm_nt(left, right):
    return lax.dot_general(left, right, (((1,), (1,)), ((), ())), preferred_element_type=F32)


def mm_tn(left, right):
    return lax.dot_general(left, right, (((0,), (0,)), ((), ())), preferred_element_type=F32)


def rotary_tables():
    half = ROT // 2
    places = np.arange(SLOT, dtype=np.float32)
    frequency = np.float32(1.0) / np.float32(10000.0) ** (
        np.arange(half, dtype=np.float32) * np.float32(2.0) / np.float32(ROT)
    )
    phases = (places[:, None] * frequency[None, :]).astype(np.float32)
    cosine, sine = np.cos(phases), np.sin(phases)
    zero = np.zeros_like(sine)
    rest = np.zeros((SLOT, HD - ROT), np.float32)
    cos_head = np.concatenate([cosine, cosine, rest + 1.0], 1)
    up_head = np.concatenate([-sine, zero, rest], 1)
    down_head = np.concatenate([zero, sine, rest], 1)
    return tuple(
        jnp.asarray(np.concatenate([t, t], 1), F32) for t in (cos_head, up_head, down_head)
    )


def rotate(value, cos, up, down):
    return (
        value * cos
        + pltpu.roll(value, 128 - ROT // 2, axis=1) * up
        + pltpu.roll(value, ROT // 2, axis=1) * down
    )


def deal(lengths, adapter_index, groups, local_seqs):
    count = lengths.shape[0]
    pos = jnp.arange(count, dtype=jnp.int32)
    ranking = lengths * count + pos
    rank = jnp.sum((ranking[None, :] > ranking[:, None]).astype(jnp.int32), 1)
    round_num = rank // groups
    within = rank % groups
    target = jnp.where(round_num % 2 == 0, within, groups - 1 - within)
    place = target * local_seqs + round_num
    chosen = (place[None, :] == pos[:, None]).astype(jnp.int32)

    def pick(values):
        return jnp.sum(chosen * values[None, :], 1).astype(jnp.int32)

    return pick(pos), pick(lengths), pick(adapter_index)


def gather_rows_kernel(order, source, target, held, sem_in, sem_out):
    count = source.shape[0]
    fetch = [
        pltpu.make_async_copy(source.at[order[i]], held.at[i], sem_in.at[i]) for i in range(count)
    ]
    store = [pltpu.make_async_copy(held.at[i], target.at[i], sem_out.at[i]) for i in range(count)]
    for copy in fetch:
        copy.start()
    for i in range(count):
        fetch[i].wait()
        store[i].start()
    for copy in store:
        copy.wait()


def scatter_rows_kernel(order, *refs):
    seqs = len(refs) - 4
    sources, (target, held, sem_in, sem_out) = refs[:seqs], refs[seqs:]
    groups = sources[0].shape[0]
    fetch = []
    store = []
    for g in range(groups):
        for s in range(seqs):
            i = g * seqs + s
            source = sources[s].at[g, 0 : held.shape[1]]
            fetch.append(pltpu.make_async_copy(source, held.at[i], sem_in.at[i]))
            store.append(pltpu.make_async_copy(held.at[i], target.at[order[i]], sem_out.at[i]))
    for copy in fetch:
        copy.start()
    for take, put in zip(fetch, store, strict=True):
        take.wait()
        put.start()
    for copy in store:
        copy.wait()


def move_rows(kernel, order, arrays, name):
    count = sum(a.shape[0] for a in arrays)
    rest = arrays[0].shape[1:]
    size = sum(a.size for a in arrays)
    return pl.pallas_call(
        kernel,
        out_shape=jax.ShapeDtypeStruct((count,) + rest, BF16),
        grid_spec=pltpu.PrefetchScalarGridSpec(
            num_scalar_prefetch=1,
            grid=(1,),
            in_specs=[ANY] * len(arrays),
            out_specs=ANY,
            scratch_shapes=[
                pltpu.VMEM((count,) + rest, BF16),
                pltpu.SemaphoreType.DMA((count,)),
                pltpu.SemaphoreType.DMA((count,)),
            ],
        ),
        compiler_params=pltpu.CompilerParams(vmem_limit_bytes=16 * 1024 * 1024),
        cost_estimate=pl.CostEstimate(flops=0, transcendentals=0, bytes_accessed=int(4 * size * COST)),
        name=name,
    )(order, *arrays)


def weight_copies(kind, refs, order, target, sem, stacked):
    count = refs[0].shape[0] if stacked else len(refs)
    rows = target.shape[1 if kind in ("q", "lane") else 0]
    width = rows // count
    copies = []
    for s in range(count):
        source = refs[0].at[s] if stacked else refs[s]
        offset = s * width if stacked else pl.multiple_of(order[s] * width, width)
        if kind == "q":
            place = target.at[:, pl.ds(offset, width), :]
        elif kind == "row":
            place = target.at[pl.ds(offset, width), :]
        else:
            place = target.at[:, pl.ds(offset, width)]
        copies.append(pltpu.make_async_copy(source, place, sem.at[s]))
    return copies


def ring_copies(refs, order, sems, wq, wd):
    copies = []
    if len(refs[0].shape) > 2:
        for i, target in ((0, wq), (3, wd)):
            if target is not None:
                source = refs[min(i, 1)].at[0]
                copies.append(pltpu.make_async_copy(source, target, sems.at[i, 0]))
        return copies
    width = refs[0].shape[0] // 4
    for s, ref in enumerate(refs):
        place = pl.ds(pl.multiple_of(order[s] * width, width), width)
        for c in range(3):
            if wq is not None:
                source = ref.at[c * width : (c + 1) * width, :]
                copies.append(
                    pltpu.make_async_copy(source, wq.at[c, place, :], sems.at[c, s])
                )
        for i in range(ref.shape[1] // width):
            if wd is not None:
                lanes = slice(i * width, (i + 1) * width)
                source = ref.at[3 * width : 4 * width, lanes]
                copies.append(
                    pltpu.make_async_copy(source, wd.at[lanes, place], sems.at[3 + i, s])
                )
    return copies


def mlp_copies(first, second, order, w1, w2, sems):
    if second:
        copies = weight_copies("row", first, order, w1, sems[0], True)
        return copies + weight_copies("lane", second, order, w2, sems[1], True)
    packed = first[0]
    count = packed.shape[0]
    width = w1.shape[0] // count
    copies = []
    for s in range(count):
        lanes = pl.ds(s * width, width)
        copies.append(
            pltpu.make_async_copy(packed.at[s, 0:width, :], w1.at[lanes, :], sems[0].at[s])
        )
        for i in range(0, w2.shape[0], width):
            copies.append(
                pltpu.make_async_copy(
                    packed.at[s, width : 2 * width, i : i + width],
                    w2.at[i : i + width, lanes],
                    sems[1 + i // width].at[s],
                )
            )
    return copies


def first_step():
    return (pl.program_id(0) == 0) & (pl.program_id(1) == 0)


def norm_kernel(meta, a0, a1, a2, a3, gain, bias, normed, stats, row):
    member = meta[0]
    share = a0.shape[-1]
    for r, ref in enumerate((a0, a1, a2, a3)):
        offset = pl.multiple_of((member ^ r) * share, share)
        row[:, pl.ds(offset, share)] = ref[:, 0].reshape(row.shape[0], share).astype(F32)
    value = row[...]
    mean = jnp.mean(value, -1, keepdims=True)
    centred = value - mean
    scale = lax.rsqrt(jnp.mean(centred * centred, -1, keepdims=True) + EPSILON)
    normed[...] = (centred * scale * gain[...] + bias[...]).astype(BF16)
    lane = lax.broadcasted_iota(jnp.int32, stats.shape, 1)
    stats[...] = jnp.where(lane == 0, mean, scale)


def qkv_kernel(
    count, meta, order, normed, local_maps, full_maps, bias, cos, up, down, *rest
):
    weights, rest = rest[:count], rest[count:]
    queries, keys, values, mixes, w, sem = rest

    @pl.when(first_step())
    def _():
        run_copies(ring_copies(weights, order, sem, w, None))

    x = normed[...]
    d = x.shape[1]
    share = queries.shape[1]
    maps = jnp.concatenate([full_maps[:, 0:d], full_maps[:, d : 2 * d]], 0)
    mix = mm_nt(x, maps)
    mixes[:, : 2 * RANK] = mix
    mix_low = mix[:, :RANK].astype(BF16)
    for c, out in enumerate((queries, keys, values)):
        value = mm(x, w[c]) + bias[c : c + 1, :] + mm(
            mix_low, local_maps[:, c * share : (c + 1) * share]
        )
        if c == 2:
            out[...] = value.astype(BF16)
        else:
            for j in range(share // 128):
                part = value[:, j * 128 : (j + 1) * 128]
                out[:, j * 128 : (j + 1) * 128] = rotate(
                    part, cos[...], up[...], down[...]
                ).astype(BF16)


def branch_kernel(
    count, places, meta, order, a0, a1, a2, a3, local_maps, full_maps, token, *rest
):
    weights, rest = rest[:count], rest[count:]
    branch, attn_grad, backs, row, w, sem = rest

    @pl.when(first_step())
    def _():
        run_copies(ring_copies(weights, order, sem, None, w))

    member = meta[0]
    length = meta[1 + pl.program_id(0)]
    share = a0.shape[-1]
    d = row.shape[1]
    dense_at = places
    for r, ref in enumerate((a0, a1, a2, a3)):
        offset = pl.multiple_of((member ^ r) * share, share)
        row[:, pl.ds(offset, share)] = ref[:, 0].reshape(row.shape[0], share)
    slot = pl.program_id(1) * row.shape[0] + lax.broadcasted_iota(jnp.int32, (row.shape[0], 1), 0)
    keep = (slot < length).astype(F32)
    value = (row[...].astype(F32) * keep).astype(BF16)
    branch[...] = value
    maps = jnp.concatenate([full_maps[:, 2 * d : 3 * d], full_maps[:, 3 * d : 4 * d]], 0)
    back = mm_nt(value, maps)
    backs[:, : 2 * RANK] = back
    attn_grad[...] = (
        mm_nt(value, w[...])
        + mm(back[:, :RANK].astype(BF16), local_maps[:, dense_at : dense_at + share])
    ).astype(BF16)


def attention_kernel(
    meta,
    queries,
    keys,
    values,
    out_grad,
    cos,
    up,
    down,
    attended,
    dq,
    dk,
    dv,
    dk_sum,
    dv_sum,
    outside,
):
    length = meta[1 + pl.program_id(0)]
    rows = 512
    heads = 128 // HD

    @pl.when(pl.program_id(1) == 0)
    def _():
        place = lax.broadcasted_iota(jnp.int32, outside.shape, 0)
        outside[...] = jnp.where(place < length, 0.0, MASKED)

    zero = jnp.zeros((), BF16)
    head_of = lax.broadcasted_iota(jnp.int32, (SLOT, 128), 1) // HD
    own_keys = [jnp.where(head_of == h, keys[...], zero) for h in range(heads)]
    own_values = [jnp.where(head_of == h, values[...], zero) for h in range(heads)]
    below = lax.broadcasted_iota(jnp.int32, (rows, rows), 0) <= lax.broadcasted_iota(
        jnp.int32, (rows, rows), 1
    )
    dk_sum[...] = jnp.zeros_like(dk_sum)
    dv_sum[...] = jnp.zeros_like(dv_sum)
    for at in range(0, SLOT, rows):
        n = at + rows
        all_q = queries[at:n, :] * jnp.asarray(0.125, BF16)
        all_g = out_grad[at:n, :]
        out = jnp.zeros((128, rows), F32)
        dq_sum = jnp.zeros((128, rows), F32)
        for h in range(heads):
            q = jnp.where(head_of[:rows] == h, all_q, zero)
            g = jnp.where(head_of[:rows] == h, all_g, zero)
            score = mm_nt(keys[0:n, :], q)
            score = score + jnp.concatenate([outside[0:n, :]] * (rows // 128), 1)
            corner = jnp.where(below, score[at:n], MASKED)
            score = jnp.concatenate([score[0:at], corner], 0) if at else corner
            weight = jnp.exp(score - jnp.max(score, 0, keepdims=True))
            probs = weight * (1.0 / jnp.sum(weight, 0, keepdims=True))
            low = probs.astype(BF16)
            prob_grad = mm_nt(values[0:n, :], g)
            inner = jnp.sum(probs * prob_grad, 0, keepdims=True)
            score_grad = (probs * (prob_grad - inner)).astype(BF16)
            out += mm_tn(own_values[h][0:n], low)
            dq_sum += mm_tn(own_keys[h][0:n], score_grad)
            dk_sum[0:n, :] += mm(score_grad, q)
            dv_sum[0:n, :] += mm(low, g)
        attended[at:n, :] = jnp.transpose(out).astype(BF16)
        dq[at:n, :] = rotate(
            jnp.transpose(dq_sum) * 0.125, cos[at:n, :], -up[at:n, :], -down[at:n, :]
        ).astype(BF16)
    dk[...] = rotate(dk_sum[...], cos[...], -up[...], -down[...]).astype(BF16)
    dv[...] = dv_sum[...].astype(BF16)


def mlp_half(
    x, b, mix_fc1, back_fc2, w1, w2, up_maps, down_maps, fc1_bias, active, hidden_grad, grads
):
    step = 512
    for at in range(0, w1.shape[1], step):
        lanes = slice(at, min(at + step, w1.shape[1]))
        v = mm(x[...], w1[:, lanes]) + fc1_bias[:, lanes] + mm(mix_fc1, up_maps[:, lanes])
        square = v * v
        t = jnp.tanh(0.7978845608028654 * (v + 0.044715 * v * square))
        half = 0.5 * (1.0 + t)
        slope = half + (0.5 * 0.7978845608028654) * v * (1.0 - t * t) * (
            1.0 + (3.0 * 0.044715) * square
        )
        active[:, lanes] = (v * half).astype(BF16)
        pull = mm_nt(b[...], w2[lanes, :]) + mm(back_fc2, down_maps[:, lanes])
        hidden_grad[:, lanes] = (pull * slope).astype(BF16)
    grads[0][...] += mm_tn(mix_fc1, hidden_grad[...])
    grads[1][...] += mm_tn(back_fc2, active[...])
    return mm_nt(active[...], down_maps), mm_nt(hidden_grad[...], up_maps)


def run_copies(copies):
    for c in copies:
        c.start()
    for c in copies:
        c.wait()


def split_refs(rest, counts):
    refs = []
    for count in counts:
        refs.append(rest[:count])
        rest = rest[count:]
    return refs, rest


def heads_kernel(
    meta, order, normed, branch, attended, dq, dk, dv, mixes, backs, local_maps, *rest
):
    refs, rest = rest[:-8], rest[-8:]
    out_sum, grad_sum, carried, grad_local, grad_full, wq, wd, sem = rest

    @pl.when(first_step())
    def _():
        run_copies(ring_copies(refs, order, sem, wq, wd))

    @pl.when(pl.program_id(1) == 0)
    def _():
        grad_local[...] = jnp.zeros_like(grad_local)
        grad_full[...] = jnp.zeros_like(grad_full)

    d = normed.shape[1]
    share = attended.shape[1]
    dense_at = 3 * share
    fc1_at = dense_at + share
    att = attended[...]
    mix_qkv = mixes[:, :RANK].astype(BF16)
    back_dense = backs[:, :RANK].astype(BF16)
    mix_dense = mm_nt(att, local_maps[:, dense_at:fc1_at])
    grad_local[0, :, dense_at:fc1_at] += mm_tn(back_dense, att)
    grad_full[0, :, d : 2 * d] += mm_tn(mix_dense.astype(BF16), branch[...])
    back_qkv = jnp.zeros(mix_dense.shape, F32)
    for c, part in enumerate((dq, dk, dv)):
        lanes = slice(c * share, (c + 1) * share)
        back_qkv += mm_nt(part[...], local_maps[:, lanes])
        grad_local[0, :, lanes] += mm_tn(mix_qkv, part[...])
    grad_full[0, :, 0:d] += mm_tn(back_qkv.astype(BF16), normed[...])
    for at in range(0, d, 512):
        lanes = slice(at, at + 512)
        out_sum[:, lanes] = mm(att, wd[:, lanes]).astype(BF16)
        total = mm_nt(dq[...], wq[0, lanes, :])
        for c, part in ((1, dk), (2, dv)):
            total += mm_nt(part[...], wq[c, lanes, :])
        grad_sum[:, lanes] = total.astype(BF16)
    carried[:, 0:RANK] = mix_dense
    carried[:, 2 * RANK : 3 * RANK] = back_qkv


def first_kernel(
    ff,
    counts,
    meta,
    order,
    normed,
    branch,
    out_part,
    grad_part,
    mixes,
    backs,
    heads,
    local_maps,
    fc1_bias,
    *rest,
):
    refs, rest = split_refs(rest, counts)
    out_sum, grad_sum, carried, grad_local = rest[0:4]
    w1, w2, active, hidden_grad, fc_sem = rest[4:]

    @pl.when(first_step())
    def _():
        sems = [fc_sem.at[i] for i in range(fc_sem.shape[0])]
        run_copies(mlp_copies(refs[0], refs[1], order, w1, w2, sems))

    @pl.when(pl.program_id(1) == 0)
    def _():
        grad_local[...] = jnp.zeros_like(grad_local)

    d = normed.shape[1]
    fh = w1.shape[1]
    fc1_at = d
    fc2_at = fc1_at + ff
    mix_fc2, back_fc1 = mlp_half(
        normed,
        branch,
        mixes[:, RANK : 2 * RANK].astype(BF16),
        backs[:, RANK : 2 * RANK].astype(BF16),
        w1,
        w2,
        local_maps[:, fc1_at : fc1_at + fh],
        local_maps[:, fc2_at : fc2_at + fh],
        fc1_bias,
        active,
        hidden_grad,
        (grad_local.at[0, :, 0:fh], grad_local.at[0, :, fh : 2 * fh]),
    )
    for at in range(0, d, 512):
        lanes = slice(at, at + 512)
        total = out_part[:, lanes].astype(F32) + mm(active[...], w2[:, lanes])
        out_sum[:, lanes] = total.astype(BF16)
        total = grad_part[:, lanes].astype(F32) + mm_nt(hidden_grad[...], w1[lanes, :])
        grad_sum[:, lanes] = total.astype(BF16)
    carried[:, 0:RANK] = heads[:, 0:RANK]
    carried[:, RANK : 2 * RANK] = mix_fc2
    carried[:, 2 * RANK : 3 * RANK] = heads[:, 2 * RANK : 3 * RANK]
    carried[:, 3 * RANK : 4 * RANK] = back_fc1


def last_kernel(
    ff,
    counts,
    resumed,
    meta,
    order,
    normed,
    branch,
    out_part,
    grad_part,
    mixes,
    backs,
    carried,
    local_maps,
    full_maps,
    fc1_bias,
    gain,
    ln_bias,
    *rest,
):
    refs, rest = split_refs(rest, counts)
    if resumed:
        local_before, full_before = rest[9:11]
        rest = rest[11:]
    outs, grads = rest[0:4], rest[4:8]
    row_sums, grad_local, grad_full = rest[8:11]
    w1, w2, active, hidden_grad, sem = rest[11:]

    @pl.when(pl.program_id(0) == 0)
    def _():
        sems = [sem.at[i] for i in range(sem.shape[0])]
        run_copies(mlp_copies(refs[0], refs[1], order, w1, w2, sems))
        if resumed:
            grad_local[...] = local_before[...]
            grad_full[...] = full_before[...]
        else:
            grad_local[...] = jnp.zeros_like(grad_local)
            grad_full[...] = jnp.zeros_like(grad_full)

    member = meta[0]
    d = normed.shape[1]
    fh = w1.shape[1]
    fc1_at = d
    fc2_at = fc1_at + ff
    start = ff - fh
    mix_fc1 = mixes[:, RANK : 2 * RANK].astype(BF16)
    back_fc2 = backs[:, RANK : 2 * RANK].astype(BF16)
    mix_fc2, back_fc1 = mlp_half(
        normed,
        branch,
        mix_fc1,
        back_fc2,
        w1,
        w2,
        local_maps[:, fc1_at + start : fc1_at + ff],
        local_maps[:, fc2_at + start : fc2_at + ff],
        fc1_bias,
        active,
        hidden_grad,
        (grad_local.at[:, 0:fh], grad_local.at[:, fh : 2 * fh]),
    )
    mix_fc2 = (mix_fc2 + carried[:, RANK : 2 * RANK]).astype(BF16)
    back_fc1 = (back_fc1 + carried[:, 3 * RANK : 4 * RANK]).astype(BF16)
    grad_full[:, d : 2 * d] += mm_tn(mix_fc2, branch[...])
    grad_full[:, 0:d] += mm_tn(back_fc1, normed[...])
    out_mix = jnp.concatenate([carried[:, 0:RANK].astype(BF16), mix_fc2], 1)
    in_mix = jnp.concatenate([carried[:, 2 * RANK : 3 * RANK].astype(BF16), back_fc1], 1)
    rows = normed.shape[0]
    first = jnp.zeros((rows, 1), F32)
    second = jnp.zeros((rows, 1), F32)
    width = d // 4
    for r in range(4):
        offset = pl.multiple_of((member ^ r) * width, width)
        lanes = pl.ds(offset, width)

        def maps(i, offset=offset):
            return full_maps[:, pl.ds(pl.multiple_of(i * d + offset, width), width)]

        out = out_part[:, lanes].astype(F32) + mm(active[...], w2[:, lanes])
        out += mm(out_mix, jnp.concatenate([maps(2), maps(3)], 0))
        outs[r][...] = out.astype(BF16)
        total = grad_part[:, lanes].astype(F32) + mm_nt(hidden_grad[...], w1[lanes, :])
        total += mm(in_mix, jnp.concatenate([maps(0), maps(1)], 0))
        grads[r][...] = total.astype(BF16)
        first += jnp.sum(total * gain[:, lanes], -1, keepdims=True)
        second += jnp.sum(
            total * (normed[:, lanes].astype(F32) - ln_bias[:, lanes]), -1, keepdims=True
        )
    lane = lax.broadcasted_iota(jnp.int32, (rows, 128), 1)
    row_sums[...] = jnp.transpose(jnp.where(lane == 0, first, second))[0:8, :]


def kept_rows(length, rows):
    slot = pl.program_id(0) * rows + lax.broadcasted_iota(jnp.int32, (rows, 1), 0)
    return (slot < length).astype(F32)


def out_kernel(seq, meta, x, part, first, second, bias, out):
    rows, share = part.shape
    total = part[...].astype(F32) + first[...].astype(F32) + second[...].astype(F32)
    value = x[:, 0].reshape(rows, share).astype(F32) + total + bias[...]
    value = value * kept_rows(meta[1 + seq], rows)
    out[...] = value.astype(BF16).reshape(out.shape)


def grad_kernel(seq, d, meta, x, cot, part, first, second, stats, row_sums, gain, out):
    rows, share = part.shape
    total = part[...].astype(F32) + first[...].astype(F32) + second[...].astype(F32)
    mean, scale = stats[:, 0:1], stats[:, 1:2]
    unit = (x[:, 0].reshape(rows, share).astype(F32) - mean) * scale
    sums = jnp.transpose(
        jnp.concatenate([row_sums[...], jnp.zeros((120, rows), F32)], 0)
    ) * (1.0 / d)
    value = scale * (total * gain[...] - sums[:, 0:1] - unit * sums[:, 1:2])
    value += kept_rows(meta[1 + seq], rows) * cot[:, 0].reshape(rows, share).astype(F32)
    out[...] = value.astype(BF16).reshape(out.shape)


def local(
    tokens,
    cotangent,
    lengths,
    adapter_index,
    ln_gain,
    ln_bias,
    w_qkv,
    qkv_bias,
    w_dense,
    w_fc1,
    fc1_bias,
    w_fc2,
    out_bias,
    qkv_down,
    qkv_up,
    dense_down,
    dense_up,
    fc1_down,
    fc1_up,
    fc2_down,
    fc2_up,
):
    groups = lax.axis_size("dp")
    members = lax.axis_size("mp")
    group = lax.axis_index("dp")
    member = lax.axis_index("mp")
    seqs = tokens.shape[0] // groups
    block, share = tokens.shape[1], tokens.shape[2]
    d = share * members
    ff = w_fc1.shape[1]
    tiles = SLOT // TILE
    per_tile = TILE // block
    count_rows = seqs * SLOT
    permutation, dealt_lengths, dealt_adapters = deal(lengths, adapter_index, groups, seqs)
    my_lengths = lax.dynamic_slice_in_dim(dealt_lengths, group * seqs, seqs)
    my_adapters = lax.dynamic_slice_in_dim(dealt_adapters, group * seqs, seqs)
    meta = jnp.concatenate([member[None].astype(jnp.int32), my_lengths, my_adapters])

    def near(value):
        return lax.ppermute(value, "mp", [(i, i ^ 1) for i in range(members)])

    def far(value):
        return lax.ppermute(value, "mp", [(i, i ^ 2) for i in range(members)])

    def hop(value):
        return near(value[0:8])

    def dealt(values):
        return move_rows(gather_rows_kernel, permutation, (values,), "gather_rows")

    def entered(values):
        return lax.all_to_all(values, "dp", split_axis=0, concat_axis=0, tiled=True)

    def widened(mine, across):
        shape = (groups, seqs, block, share)
        return tuple(a.reshape(shape) for a in (mine, near(mine), across, near(across)))

    dealt_tokens = dealt(tokens)
    my_tokens = entered(dealt_tokens)
    far_tokens = far(my_tokens)

    wide = (d // groups) % 128 == 0
    inner = 2
    outer = groups // inner
    place_out, place_in = group // inner, group % inner

    def gathered(weight, axis):
        if wide:
            return (lax.all_gather(weight, "dp", axis=0, tiled=False),)
        return (lax.all_gather(weight, "dp", axis=axis, tiled=True)[None],)

    def beside(value):
        return lax.ppermute(value, "dp", [(i, i ^ 1) for i in range(groups)])

    def onward(value):
        return lax.ppermute(value, "dp", [(i, (i + inner) % groups) for i in range(groups)])

    def ring(weight, *waits):
        held = [weight]
        crossed = []
        for k in range(outer - 1):
            step = after(held[k], *waits, *crossed[-1:])
            crossed.append(beside(held[k]))
            held.append(onward(step))
            waits = ()
        done = tuple(held) + tuple(crossed)
        crossed.append(beside(held[-1]))
        return tuple(a for pair in zip(held, crossed, strict=True) for a in pair), done

    pieces = share // w_dense.shape[1]
    ring_sems = pltpu.SemaphoreType.DMA((3 + pieces, groups))
    order = jnp.stack(
        [
            (place_out - k) % outer * inner + (place_in + j) % inner
            for k in range(outer)
            for j in range(inner)
        ]
    ).astype(jnp.int32)
    if wide:
        rows = [w_dense[i * w_dense.shape[1] : (i + 1) * w_dense.shape[1]] for i in range(pieces)]
        packed = jnp.concatenate([w_qkv.reshape(-1, share), jnp.concatenate(rows, 1)], 0)
        ring_slots, ring_early = ring(packed, my_tokens)
    else:
        ring_slots, ring_early = gathered(w_qkv, 1) + gathered(w_dense, 1), ()
    rows_in = widened(my_tokens, after(far_tokens, *ring_early))
    cos, up, down = rotary_tables()
    gain_row = ln_gain[None, :]
    bias_row = ln_bias[None, :]

    piece = pl.BlockSpec((per_tile, 1, block, share), lambda s, t, *_: (t, s, 0, 0))
    wide_row = pl.BlockSpec((TILE, d), lambda s, t, *_: (s * tiles + t, 0))
    share_row = pl.BlockSpec((TILE, share), lambda s, t, *_: (s * tiles + t, 0))
    stat_row = pl.BlockSpec((TILE, 128), lambda s, t, *_: (s * tiles + t, 0))
    table_row = pl.BlockSpec((TILE, 128), lambda s, t, *_: (t, 0))
    cols = 4 * share + 2 * ff
    local_map = pl.BlockSpec((RANK, cols), lambda s, t, meta, *_: (meta[1 + seqs + s], 0))
    full_map = pl.BlockSpec((RANK, 4 * d), lambda s, t, *_: (s, 0))

    def whole(shape):
        return pl.BlockSpec(shape, lambda s, t, *_: tuple(0 for _ in shape))

    def shaped(*shape, dtype=BF16):
        return jax.ShapeDtypeStruct(shape, dtype)

    def cost(flops, nbytes, exps=0):
        return pl.CostEstimate(
            flops=int(flops * COST), transcendentals=int(exps * COST), bytes_accessed=int(nbytes * COST)
        )

    limit = pltpu.CompilerParams(vmem_limit_bytes=58 * 1024 * 1024)

    normed, stats = pl.pallas_call(
        norm_kernel,
        out_shape=(shaped(count_rows, d), shaped(count_rows, 128, dtype=F32)),
        grid_spec=pltpu.PrefetchScalarGridSpec(
            num_scalar_prefetch=1,
            grid=(seqs, tiles),
            in_specs=[piece] * 4 + [whole((1, d))] * 2,
            out_specs=[wide_row, stat_row],
            scratch_shapes=[pltpu.VMEM((TILE, d), F32)],
        ),
        compiler_params=limit,
        cost_estimate=cost(10 * count_rows * d, 4 * count_rows * d),
        name="norm_rows",
    )(meta, *rows_in, gain_row, bias_row)

    my_cotangent = entered(after(dealt(cotangent), *ring_early, *rows_in))
    fh = ff * FIRST // 8
    fl = ff - fh
    local_part = jnp.concatenate(
        [qkv_up[0], qkv_up[1], qkv_up[2], dense_down, fc1_up, fc2_down], 1
    ).astype(BF16)
    cols = local_part.shape[1]
    full_rows = qkv_down.shape[0]
    full_part = jnp.stack([qkv_down, fc1_down, dense_up, fc2_up], 1).astype(BF16)
    full_part = after(full_part, dealt_tokens)
    full_part = jnp.transpose(full_part.reshape(full_rows, 4, members, share), (2, 0, 1, 3))
    full_part = lax.all_to_all(
        full_part.reshape(members, full_rows, 4 * share),
        "mp",
        split_axis=0,
        concat_axis=0,
        tiled=True,
    )
    all_part = jnp.concatenate(
        [local_part, full_part.reshape(members * full_rows, 4 * share)], 1
    )
    all_part = after(all_part, my_tokens)
    local_maps = lax.all_gather(all_part, "dp", axis=0, tiled=True)
    my_maps = jnp.stack(
        [
            lax.dynamic_slice(
                local_maps, (my_adapters[s] * RANK, cols), (RANK, 4 * share)
            )
            for s in range(seqs)
        ]
    ).reshape(seqs * RANK, 4, share)
    full_maps = jnp.transpose(lax.all_gather(my_maps, "mp", axis=0, tiled=False), (1, 2, 0, 3))
    full_maps = full_maps.reshape(seqs * RANK, 4 * d)
    w_fc1, w_fc2 = after(w_fc1, my_cotangent), after(w_fc2, my_cotangent)
    my_cotangent = after(my_cotangent, full_maps)
    far_cotangent = far(my_cotangent)

    def mlp_weights(j):
        start, stop = (0, fh) if j == 0 else (fh, ff)
        first, second = w_fc1[:, start:stop], w_fc2[start:stop, :]
        if not wide:
            return gathered(first, 0), gathered(second, 1)
        width = second.shape[1]
        parts = [second[i : i + width] for i in range(0, stop - start, width)]
        packed = jnp.concatenate([first, jnp.concatenate(parts, 1)], 0)
        return (lax.all_gather(packed, "dp", axis=0, tiled=False),), ()

    halves_fc = [mlp_weights(j) for j in range(2)]
    slots = groups
    dense_at = 3 * share

    queries, keys, values, mixes = pl.pallas_call(
        functools.partial(qkv_kernel, len(ring_slots)),
        out_shape=(
            shaped(count_rows, share),
            shaped(count_rows, share),
            shaped(count_rows, share),
            shaped(count_rows, 128, dtype=F32),
        ),
        grid_spec=pltpu.PrefetchScalarGridSpec(
            num_scalar_prefetch=2,
            grid=(seqs, tiles),
            in_specs=[wide_row, local_map, full_map, whole((3, share))]
            + [table_row] * 3
            + [ANY] * len(ring_slots),
            out_specs=[share_row, share_row, share_row, stat_row],
            scratch_shapes=[
                pltpu.VMEM((3, d, share), BF16),
                ring_sems,
            ],
        ),
        compiler_params=limit,
        cost_estimate=cost(6 * count_rows * d * share, 16 * 2**20),
        name="project_rows",
    )(meta, order, normed, local_maps, full_maps, qkv_bias.astype(F32), cos, up, down, *ring_slots)

    projected = hop(mixes)
    grads_in = widened(my_cotangent, after(far_cotangent, projected))
    branch, attn_grad, backs = pl.pallas_call(
        functools.partial(branch_kernel, len(ring_slots), dense_at),
        out_shape=(
            shaped(count_rows, d),
            shaped(count_rows, share),
            shaped(count_rows, 128, dtype=F32),
        ),
        grid_spec=pltpu.PrefetchScalarGridSpec(
            num_scalar_prefetch=2,
            grid=(seqs, tiles),
            in_specs=[piece] * 4 + [local_map, full_map] + [ANY] * (1 + len(ring_slots)),
            out_specs=[wide_row, share_row, stat_row],
            scratch_shapes=[
                pltpu.VMEM((TILE, d), BF16),
                pltpu.VMEM((share, d), BF16),
                ring_sems,
            ],
        ),
        compiler_params=limit,
        cost_estimate=cost(2 * count_rows * d * share, 20 * 2**20),
        name="branch_rows",
    )(meta, order, *grads_in, local_maps, full_maps, projected, *ring_slots)

    pair = pl.BlockSpec((SLOT, 128), lambda s, h, *_: (s, h))
    attended, dq, dk, dv = pl.pallas_call(
        attention_kernel,
        out_shape=(shaped(count_rows, share),) * 4,
        grid_spec=pltpu.PrefetchScalarGridSpec(
            num_scalar_prefetch=1,
            grid=(seqs, share // 128),
            in_specs=[pair] * 4 + [whole((SLOT, 128))] * 3,
            out_specs=[pair] * 4,
            scratch_shapes=[
                pltpu.VMEM((SLOT, 128), F32),
                pltpu.VMEM((SLOT, 128), F32),
                pltpu.VMEM((SLOT, 128), F32),
            ],
        ),
        compiler_params=limit,
        cost_estimate=cost(
            6 * 4 * count_rows * SLOT * share, 16 * 2**20, count_rows * SLOT * share // HD
        ),
        name="attend_rows",
    )(meta, queries, keys, values, attn_grad, cos, up, down)

    big = BIG
    big_tiles = SLOT // big

    def big_row(width):
        return pl.BlockSpec((big, width), lambda s, t, *_: (s * big_tiles + t, 0))

    def per_seq(*shape):
        return pl.BlockSpec((1,) + shape, lambda s, t, *_: (s,) + tuple(0 for _ in shape))

    bias_all = fc1_bias.astype(F32)[None, :]
    out_heads, grad_heads, heads, local_heads, full_heads = pl.pallas_call(
        heads_kernel,
        out_shape=(
            shaped(count_rows, d),
            shaped(count_rows, d),
            shaped(count_rows, 128, dtype=F32),
            shaped(seqs, RANK, 4 * share, dtype=F32),
            shaped(seqs, RANK, 2 * d, dtype=F32),
        ),
        grid_spec=pltpu.PrefetchScalarGridSpec(
            num_scalar_prefetch=2,
            grid=(seqs, big_tiles),
            in_specs=[big_row(d)] * 2
            + [big_row(share)] * 4
            + [big_row(128)] * 2
            + [local_map]
            + [ANY] * len(ring_slots),
            out_specs=[
                big_row(d),
                big_row(d),
                big_row(128),
                per_seq(RANK, 4 * share),
                per_seq(RANK, 2 * d),
            ],
            scratch_shapes=[
                pltpu.VMEM((3, d, share), BF16),
                pltpu.VMEM((share, d), BF16),
                ring_sems,
            ],
        ),
        compiler_params=limit,
        cost_estimate=cost(8 * count_rows * d * share, 48 * 2**20),
        name="head_sums",
    )(meta, order, normed, branch, attended, dq, dk, dv, mixes, backs, local_maps, *ring_slots)

    first_weights = halves_fc[0]
    counts = tuple(len(w) for w in first_weights)
    out_part, grad_part, carried, local_first = pl.pallas_call(
        functools.partial(first_kernel, ff, counts),
        out_shape=(
            shaped(count_rows, d),
            shaped(count_rows, d),
            shaped(count_rows, 128, dtype=F32),
            shaped(seqs, RANK, 2 * fh, dtype=F32),
        ),
        grid_spec=pltpu.PrefetchScalarGridSpec(
            num_scalar_prefetch=2,
            grid=(seqs, big_tiles),
            in_specs=[big_row(d)] * 4
            + [big_row(128)] * 3
            + [local_map, whole((1, fh))]
            + [ANY] * sum(counts),
            out_specs=[big_row(d), big_row(d), big_row(128), per_seq(RANK, 2 * fh)],
            scratch_shapes=[
                pltpu.VMEM((d, fh), BF16),
                pltpu.VMEM((fh, d), BF16),
                pltpu.VMEM((big, fh), BF16),
                pltpu.VMEM((big, fh), BF16),
                pltpu.SemaphoreType.DMA((1 + fh // (d // slots), slots)),
            ],
        ),
        compiler_params=limit,
        cost_estimate=cost(8 * count_rows * d * fh, 60 * 2**20, count_rows * fh),
        name="first_half",
    )(
        meta,
        order,
        normed,
        branch,
        out_heads,
        grad_heads,
        mixes,
        backs,
        heads,
        local_maps,
        bias_all[:, :fh],
        *[a for w in first_weights for a in w],
    )

    def add_low(left, right):
        return (left.astype(F32) + right.astype(F32)).astype(BF16)

    def half_reduced(parts):
        return add_low(parts[2], near(parts[3]))

    def reduced(parts, half):
        return parts[0], near(parts[1]), far(half)

    adapters = qkv_down.shape[0] * groups * members // RANK
    owned = adapters * RANK // groups

    blocks = RANK // owned
    each = owned // members

    def spread_sums(local_grad, full_grad):
        width = full_grad.shape[2]
        rows = full_grad.astype(BF16).reshape(seqs, blocks, members, each, width)
        rows = jnp.transpose(rows, (2, 0, 1, 3, 4)).reshape(members, seqs * blocks * each, width)
        parts = [
            lax.dynamic_index_in_dim(rows, member ^ r, 0, keepdims=False) for r in range(members)
        ]
        total, beside_part, across_part = reduced(parts, half_reduced(parts))
        mine = total.astype(F32) + beside_part.astype(F32) + across_part.astype(F32)
        mine = mine.reshape(seqs, blocks * each * members, width // members)
        update = jnp.concatenate([local_grad, mine], 2)
        spread = jnp.zeros((adapters,) + update.shape[1:], F32)
        for s in range(seqs):
            here = jnp.arange(adapters, dtype=jnp.int32) == my_adapters[s]
            spread = spread + jnp.where(here[:, None, None], update[s][None], 0.0)
        return spread.astype(BF16).reshape(groups, owned, update.shape[2])

    def owned_sums(arrived, width):
        summed = jnp.sum(arrived.astype(F32), 0)
        mine = summed[:, width:].reshape(each, -1, d)
        return summed, jnp.transpose(mine, (1, 0, 2))

    sent_first = spread_sums(
        jnp.concatenate([local_heads, local_first], 2), after(full_heads, carried)
    )
    arrived_first = entered(sent_first)
    last_weights = halves_fc[1]
    counts = tuple(len(w) for w in last_weights)
    my_gain = lax.dynamic_slice_in_dim(gain_row, member * share, share, 1)
    def last_call(seq, first_tile, count, token, given):
        def rows_of(width):
            return pl.BlockSpec((big, width), lambda t, *_: (seq * big_tiles + first_tile + t, 0))

        def fixed(shape, first=0):
            return pl.BlockSpec(shape, lambda t, *_: (first,) + (0,) * (len(shape) - 1))

        def own(width):
            return pl.BlockSpec((big, width), lambda t, *_: (first_tile + t, 0))

        sum_block = pl.BlockSpec((8, big), lambda t, *_: (0, first_tile + t))
        own_map = pl.BlockSpec((RANK, cols), lambda t, meta, *_: (meta[1 + seqs + seq], 0))
        operands = (
            token,
            order,
            normed,
            branch,
            out_part,
            grad_part,
            mixes,
            backs,
            carried,
            local_maps,
            full_maps,
            bias_all[:, fh:],
            gain_row,
            bias_row,
            *[a for w in last_weights for a in w],
        )
        given = tuple(given)
        return pl.pallas_call(
            functools.partial(
                last_kernel, ff, counts, len(given) > 0
            ),
            out_shape=(shaped(SLOT, share),) * 8
            + (
                shaped(8, SLOT, dtype=F32),
                shaped(RANK, 2 * fl, dtype=F32),
                shaped(RANK, 2 * d, dtype=F32),
            ),
            grid_spec=pltpu.PrefetchScalarGridSpec(
                num_scalar_prefetch=2,
                grid=(count,),
                in_specs=[rows_of(d)] * 4
                + [rows_of(128)] * 3
                + [own_map, fixed((RANK, 4 * d), seq)]
                + [fixed((1, fl)), fixed((1, d)), fixed((1, d))]
                + [ANY] * (sum(counts) + 9 * (len(given) > 0))
                + [fixed((RANK, 2 * fl)), fixed((RANK, 2 * d))] * (len(given) > 0),
                out_specs=[own(share)] * 8
                + [sum_block, fixed((RANK, 2 * fl)), fixed((RANK, 2 * d))],
                scratch_shapes=[
                    pltpu.VMEM((d, fl), BF16),
                    pltpu.VMEM((fl, d), BF16),
                    pltpu.VMEM((big, fl), BF16),
                    pltpu.VMEM((big, fl), BF16),
                    pltpu.SemaphoreType.DMA((1 + fl // (d // slots), slots)),
                ],
            ),
            input_output_aliases={len(operands) + i: i for i in range(len(given))},
            compiler_params=limit,
            cost_estimate=cost(
                8 * count * big * d * fl, 10 * count * 2**20, count * big * fl
            ),
            name="last_half",
        )(*operands, *given)

    tall = 2 * TILE

    def out_call(seq, parts):
        return pl.pallas_call(
            functools.partial(out_kernel, seq),
            out_shape=shaped(groups, block, share),
            grid_spec=pltpu.PrefetchScalarGridSpec(
                num_scalar_prefetch=1,
                grid=(SLOT // tall,),
                in_specs=[piece_of(seq)] + [own_row] * 3 + [row_block],
                out_specs=back_block,
            ),
            compiler_params=limit,
            cost_estimate=cost(6 * SLOT * share, 10 * SLOT * share),
            name="output_rows",
        )(meta, rows_in[0], *parts, out_bias.astype(F32)[None, :])

    def grad_call(seq, parts, totals):
        return pl.pallas_call(
            functools.partial(grad_kernel, seq, d),
            out_shape=shaped(groups, block, share),
            grid_spec=pltpu.PrefetchScalarGridSpec(
                num_scalar_prefetch=1,
                grid=(SLOT // tall,),
                in_specs=[piece_of(seq)] * 2
                + [own_row] * 3
                + [
                    pl.BlockSpec((tall, 128), lambda t, *_: (seq * (SLOT // tall) + t, 0)),
                    pl.BlockSpec((8, tall), lambda t, *_: (0, t)),
                    row_block,
                ],
                out_specs=back_block,
            ),
            compiler_params=limit,
            cost_estimate=cost(10 * SLOT * share, 12 * SLOT * share),
            name="input_grad_rows",
        )(meta, rows_in[0], grads_in[0], *parts, stats, totals, my_gain)

    def piece_of(seq):
        return pl.BlockSpec((tall // block, 1, block, share), lambda t, *_: (t, seq, 0, 0))

    own_row = pl.BlockSpec((tall, share), lambda t, *_: (t, 0))
    row_block = pl.BlockSpec((1, share), lambda t, *_: (0, 0))
    back_block = pl.BlockSpec((tall // block, block, share), lambda t, *_: (t, 0, 0))

    def near_sums(results, *waits):
        parts = [after(results[r], *waits) if r in (2, 6) else results[r] for r in range(8)]
        half_sums = results[8] + near(results[8])
        return parts, half_reduced(parts[0:4]), half_reduced(parts[4:8]), half_sums

    def far_sums(parts, half_out, half_grad, half_sums):
        return (
            reduced(parts[0:4], half_out),
            reduced(parts[4:8], half_grad),
            half_sums + far(half_sums),
        )

    back_outs = []
    back_grads = []
    local_last = []
    full_last = []
    waits = (arrived_first,)
    token = after(meta, sent_first)
    for seq in range(seqs):
        if seq == 0:
            results = last_call(seq, 0, big_tiles, token, ())
        else:
            results = last_call(seq, 0, big_tiles // 2, token, ())
            out_rows = out_call(seq - 1, after(out_parts, results[9]))
            results = last_call(
                seq, big_tiles // 2, big_tiles // 2, after(meta, out_rows), results
            )
            back_outs.append(entered(after(out_rows, *back_grads)))
        local_last.append(results[9])
        full_last.append(results[10])
        halves = near_sums(results, *waits)
        if seq > 0:
            grad_rows = grad_call(seq - 1, after(grad_parts, results[9]), row_totals)
            back_grads.append(entered(after(grad_rows, back_outs[-1])))
        out_parts, grad_parts, row_totals = far_sums(*halves)
        token = after(meta, *halves[1:])
        waits = (out_parts[2], grad_parts[2])
    sent_last = spread_sums(jnp.stack(local_last), after(jnp.stack(full_last), *halves[1:]))
    out_rows = out_call(seqs - 1, out_parts)
    merged = jnp.concatenate([out_rows, sent_last.reshape(groups, -1, share)], 1)
    merged = entered(after(merged, *back_grads))
    back_outs.append(merged)
    arrived_last = merged[:, block:].reshape(sent_last.shape)
    grad_rows = grad_call(seqs - 1, grad_parts, row_totals)
    back_grads.append(entered(after(grad_rows, merged)))
    output = move_rows(scatter_rows_kernel, permutation, back_outs, "scatter_rows")
    input_grad = move_rows(scatter_rows_kernel, permutation, back_grads, "scatter_rows")

    head_sums, head_full = owned_sums(arrived_first, 4 * share + 2 * fh)
    first_sums = head_sums[:, 4 * share :]
    last_sums, last_full = owned_sums(arrived_last, 2 * fl)
    return (
        output,
        input_grad,
        head_full[0],
        jnp.stack([head_sums[:, c * share : (c + 1) * share] for c in range(3)], 0),
        head_sums[:, dense_at : dense_at + share],
        head_full[1],
        last_full[0],
        jnp.concatenate([first_sums[:, 0:fh], last_sums[:, 0:fl]], 1),
        jnp.concatenate(
            [first_sums[:, fh : 2 * fh], last_sums[:, fl : 2 * fl]], 1
        ),
        last_full[1],
    )


def solution(mesh):
    return jax.shard_map(
        local,
        mesh=mesh,
        in_specs=(
            P(None, "dp", "mp"),
            P(None, "dp", "mp"),
            P(),
            P(),
            P(),
            P(),
            P(None, "dp", "mp"),
            P(None, "mp"),
            P("mp", "dp"),
            P("dp", "mp"),
            P("mp"),
            P("mp", "dp"),
            P("mp"),
            P(("dp", "mp"), None),
            P(None, "dp", "mp"),
            P("dp", "mp"),
            P(("dp", "mp"), None),
            P(("dp", "mp"), None),
            P("dp", "mp"),
            P("dp", "mp"),
            P(("dp", "mp"), None),
        ),
        out_specs=(
            P(None, "dp", "mp"),
            P(None, "dp", "mp"),
            P(("dp", "mp"), None),
            P(None, "dp", "mp"),
            P("dp", "mp"),
            P(("dp", "mp"), None),
            P(("dp", "mp"), None),
            P("dp", "mp"),
            P("dp", "mp"),
            P(("dp", "mp"), None),
        ),
        check_vma=False,
    )
```
